32 devices in a mesh: clip: 8 (over y, x, core), tm: 4 (over z).
Axes of the slice: x: 2, y: 2, z: 4, core: 2. Of those that a mesh axis runs over, the one named last changes fastest.
Arguments:
- incoming_samples: bfloat16 [16, 2048, 512], P('clip', 'tm'), may hold values from -6 to 6
- sample_extents: int32 [16], P('clip'), may hold values from 341 to 2048, as said below
- chosen_entries: int32 [16, 256, 4], P('clip', 'tm'), may hold values from 0 to 1023
- encoder_dilated_kernels: bfloat16 [3, 7, 512, 512], replicated, may hold values from -0.09375 to 0.09375
- encoder_dilated_biases: bfloat16 [3, 512], replicated, may hold values from -3 to 3
- encoder_pointwise_tables: bfloat16 [3, 512, 512], replicated, may hold values from -0.25 to 0.25
- encoder_pointwise_offsets: bfloat16 [3, 512], replicated, may hold values from -3 to 3
- reducing_filter: bfloat16 [4096, 512], replicated, may hold values from -0.09375 to 0.09375
- reducing_offset: bfloat16 [512], replicated, may hold values from -3 to 3
- quantizer_tables: bfloat16 [2, 2, 1024, 256], replicated, may hold values from -6 to 6
- widening_filter: bfloat16 [512, 4096], replicated, may hold values from -0.25 to 0.25
- widening_offset: bfloat16 [512], replicated, may hold values from -3 to 3
- decoder_dilated_filters: bfloat16 [3, 7, 512, 512], replicated, may hold values from -0.09375 to 0.09375
- decoder_dilated_offsets: bfloat16 [3, 512], replicated, may hold values from -3 to 3
- decoder_pointwise_tables: bfloat16 [3, 512, 512], replicated, may hold values from -0.25 to 0.25
- decoder_pointwise_offsets: bfloat16 [3, 512], replicated, may hold values from -3 to 3
- result_cotangent: bfloat16 [16, 2048, 512], P('clip', 'tm'), may hold values from -6 to 6
Outputs:
- output: bfloat16 [16, 2048, 512], P('clip', 'tm')
- quantized: bfloat16 [16, 256, 512], P('clip', 'tm')
- masked_loss: float32 [], replicated
- input_grad: bfloat16 [16, 2048, 512], P('clip', 'tm')
- analysis_grad: float32 [3, 7, 512, 512], P(None, None, 'clip', 'tm')
- offsets_grad: float32 [3, 512], replicated
- mixers_grad: float32 [3, 512, 512], P(None, 'clip', 'tm')
- shifts_grad: float32 [3, 512], replicated
- downsampling_gradient: float32 [4096, 512], P('clip', 'tm')
- pooling_grad: float32 [512], replicated
- codebooks_grad: float32 [2, 2, 1024, 256], P(None, None, 'clip', 'tm')
- upsample_grad: float32 [512, 4096], P('clip', 'tm')
- spreading_grad: float32 [512], replicated
- synthesis_grad: float32 [3, 7, 512, 512], P(None, None, 'clip', 'tm')
- biasing_grad: float32 [3, 512], replicated
- remixers_grad: float32 [3, 512, 512], P(None, 'clip', 'tm')
- tilting_grad: float32 [3, 512], replicated
The draws below stay inside these ranges and needn't reach their ends.
Inputs may be any that keep to these rules, and one draw needn't show every extreme that they name: `sample_extents`: the first clip has 341 frames and the last clip has 2048 frames; frames of a clip from its length on are padding.
All inputs are finite; a program needn't handle non-finite values.
Results may differ from the reference program's by a relative error of at most 0.02.
Values may be sent and summed in bfloat16 or wider, within the bound.
No kernel may reach another device: no remote copies, remote signals or barrier semaphores. Data moves between devices by JAX's collectives and lax.ppermute only.
A program may use at most 256 MiB of HBM per device.

```python
import jax
import jax.numpy as jnp
from jax import lax

HIDDEN_DEPTH = 512
CODES = 1024
GROUPS = 2
LEVELS = 2
KSIZE = 7
UNITS = 3
HOP_FACTOR = 8
GDIM = 256
CLIP_LEN = 2048
CLIPS = 16
NLAT = 256


def draw_sample_extents(key, part):
    position = jnp.arange(CLIPS, dtype=jnp.int32)
    shortest = CLIP_LEN // 6
    rising = shortest + position * ((CLIP_LEN - shortest) * 2 // 3) // CLIPS
    spread = jax.random.randint(key, (CLIPS,), 0, CLIP_LEN // 4 + 1, dtype=jnp.int32)
    drawn = jnp.minimum(rising + spread, CLIP_LEN)
    drawn = drawn.at[0].set(shortest)
    return drawn.at[CLIPS - 1].set(CLIP_LEN)


def touch_ends(array, own_key, smallest, top_value):
    place = [jax.random.randint(jax.random.fold_in(own_key, axis), (), 0, length) for axis, length in enumerate(array.shape)]
    widest = array.shape.index(max(array.shape))
    beside = place[:widest] + [(place[widest] + 1) % array.shape[widest]] + place[widest + 1:]
    return array.at[tuple(place)].set(smallest).at[tuple(beside)].set(top_value)


def with_spikes(values, own_key, source, target, blocks, factor):
    def block_of(dim):
        return (jnp.arange(values.shape[dim]) // (values.shape[dim] // blocks)).reshape((-1,) + (1,) * (values.ndim - 1 - dim))

    first = jax.random.permutation(own_key, blocks)[block_of(target)]
    other_side = (block_of(target) + blocks // 2) % blocks
    return jnp.where((block_of(source) == first) | (block_of(source) == other_side), factor * values, values)


def level_of(stream_key, shape, shards, least, high):
    factor_of, own = 1.0, jax.random.fold_in(stream_key, 6)
    for dim, parts in shards:
        heights = jnp.exp(jax.random.uniform(jax.random.fold_in(own, dim), (parts,), jnp.float32, least / len(shards), high / len(shards)))
        factor_of = factor_of * jnp.repeat(heights, shape[dim] // parts).reshape([-1 if axis == dim else 1 for axis in range(len(shape))])
    return factor_of


def normal_values(stream_key, extent, scale, limit, cuts=(), kind=jnp.bfloat16):
    loudness = level_of(stream_key, extent, cuts, -0.22, 0.18) if cuts else 1.0
    values = jax.random.normal(stream_key, extent, jnp.float32) * scale * loudness
    return jnp.minimum(jnp.maximum(values, -limit), limit).astype(kind)


def gaussian_with(own_key, extent, scale, bound, split, heavy, kind=jnp.bfloat16):
    result = scale * jax.random.normal(own_key, extent, jnp.float32)
    if split:
        result = result * level_of(own_key, extent, split, -0.22, 0.18)
    return jnp.clip(with_spikes(result, jax.random.fold_in(own_key, 3), *heavy), -bound, bound).astype(kind)


def setup_inputs(seed: int = 0) -> dict:
    arg_keys = jax.random.split(jax.random.key(seed), 18)
    incoming_samples = gaussian_with(arg_keys[0], (CLIPS, CLIP_LEN, HIDDEN_DEPTH), 1.0, 6.0, ((0, 8), (1, 4)), (0, 2, 8, 2.0))
    sample_extents = draw_sample_extents(jax.random.fold_in(arg_keys[17], 71), 0)
    chosen_entries = touch_ends(jax.random.randint(arg_keys[2], (CLIPS, NLAT, GROUPS * LEVELS), 0, CODES), jax.random.fold_in(arg_keys[2], 1), 0, CODES - 1).astype(jnp.int32)
    encoder_dilated_kernels = normal_values(arg_keys[3], (UNITS, KSIZE, HIDDEN_DEPTH, HIDDEN_DEPTH), (KSIZE * HIDDEN_DEPTH) ** -0.5, 0.09375)
    encoder_dilated_biases = normal_values(arg_keys[4], (UNITS, HIDDEN_DEPTH), 0.2, 3.0)
    encoder_pointwise_tables = normal_values(arg_keys[5], (UNITS, HIDDEN_DEPTH, HIDDEN_DEPTH), HIDDEN_DEPTH ** -0.5, 0.25)
    encoder_pointwise_offsets = normal_values(arg_keys[6], (UNITS, HIDDEN_DEPTH), 0.2, 3.0)
    reducing_filter = normal_values(arg_keys[7], (HOP_FACTOR * HIDDEN_DEPTH, HIDDEN_DEPTH), (HOP_FACTOR * HIDDEN_DEPTH) ** -0.5, 0.09375)
    reducing_offset = normal_values(arg_keys[8], (HIDDEN_DEPTH,), 0.2, 3.0)
    quantizer_tables = normal_values(arg_keys[9], (GROUPS, LEVELS, CODES, GDIM), 1.0, 6.0)
    widening_filter = normal_values(arg_keys[10], (HIDDEN_DEPTH, HOP_FACTOR * HIDDEN_DEPTH), HIDDEN_DEPTH ** -0.5, 0.25)
    widening_offset = normal_values(arg_keys[11], (HIDDEN_DEPTH,), 0.2, 3.0)
    decoder_dilated_filters = normal_values(arg_keys[12], (UNITS, KSIZE, HIDDEN_DEPTH, HIDDEN_DEPTH), (KSIZE * HIDDEN_DEPTH) ** -0.5, 0.09375)
    decoder_dilated_offsets = normal_values(arg_keys[13], (UNITS, HIDDEN_DEPTH), 0.2, 3.0)
    decoder_pointwise_tables = normal_values(arg_keys[14], (UNITS, HIDDEN_DEPTH, HIDDEN_DEPTH), HIDDEN_DEPTH ** -0.5, 0.25)
    decoder_pointwise_offsets = normal_values(arg_keys[15], (UNITS, HIDDEN_DEPTH), 0.2, 3.0)
    result_cotangent = normal_values(arg_keys[16], (CLIPS, CLIP_LEN, HIDDEN_DEPTH), 1.0, 6.0, ((0, 8), (1, 4)))
    return dict(incoming_samples=incoming_samples, sample_extents=sample_extents, chosen_entries=chosen_entries, encoder_dilated_kernels=encoder_dilated_kernels, encoder_dilated_biases=encoder_dilated_biases, encoder_pointwise_tables=encoder_pointwise_tables, encoder_pointwise_offsets=encoder_pointwise_offsets, reducing_filter=reducing_filter, reducing_offset=reducing_offset, quantizer_tables=quantizer_tables, widening_filter=widening_filter, widening_offset=widening_offset, decoder_dilated_filters=decoder_dilated_filters, decoder_dilated_offsets=decoder_dilated_offsets, decoder_pointwise_tables=decoder_pointwise_tables, decoder_pointwise_offsets=decoder_pointwise_offsets, result_cotangent=result_cotangent)


@jax.custom_vjp
def low(v):
    return lax.optimization_barrier(v.astype(jnp.bfloat16)).astype(jnp.float32)

@jax.custom_vjp
def first_half_pullback(v):
    return v

def low_keep(v):
    return (low(v), None)

def low_pass(kept, grad):
    return (grad,)

def back_keep(v):
    return (v, None)

def back_low(kept, grad):
    return (low(grad),)
low.defvjp(low_keep, low_pass)
first_half_pullback.defvjp(back_keep, back_low)
commit_weight = 0.25
highest = lax.Precision.HIGHEST

def multiply_tables(left, right):
    return jnp.dot(left, right, precision=highest, preferred_element_type=jnp.float32)

def dilated(source, kernel, dilation):
    margin = KSIZE // 2 * dilation
    frames = source.shape[0]
    padded = jnp.pad(source, ((margin, margin), (0, 0)))
    stacked = jnp.concatenate([padded[tap_index * dilation:tap_index * dilation + frames] for tap_index in range(KSIZE)], axis=1)
    return multiply_tables(stacked, kernel.reshape(KSIZE * HIDDEN_DEPTH, HIDDEN_DEPTH))

def residual_stack(stream, kernels, encoder_dilated_biases, encoder_pointwise_tables, encoder_pointwise_offsets):
    for unit_index in range(UNITS):
        source = low(jax.nn.elu(stream))
        before = first_half_pullback(dilated(source, kernels[unit_index], 3 ** unit_index) + encoder_dilated_biases[unit_index])
        pointed = low(jax.nn.elu(before))
        branch = first_half_pullback(multiply_tables(pointed, encoder_pointwise_tables[unit_index]) + encoder_pointwise_offsets[unit_index])
        stream = stream + branch
    return stream

def analyse_segment(sample_feature_slices, encoder_dilated_kernels, encoder_dilated_biases, encoder_pointwise_tables, encoder_pointwise_offsets, reducing_filter, reducing_offset):
    stream = residual_stack(sample_feature_slices, encoder_dilated_kernels, encoder_dilated_biases, encoder_pointwise_tables, encoder_pointwise_offsets)
    reduced_samples = low(jax.nn.elu(stream)).reshape(NLAT, HOP_FACTOR * HIDDEN_DEPTH)
    return first_half_pullback(multiply_tables(reduced_samples, reducing_filter) + reducing_offset)

def lookup(quantizer_tables, index_in):
    picked = []
    for group_index in range(GROUPS):
        level_rows = []
        for level_index in range(LEVELS):
            column = index_in[:, group_index * LEVELS + level_index]
            onehot = (column[:, None] == jnp.arange(CODES, dtype=jnp.int32)[None, :]).astype(jnp.float32)
            level_rows.append(multiply_tables(onehot, quantizer_tables[group_index, level_index]))
        picked.append(jnp.stack(level_rows))
    return jnp.stack(picked)

def decode(decoder_in, widening_filter, widening_offset, decoder_dilated_filters, decoder_dilated_offsets, decoder_pointwise_tables, decoder_pointwise_offsets):
    widened = multiply_tables(decoder_in, widening_filter).reshape(CLIP_LEN, HIDDEN_DEPTH) + widening_offset
    stream = low(first_half_pullback(widened))
    return residual_stack(stream, decoder_dilated_filters, decoder_dilated_offsets, decoder_pointwise_tables, decoder_pointwise_offsets)

def clip_terms(parameter_tensors, sample_feature_slices, index_in, valid_in, fixed_latent, fixed_codes):
    latent = analyse_segment(sample_feature_slices, *parameter_tensors[:6])
    picked = lookup(parameter_tensors[6], index_in)
    objective = jnp.float32(0.0)
    for group_index in range(GROUPS):
        lower_edge = group_index * GDIM
        residue = latent[:, lower_edge:lower_edge + GDIM]
        fixed_residue = fixed_latent[:, lower_edge:lower_edge + GDIM]
        for level_index in range(LEVELS):
            book_term = fixed_residue - picked[group_index, level_index]
            objective = objective + jnp.sum(valid_in[:, None] * book_term * book_term)
            residue = residue - fixed_codes[group_index, level_index]
            fixed_residue = fixed_residue - fixed_codes[group_index, level_index]
            objective = objective + commit_weight * jnp.sum(valid_in[:, None] * residue * residue)
    fixed_quant = lax.optimization_barrier(jnp.sum(fixed_codes, axis=1)).transpose(1, 0, 2).reshape(NLAT, HIDDEN_DEPTH)
    decoder_in = low(latent + (fixed_quant - fixed_latent))
    return (decode(decoder_in, *parameter_tensors[7:]), objective)

def reference(incoming_samples, sample_extents, chosen_entries, encoder_dilated_kernels, encoder_dilated_biases, encoder_pointwise_tables, encoder_pointwise_offsets, reducing_filter, reducing_offset, quantizer_tables, widening_filter, widening_offset, decoder_dilated_filters, decoder_dilated_offsets, decoder_pointwise_tables, decoder_pointwise_offsets, result_cotangent):
    parameter_tensors = tuple((parameter_table.astype(jnp.float32) for parameter_table in (encoder_dilated_kernels, encoder_dilated_biases, encoder_pointwise_tables, encoder_pointwise_offsets, reducing_filter, reducing_offset, quantizer_tables, widening_filter, widening_offset, decoder_dilated_filters, decoder_dilated_offsets, decoder_pointwise_tables, decoder_pointwise_offsets)))
    inputs = incoming_samples.astype(jnp.float32)
    validity = (jnp.arange(NLAT, dtype=jnp.int32)[None, :] * HOP_FACTOR < sample_extents[:, None]).astype(jnp.float32)
    total_count = jnp.sum(validity)
    fixed_latent = lax.map(lambda sample_feature_slices: analyse_segment(sample_feature_slices, *parameter_tensors[:6]), inputs)
    fixed_codes = lax.map(lambda index_in: lookup(parameter_tensors[6], index_in), chosen_entries)
    quantized = low(lax.optimization_barrier(jnp.sum(fixed_codes, axis=2)).transpose(0, 2, 1, 3).reshape(CLIPS, NLAT, HIDDEN_DEPTH))

    def total(weight_list, inputs_all):
        clip_step = jax.checkpoint(clip_terms)

        def advance(running, sliced):
            sample_feature_slices, index_in, valid_in, latent_in, codes_in = sliced
            produced, objective = clip_step(weight_list, sample_feature_slices, index_in, valid_in, latent_in, codes_in)
            return (running + objective, produced)
        objective, produced = lax.scan(advance, jnp.float32(0.0), (inputs_all, chosen_entries, validity, fixed_latent, fixed_codes))
        return (produced, objective)
    (produced, objective), pullback = jax.vjp(total, parameter_tensors, inputs)
    weight_grads, input_grad = pullback((result_cotangent.astype(jnp.float32), jnp.ones_like(objective)))
    masked_loss = objective / (total_count * HIDDEN_DEPTH)
    return (produced.astype(jnp.bfloat16), quantized.astype(jnp.bfloat16), masked_loss, input_grad.astype(jnp.bfloat16), weight_grads[0], weight_grads[1], weight_grads[2], weight_grads[3], weight_grads[4], weight_grads[5], weight_grads[6], weight_grads[7], weight_grads[8], weight_grads[9], weight_grads[10], weight_grads[11], weight_grads[12])
```

```python
import functools

import jax
import jax.numpy as jnp
from jax import lax
from jax.experimental import pallas as pl
from jax.experimental.pallas import tpu as pltpu
from jax.sharding import PartitionSpec as P

GROUPS = 2
LEVELS = 2
KSIZE = 7
UNITS = 3
HOP_FACTOR = 8


commit_weight = 0.25


def from_behind(block, axis, distance):
    devices = range(lax.axis_size(axis))
    route = [(i - distance, i) for i in devices if i - distance in devices]
    return lax.ppermute(block, axis, route)


def padded(cells, sides, width):
    for axis, dim in sides:
        count = lax.axis_size(axis)
        ends = count - 1
        head = lax.slice_in_dim(cells, 0, width, axis=dim)
        tail = lax.slice_in_dim(cells, cells.shape[dim] - width, cells.shape[dim], axis=dim)
        cells = jnp.concatenate(
            [
                lax.ppermute(tail, axis, [(i, (i + 1) % count) for i in range(ends)]),
                cells,
                lax.ppermute(head, axis, [((i + 1) % count, i) for i in range(ends)]),
            ],
            axis=dim,
        )
    return cells


def elu_slope(values):
    return jnp.where(values > 0, 1.0, jnp.exp(jnp.minimum(values, 0.0)))


def gather_taps(source, dilation, frames):
    return jnp.concatenate(
        [
            source[:, tap_index * dilation : tap_index * dilation + frames]
            for tap_index in range(KSIZE)
        ],
        axis=2,
    )


def dilated(source, kernel, dilation):
    frames = source.shape[1] - (KSIZE - 1) * dilation
    stacked = gather_taps(source, dilation, frames)
    flattened = kernel.reshape(KSIZE * kernel.shape[1], kernel.shape[2])
    return jnp.einsum("cti,io->cto", stacked, flattened, preferred_element_type=jnp.float32)


def dilated_back(source, kernel, dilation, grad_out):
    frames = grad_out.shape[1]
    stacked = gather_taps(source, dilation, frames)
    flattened = kernel.reshape(KSIZE * kernel.shape[1], kernel.shape[2])
    kernel_grad = jnp.einsum(
        "cti,cto->io", stacked, grad_out, preferred_element_type=jnp.float32
    ).reshape(kernel.shape)
    spread = jnp.einsum("cto,io->cti", grad_out, flattened, preferred_element_type=jnp.float32)
    channels = kernel.shape[1]
    source_grad = jnp.zeros(source.shape, jnp.float32)
    for tap_index in range(KSIZE):
        source_grad = source_grad.at[:, tap_index * dilation : tap_index * dilation + frames].add(
            spread[:, :, tap_index * channels : (tap_index + 1) * channels]
        )
    return (kernel_grad, source_grad)


def return_rims(grad_full, margin_width):
    length = grad_full.shape[1]
    owned = grad_full[:, margin_width : length - margin_width]
    from_above = from_behind(grad_full[:, :margin_width].astype(jnp.bfloat16), "tm", -1).astype(
        jnp.float32
    )
    from_below = from_behind(
        grad_full[:, length - margin_width :].astype(jnp.bfloat16), "tm", 1
    ).astype(jnp.float32)
    owned = owned.at[:, owned.shape[1] - margin_width :].add(from_above)
    return owned.at[:, :margin_width].add(from_below)


def unit_source(stream, margin_width):
    activated = jax.nn.elu(stream)
    return padded(activated.astype(jnp.bfloat16), (("tm", 1),), margin_width)


def source_back(source_grad, margin_width):
    return return_rims(source_grad, margin_width)


def stack_forward(
    stream,
    kernels,
    encoder_dilated_biases,
    encoder_pointwise_tables,
    encoder_pointwise_offsets,
    first_frame,
    frames,
):
    kept_list = []
    for unit_index in range(UNITS):
        dilation = 3**unit_index
        margin_width = KSIZE // 2 * dilation
        extra_frames = (stream.shape[1] - frames) // 2
        positions = first_frame - extra_frames + jnp.arange(stream.shape[1], dtype=jnp.int32)
        source = unit_source(stream, margin_width)
        before = dilated(source, kernels[unit_index], dilation) + encoder_dilated_biases[
            unit_index
        ].astype(jnp.float32)
        pointed = jax.nn.elu(before).astype(jnp.bfloat16)
        branch = jnp.einsum(
            "ctd,de->cte",
            pointed,
            encoder_pointwise_tables[unit_index],
            preferred_element_type=jnp.float32,
        )
        branch = branch + encoder_pointwise_offsets[unit_index].astype(jnp.float32)
        kept_list.append((stream, source, before, pointed, positions))
        stream = stream + branch
    return (stream, kept_list)


def stack_backward(grad_stream, kept_list, kernels, encoder_pointwise_tables):
    kernel_grads, offset_grads, mixer_grads, shift_grads = ([], [], [], [])
    for unit_index in reversed(range(UNITS)):
        stream, source, before, pointed, positions = kept_list[unit_index]
        dilation = 3**unit_index
        margin_width = KSIZE // 2 * dilation
        branch_grad = grad_stream.astype(jnp.bfloat16)
        mixer_grads.insert(
            0, jnp.einsum("ctd,cte->de", pointed, branch_grad, preferred_element_type=jnp.float32)
        )
        shift_grads.insert(0, jnp.sum(branch_grad.astype(jnp.float32), axis=(0, 1)))
        pointed_grad = jnp.einsum(
            "cte,de->ctd",
            branch_grad,
            encoder_pointwise_tables[unit_index],
            preferred_element_type=jnp.float32,
        )
        before_grad = (pointed_grad * elu_slope(before)).astype(jnp.bfloat16)
        offset_grads.insert(0, jnp.sum(before_grad.astype(jnp.float32), axis=(0, 1)))
        kernel_grad, source_grad = dilated_back(source, kernels[unit_index], dilation, before_grad)
        kernel_grads.insert(0, kernel_grad)
        owned_grad = source_back(source_grad, margin_width)
        grad_stream = grad_stream + owned_grad * elu_slope(stream)
    return (
        grad_stream,
        (
            jnp.stack(kernel_grads),
            jnp.stack(offset_grads),
            jnp.stack(mixer_grads),
            jnp.stack(shift_grads),
        ),
    )


def over_clips(matrices):
    return (
        lax.psum_scatter(
            matrices[0].astype(jnp.bfloat16), "clip", scatter_dimension=2, tiled=True
        ).astype(jnp.float32),
        lax.psum_scatter(
            matrices[1].astype(jnp.bfloat16), "clip", scatter_dimension=1, tiled=True
        ).astype(jnp.float32),
        lax.psum_scatter(
            matrices[2].astype(jnp.bfloat16), "clip", scatter_dimension=0, tiled=True
        ).astype(jnp.float32),
        lax.psum_scatter(
            matrices[3].astype(jnp.bfloat16), "clip", scatter_dimension=2, tiled=True
        ).astype(jnp.float32),
        lax.psum_scatter(
            matrices[4].astype(jnp.bfloat16), "clip", scatter_dimension=0, tiled=True
        ).astype(jnp.float32),
        lax.psum_scatter(
            matrices[5].astype(jnp.bfloat16), "clip", scatter_dimension=2, tiled=True
        ).astype(jnp.float32),
        lax.psum_scatter(
            matrices[6].astype(jnp.bfloat16), "clip", scatter_dimension=1, tiled=True
        ).astype(jnp.float32),
    )


def over_segments(matrices):
    return (
        lax.psum_scatter(
            matrices[0].astype(jnp.bfloat16), "tm", scatter_dimension=3, tiled=True
        ).astype(jnp.float32),
        lax.psum_scatter(
            matrices[1].astype(jnp.bfloat16), "tm", scatter_dimension=2, tiled=True
        ).astype(jnp.float32),
        lax.psum_scatter(
            matrices[2].astype(jnp.bfloat16), "tm", scatter_dimension=1, tiled=True
        ).astype(jnp.float32),
        lax.psum_scatter(
            matrices[3].astype(jnp.bfloat16), "tm", scatter_dimension=3, tiled=True
        ).astype(jnp.float32),
        lax.psum_scatter(
            matrices[4].astype(jnp.bfloat16), "tm", scatter_dimension=1, tiled=True
        ).astype(jnp.float32),
        lax.psum_scatter(
            matrices[5].astype(jnp.bfloat16), "tm", scatter_dimension=3, tiled=True
        ).astype(jnp.float32),
        lax.psum_scatter(
            matrices[6].astype(jnp.bfloat16), "tm", scatter_dimension=2, tiled=True
        ).astype(jnp.float32),
    )


def on_device(
    incoming_samples,
    sample_extents,
    chosen_entries,
    encoder_dilated_kernels,
    encoder_dilated_biases,
    encoder_pointwise_tables,
    encoder_pointwise_offsets,
    reducing_filter,
    reducing_offset,
    quantizer_tables,
    widening_filter,
    widening_offset,
    decoder_dilated_filters,
    decoder_dilated_offsets,
    decoder_pointwise_tables,
    decoder_pointwise_offsets,
    result_cotangent,
):
    segment = lax.axis_index("tm")
    clips = incoming_samples.shape[0]
    frames = incoming_samples.shape[1]
    channels = incoming_samples.shape[2]
    first_frame = segment * frames
    latents = frames // HOP_FACTOR
    total_count = lax.psum(
        jnp.sum((sample_extents + HOP_FACTOR - 1) // HOP_FACTOR).astype(jnp.float32), "clip"
    )
    stream = incoming_samples.astype(jnp.float32)
    encoded, encoder_kept = stack_forward(
        stream,
        encoder_dilated_kernels,
        encoder_dilated_biases,
        encoder_pointwise_tables,
        encoder_pointwise_offsets,
        first_frame,
        frames,
    )
    reduced_samples = (
        jax.nn.elu(encoded).astype(jnp.bfloat16).reshape(clips, latents, HOP_FACTOR * channels)
    )
    latent = jnp.einsum(
        "kde,er->kdr", reduced_samples, reducing_filter, preferred_element_type=jnp.float32
    ) + reducing_offset.astype(jnp.float32)
    validity = (
        (first_frame + HOP_FACTOR * jnp.arange(latents, dtype=jnp.int32))[None, :]
        < sample_extents[:, None]
    ).astype(jnp.float32)
    masked = validity[..., None]
    group_width = channels // GROUPS
    code_range = jnp.arange(quantizer_tables.shape[2], dtype=jnp.int32)
    loss_local = jnp.float32(0.0)
    quant_parts, commit_parts, book_rows = ([], [], [])
    for group_index in range(GROUPS):
        residue = latent[:, :, group_index * group_width : (group_index + 1) * group_width]
        commit_sum = jnp.zeros_like(residue)
        group_code = jnp.zeros_like(residue)
        level_rows = []
        for level_index in range(LEVELS):
            column = group_index * LEVELS + level_index
            onehot = (chosen_entries[:, :, column][..., None] == code_range).astype(jnp.bfloat16)
            picked = jnp.einsum(
                "kde,er->kdr",
                onehot,
                quantizer_tables[group_index, level_index],
                preferred_element_type=jnp.float32,
            )
            residue = residue - picked
            level_rows.append(
                jnp.einsum(
                    "cnk,cnd->kd",
                    onehot.astype(jnp.float32),
                    -2.0 * masked * residue,
                    precision=lax.Precision.HIGHEST,
                    preferred_element_type=jnp.float32,
                )
            )
            commit_sum = commit_sum + residue
            loss_local = loss_local + jnp.sum(masked * residue * residue)
            group_code = group_code + picked
        book_rows.append(jnp.stack(level_rows))
        commit_parts.append(2.0 * commit_weight * masked * commit_sum)
        quant_parts.append(group_code)
    loss_local = (1.0 + commit_weight) * loss_local
    quantized = jnp.concatenate(quant_parts, axis=2).astype(jnp.bfloat16)
    loss_sum = lax.psum(loss_local, ("clip", "tm"))
    masked_loss = loss_sum / (total_count * channels)
    widened = jnp.einsum(
        "cnd,de->cne", quantized, widening_filter, preferred_element_type=jnp.float32
    )
    decoder_start = (
        widened.reshape(clips, frames, channels) + widening_offset.astype(jnp.float32)
    ).astype(jnp.bfloat16)
    stream = decoder_start.astype(jnp.float32)
    decoded, decoder_kept = stack_forward(
        stream,
        decoder_dilated_filters,
        decoder_dilated_offsets,
        decoder_pointwise_tables,
        decoder_pointwise_offsets,
        first_frame,
        frames,
    )
    output = decoded.astype(jnp.bfloat16)
    grad_decoder, decoder_grads = stack_backward(
        result_cotangent.astype(jnp.float32),
        decoder_kept,
        decoder_dilated_filters,
        decoder_pointwise_tables,
    )
    widened_grad = grad_decoder.astype(jnp.bfloat16)
    spreading_grad = jnp.sum(widened_grad.astype(jnp.float32), axis=(0, 1))
    folded_grad = widened_grad.reshape(clips, latents, HOP_FACTOR * channels)
    upsample_grad = jnp.einsum(
        "cnd,cne->de", quantized, folded_grad, preferred_element_type=jnp.float32
    )
    latent_grad = jnp.einsum(
        "cne,de->cnd", folded_grad, widening_filter, preferred_element_type=jnp.float32
    )
    hidden_first_half = (latent_grad + jnp.concatenate(commit_parts, axis=2)).astype(jnp.bfloat16)
    pooling_grad = jnp.sum(hidden_first_half.astype(jnp.float32), axis=(0, 1))
    downsampling_gradient = jnp.einsum(
        "cnk,cnd->kd", reduced_samples, hidden_first_half, preferred_element_type=jnp.float32
    )
    pooled_grad = jnp.einsum(
        "npk,xk->npx", hidden_first_half, reducing_filter, preferred_element_type=jnp.float32
    )
    pooled_grad = pooled_grad.reshape(clips, frames, channels) * elu_slope(encoded)
    grad_encoder, encoder_grads = stack_backward(
        pooled_grad, encoder_kept, encoder_dilated_kernels, encoder_pointwise_tables
    )
    input_grad = grad_encoder.astype(jnp.bfloat16)
    codebook_grad = jnp.stack(book_rows)
    matrices = (
        encoder_grads[0],
        encoder_grads[2],
        downsampling_gradient,
        codebook_grad,
        upsample_grad,
        decoder_grads[0],
        decoder_grads[2],
    )
    matrices = over_segments(over_clips(matrices))
    biases = lax.psum(
        (
            encoder_grads[1],
            encoder_grads[3],
            pooling_grad,
            spreading_grad,
            decoder_grads[1],
            decoder_grads[3],
        ),
        ("clip", "tm"),
    )
    return (
        output,
        quantized,
        masked_loss,
        input_grad,
        matrices[0],
        biases[0],
        matrices[1],
        biases[1],
        matrices[2],
        biases[2],
        matrices[3],
        matrices[4],
        biases[3],
        matrices[5],
        biases[4],
        matrices[6],
        biases[5],
    )

PAD = 32
LANES = 128
LATENT_REACH = 10
GRAD_REACH = 6
NT = (((1,), (1,)), ((), ()))
VMEM_BYTES = 60 * 1024 * 1024


def elu(values):
    return jnp.where(values > 0, values, jnp.exp(jnp.minimum(values, 0.0)) - 1.0)


def slope_from_elu(activated):
    return jnp.where(activated > 0, 1.0, activated + 1.0)


def whole(array):
    return pl.BlockSpec(array.shape, lambda i: (0,) * len(array.shape))


def smem():
    return pl.BlockSpec(memory_space=pltpu.SMEM)


def compiler_params():
    return pltpu.CompilerParams(
        vmem_limit_bytes=VMEM_BYTES, dimension_semantics=("arbitrary",)
    )


def forward_kernel(
    dilation, first, rows, where_ref, h_ref, w_ref, b_ref, m_ref, s_ref, e_ref, p_ref, out_ref, lines
):
    clips, length, channels = h_ref.shape
    low, high = where_ref[0], where_ref[1]
    tiles = channels // LANES
    position = lax.broadcasted_iota(jnp.int32, (length, LANES), 0)
    inside = (position >= low) & (position < high)
    for clip in range(clips):
        for tile in range(tiles):
            lanes = slice(tile * LANES, (tile + 1) * LANES)
            lines[clip, tile, :PAD, :] = jnp.zeros((PAD, LANES), jnp.float32)
            lines[clip, tile, PAD + length :, :] = jnp.zeros((PAD, LANES), jnp.float32)
            active = jnp.where(inside, elu(h_ref[clip, :, lanes].astype(jnp.float32)), 0.0)
            active = active.astype(jnp.bfloat16)
            e_ref[clip, :, lanes] = active
            lines[clip, tile, PAD : PAD + length, :] = active.astype(jnp.float32)
    kernel = w_ref[0].reshape(KSIZE * channels, channels)
    mixer = m_ref[0]
    for clip in range(clips):
        taps = []
        for tap in range(KSIZE):
            start = PAD + first + (tap - KSIZE // 2) * dilation
            for tile in range(tiles):
                taps.append(lines[clip, tile, start : start + rows, :].astype(jnp.bfloat16))
        before = jnp.dot(
            jnp.concatenate(taps, axis=1), kernel, preferred_element_type=jnp.float32
        )
        pointed = elu(before + b_ref[0].astype(jnp.float32)).astype(jnp.bfloat16)
        p_ref[clip] = pointed
        branch = jnp.dot(pointed, mixer, preferred_element_type=jnp.float32)
        branch = branch + s_ref[0].astype(jnp.float32)
        stream = h_ref[clip, first : first + rows, :].astype(jnp.float32)
        out_ref[clip] = (stream + branch).astype(out_ref.dtype)


def forward_unit(where, h, kernels, biases, mixers, shifts, unit, first, rows):
    clips, length, channels = h.shape
    outs = (
        jax.ShapeDtypeStruct((clips, length, channels), jnp.bfloat16),
        jax.ShapeDtypeStruct((clips, rows, channels), jnp.bfloat16),
        jax.ShapeDtypeStruct((clips, rows, channels), jnp.float32),
    )
    return pl.pallas_call(
        functools.partial(forward_kernel, 3**unit, first, rows),
        grid=(1,),
        in_specs=[
            smem(),
            whole(h),
            pl.BlockSpec((1, KSIZE, channels, channels), lambda i: (unit, 0, 0, 0)),
            pl.BlockSpec((1, 1, channels), lambda i: (unit, 0, 0)),
            pl.BlockSpec((1, channels, channels), lambda i: (unit, 0, 0)),
            pl.BlockSpec((1, 1, channels), lambda i: (unit, 0, 0)),
        ],
        out_specs=[whole(out) for out in outs],
        out_shape=outs,
        scratch_shapes=[
            pltpu.VMEM((clips, channels // LANES, length + 2 * PAD, LANES), jnp.float32)
        ],
        compiler_params=compiler_params(),
        name="unit_forward",
    )(where, h, kernels, biases, mixers, shifts)


def backward_kernel(
    dilation,
    rows,
    p_first,
    e_first,
    own,
    rim,
    place,
    gh_ref,
    p_ref,
    e_ref,
    w_ref,
    m_ref,
    send_ref,
    keep_ref,
    out_ref,
    sum_ref,
    lines,
    turned,
):
    clips, length, channels = gh_ref.shape
    tiles = channels // LANES
    own_first = (length - own) // 2
    shift = (length - rows) // 2
    wide = own + 2 * rim
    low, high, core = place[0], place[1], place[2]
    mixer = m_ref[0]
    position = lax.broadcasted_iota(jnp.int32, (length, channels), 0)
    inside = (position >= low) & (position < high)
    for clip in range(clips):
        gc = gh_ref[clip].astype(jnp.bfloat16)
        send_ref[clips * wide + clip * own : clips * wide + (clip + 1) * own, :] = gc[
            own_first : own_first + own
        ]
        gp = lax.dot_general(gc, mixer, NT, preferred_element_type=jnp.float32)
        pointed = p_ref[clip, p_first : p_first + length, :].astype(jnp.float32)
        ga = jnp.where(inside, gp * slope_from_elu(pointed), 0.0).astype(jnp.bfloat16)
        send_ref[clip * wide : (clip + 1) * wide, :] = ga[
            own_first - rim : own_first + own + rim
        ]
        ga = ga.astype(jnp.float32)
        a_sum = jnp.sum(ga[own_first : own_first + own], axis=0, keepdims=True)
        c_sum = jnp.sum(
            gc[own_first : own_first + own].astype(jnp.float32), axis=0, keepdims=True
        )
        if clip == 0:
            sum_ref[0:1, :] = a_sum
            sum_ref[1:2, :] = c_sum
        else:
            sum_ref[0:1, :] = sum_ref[0:1, :] + a_sum
            sum_ref[1:2, :] = sum_ref[1:2, :] + c_sum
        for tile in range(tiles):
            lines[clip, tile, :PAD, :] = jnp.zeros((PAD, LANES), jnp.float32)
            lines[clip, tile, PAD + length :, :] = jnp.zeros((PAD, LANES), jnp.float32)
            lines[clip, tile, PAD : PAD + length, :] = ga[:, tile * LANES : (tile + 1) * LANES]
    total = None
    for tap in range(KSIZE):
        start = PAD + shift - (tap - KSIZE // 2) * dilation
        moved = jnp.concatenate(
            [
                jnp.concatenate(
                    [
                        lines[clip, tile, start : start + rows, :].astype(jnp.bfloat16)
                        for tile in range(tiles)
                    ],
                    axis=1,
                )
                for clip in range(clips)
            ],
            axis=0,
        )
        part = lax.dot_general(moved, w_ref[0, tap], NT, preferred_element_type=jnp.float32)
        total = part if total is None else total + part
    for clip in range(clips):
        active = e_ref[clip, e_first : e_first + rows, :].astype(jnp.float32)
        out_ref[clip] = gh_ref[clip, shift : shift + rows, :].astype(jnp.float32) + total[
            clip * rows : (clip + 1) * rows
        ] * slope_from_elu(active)
    base = clips * (wide + own)
    block = channels // 8
    sources = ((e_ref, e_first + (rows - own) // 2), (p_ref, p_first + own_first))
    for which, (ref, start) in enumerate(sources):
        for clip in range(clips):
            turned[...] = jnp.transpose(ref[clip, start : start + own, :])
            for rx in range(2):
                for ry in range(2):
                    pair = jnp.bitwise_xor(place[4], ry) * 4 + jnp.bitwise_xor(place[3], rx) * 2
                    to = (which * clips + clip) * (channels // 2) + (rx * 2 + ry) * block
                    mine = pl.multiple_of((pair + core) * block, block)
                    other = pl.multiple_of((pair + 1 - core) * block, block)
                    keep_ref[to : to + block, :] = turned[pl.ds(mine, block), :]
                    send_ref[base + to : base + to + block, :] = turned[pl.ds(other, block), :]


def backward_unit(place, gh, p, e, kernels, mixers, unit, rows, p_first, e_first, own, rim):
    clips, length, channels = gh.shape
    payload = clips * (2 * own + 2 * rim + channels)
    outs = (
        jax.ShapeDtypeStruct((payload, channels), jnp.bfloat16),
        jax.ShapeDtypeStruct((clips * channels, own), jnp.bfloat16),
        jax.ShapeDtypeStruct((clips, rows, channels), jnp.float32),
        jax.ShapeDtypeStruct((8, channels), jnp.float32),
    )
    return pl.pallas_call(
        functools.partial(backward_kernel, 3**unit, rows, p_first, e_first, own, rim),
        grid=(1,),
        in_specs=[
            smem(),
            whole(gh),
            whole(p),
            whole(e),
            pl.BlockSpec((1, KSIZE, channels, channels), lambda i: (unit, 0, 0, 0)),
            pl.BlockSpec((1, channels, channels), lambda i: (unit, 0, 0)),
        ],
        out_specs=[whole(out) for out in outs],
        out_shape=outs,
        scratch_shapes=[
            pltpu.VMEM((clips, channels // LANES, length + 2 * PAD, LANES), jnp.float32),
            pltpu.VMEM((channels, own), jnp.bfloat16),
        ],
        compiler_params=compiler_params(),
        name="unit_backward",
    )(place, gh, p, e, kernels, mixers)


def emit(result, z, tap, tap_rows, first_axis, send_ref, keep_ref):
    result = result.astype(jnp.bfloat16)
    quarter = result.shape[0] // 4
    for rx in range(2):
        for ry in range(2):
            first, second = (rx, ry) if first_axis == 0 else (ry, rx)
            target = send_ref if first == 1 else keep_ref
            rows = slice((rx * 2 + ry) * quarter, (rx * 2 + ry + 1) * quarter)
            for segment in range(4):
                relative = lax.rem(segment - z + 4, 4)
                target[second, relative, tap * tap_rows : (tap + 1) * tap_rows, :] = result[
                    rows, segment * LANES : (segment + 1) * LANES
                ]


def emit_outputs(taps_per_axis, tap_rows):
    out = jax.ShapeDtypeStruct((2, 4, taps_per_axis * tap_rows, LANES), jnp.bfloat16)
    return (out,) * 4


def weights_kernel(
    dilation, own, rim, clips, place, mine_ref, other_ref, keep_ref, sx, kx, sy, ky, lines
):
    channels = mine_ref.shape[1]
    tiles = channels // LANES
    half = channels // 2
    wide = own + 2 * rim
    c_base = clips * wide
    base = c_base + clips * own
    sources = (mine_ref, other_ref)
    step = pl.program_id(0)

    @pl.when(step == 0)
    def _():
        for source in range(2):
            for clip in range(clips):
                for tile in range(tiles):
                    lines[source * clips + clip, tile, :, :] = sources[source][
                        clip * wide : (clip + 1) * wide, tile * LANES : (tile + 1) * LANES
                    ].astype(jnp.float32)

    def left(which):
        pieces = [
            keep_ref[(which * clips + clip) * half : (which * clips + clip + 1) * half, :]
            for clip in range(clips)
        ] + [
            other_ref[
                base + (which * clips + clip) * half : base + (which * clips + clip + 1) * half, :
            ]
            for clip in range(clips)
        ]
        return jnp.concatenate(pieces, axis=1)

    for tap in range(KSIZE + 1):

        @pl.when(step == tap)
        def _(tap=tap):
            if tap < KSIZE:
                start = rim - (tap - KSIZE // 2) * dilation
                right = jnp.concatenate(
                    [
                        jnp.concatenate(
                            [
                                lines[item, tile, start : start + own, :].astype(jnp.bfloat16)
                                for tile in range(tiles)
                            ],
                            axis=1,
                        )
                        for item in range(2 * clips)
                    ],
                    axis=0,
                )
                result = jnp.dot(left(0), right, preferred_element_type=jnp.float32)
            else:
                right = jnp.concatenate(
                    [
                        source[c_base + clip * own : c_base + (clip + 1) * own, :]
                        for source in sources
                        for clip in range(clips)
                    ],
                    axis=0,
                )
                result = jnp.dot(left(1), right, preferred_element_type=jnp.float32)
            if tap < 4:
                emit(result, place[5], tap, channels // 8, 0, sx, kx)
            else:
                emit(result, place[5], tap - 4, channels // 8, 1, sy, ky)


def weights_unit(place, mine, other, keep, unit, own, rim, clips):
    channels = mine.shape[1]
    outs = emit_outputs(4, channels // 8)
    return pl.pallas_call(
        functools.partial(weights_kernel, 3**unit, own, rim, clips),
        grid=(KSIZE + 1,),
        in_specs=[smem(), whole(mine), whole(other), whole(keep)],
        out_specs=[whole(out) for out in outs],
        out_shape=outs,
        scratch_shapes=[
            pltpu.VMEM((2 * clips, channels // LANES, own + 2 * rim, LANES), jnp.float32)
        ],
        compiler_params=compiler_params(),
        name="unit_weights",
    )(place, mine, other, keep)


def relative_rows(place, ref, block, start, count):
    pieces = []
    for rx in range(2):
        for ry in range(2):
            pair = jnp.bitwise_xor(place[4], ry) * 4 + jnp.bitwise_xor(place[3], rx) * 2
            first = pl.multiple_of((pair + place[2]) * block + start, 16)
            pieces.append(ref[pl.ds(first, count), :])
    return jnp.concatenate(pieces, axis=0)


def up_kernel(place, mine_ref, other_ref, sx, kx, sy, ky, turned):
    latents = mine_ref.shape[0]
    channels = turned.shape[0]
    for source, ref in enumerate((mine_ref, other_ref)):
        turned[:, source * latents : (source + 1) * latents] = jnp.transpose(ref[:, :channels])
    left = relative_rows(place, turned, channels // 8, 0, channels // 8)
    for tap in range(8):
        right = jnp.concatenate(
            [
                jnp.concatenate(
                    [
                        ref[:, channels + (z * 8 + tap) * LANES : channels + (z * 8 + tap + 1) * LANES]
                        for z in range(4)
                    ],
                    axis=1,
                )
                for ref in (mine_ref, other_ref)
            ],
            axis=0,
        )
        result = jnp.dot(left, right, preferred_element_type=jnp.float32)
        if tap < 4:
            emit(result, place[5], tap, channels // 8, 0, sx, kx)
        else:
            emit(result, place[5], tap - 4, channels // 8, 1, sy, ky)


def up_gradient(place, mine, other, channels):
    outs = emit_outputs(4, channels // 8)
    return pl.pallas_call(
        up_kernel,
        grid=(1,),
        in_specs=[smem(), whole(mine), whole(other)],
        out_specs=[whole(out) for out in outs],
        out_shape=outs,
        scratch_shapes=[pltpu.VMEM((channels, 2 * mine.shape[0]), jnp.bfloat16)],
        compiler_params=compiler_params(),
        name="upsample_weights",
    )(place, mine, other)


def down_kernel(
    place, codes_ref, mine_ref, other_ref, sx, kx, sy, ky, bsx, bkx, bsy, bky, turned
):
    latents = mine_ref.shape[0]
    long = turned.shape[0]
    channels = long // 8
    refs = (mine_ref, other_ref)
    for source, ref in enumerate(refs):
        turned[:, source * latents : (source + 1) * latents] = jnp.transpose(ref[:, :long])
    right = jnp.concatenate([ref[:, long : long + channels] for ref in refs], axis=0)
    block = channels // 8
    for tap in range(8):
        left = relative_rows(place, turned, channels, tap * block, block)
        result = jnp.dot(left, right, preferred_element_type=jnp.float32)
        if tap < 4:
            emit(result, place[5], tap, block, 0, sx, kx)
        else:
            emit(result, place[5], tap - 4, block, 1, sy, ky)
    lane = lax.broadcasted_iota(jnp.int32, (4 * 64, channels), 1)
    row = lax.broadcasted_iota(jnp.int32, (64, 2 * latents), 0)
    for book in range(4):
        gaps = jnp.concatenate(
            [
                ref[:, long + channels + book * channels : long + channels + (book + 1) * channels]
                for ref in refs
            ],
            axis=0,
        )
        codes = codes_ref[book : book + 1, :]
        parts = []
        for part in range(2):
            pieces = []
            for rx in range(2):
                for ry in range(2):
                    pair = jnp.bitwise_xor(place[4], ry) * 4 + jnp.bitwise_xor(place[3], rx) * 2
                    first = (pair + place[2]) * 128 + part * 64
                    pieces.append(jnp.where(codes == row + first, 1.0, 0.0).astype(jnp.bfloat16))
            parts.append(
                jnp.dot(
                    jnp.concatenate(pieces, axis=0), gaps, preferred_element_type=jnp.float32
                )
            )
        result = jnp.where(lax.rem(lane, LANES) < 64, parts[0], parts[1])
        if book < 2:
            emit(result, place[5], book, 64, 0, bsx, bkx)
        else:
            emit(result, place[5], book - 2, 64, 1, bsy, bky)


def down_gradient(place, codes, mine, other, channels):
    outs = emit_outputs(4, channels // 8) + emit_outputs(2, 64)
    return pl.pallas_call(
        down_kernel,
        grid=(1,),
        in_specs=[smem(), whole(codes), whole(mine), whole(other)],
        out_specs=[whole(out) for out in outs],
        out_shape=outs,
        scratch_shapes=[pltpu.VMEM((8 * channels, 2 * mine.shape[0]), jnp.bfloat16)],
        compiler_params=compiler_params(),
        name="downsample_weights",
    )(place, codes, mine, other)


def swap(block, bit):
    return lax.ppermute(block, "clip", [(i, i ^ bit) for i in range(lax.axis_size("clip"))])


def turn(block, distance):
    count = lax.axis_size("tm")
    return lax.ppermute(block, "tm", [(i, (i + distance) % count) for i in range(count)])


def added(*parts):
    total = parts[0].astype(jnp.float32)
    for part in parts[1:]:
        total = total + part.astype(jnp.float32)
    return total


def scatter(pieces):
    sx, kx, sy, ky = pieces
    rx = swap(sx, 2)
    ry = swap(sy, 4)
    rx2 = swap(added(kx[1], rx[1]).astype(jnp.bfloat16), 4)
    ry2 = swap(added(ky[1], ry[1]).astype(jnp.bfloat16), 2)
    blocks = jnp.concatenate(
        [
            added(kx[0], rx[0], rx2).astype(jnp.bfloat16),
            added(ky[0], ry[0], ry2).astype(jnp.bfloat16),
        ],
        axis=1,
    )
    return added(blocks[0], *(turn(blocks[distance], distance) for distance in range(1, 4)))


def with_neighbours(block, reach):
    count = lax.axis_size("tm")
    ends = count - 1
    head = block[:, :reach]
    tail = block[:, block.shape[1] - reach :]
    return jnp.concatenate(
        [
            lax.ppermute(tail, "tm", [(i, i + 1) for i in range(ends)]),
            block,
            lax.ppermute(head, "tm", [(i + 1, i) for i in range(ends)]),
        ],
        axis=1,
    )


def forward_stack(where, start, kernels, biases, mixers, shifts, own):
    length = start.shape[1]
    rim = (length - own) // 2 - GRAD_REACH * HOP_FACTOR
    stream = start
    kept = []
    for unit in range(UNITS):
        last = unit == UNITS - 1
        first, rows = (rim, length - 2 * rim) if last else (0, length)
        e, p, stream = forward_unit(
            where, stream, kernels, biases[:, None, :], mixers, shifts[:, None, :], unit, first, rows
        )
        kept.append((e, p))
    return stream, kept


def backward_stack(places, grad, kept, kernels, mixers, own):
    rims = (16, 16, 32)
    reach = kept[0][0].shape[1]
    results = [None] * UNITS
    sums = [None] * UNITS
    for unit in reversed(range(UNITS)):
        e, p = kept[unit]
        rows = own if unit == 0 else own + 32
        length = grad.shape[1]
        send, keep, grad, total = backward_unit(
            places[length],
            grad,
            p,
            e,
            kernels,
            mixers,
            unit,
            rows,
            (p.shape[1] - length) // 2,
            (reach - rows) // 2,
            own,
            rims[unit],
        )
        results[unit] = (send, swap(send, 1), keep)
        sums[unit] = total
    return grad, results, sums


def unit_scatters(place, results, own, clips):
    rims = (16, 16, 32)
    out = [None] * UNITS
    for unit in reversed(range(UNITS)):
        send, other, keep = results[unit]
        out[unit] = scatter(weights_unit(place, send, other, keep, unit, own, rims[unit], clips))
    return out


def split_units(reduced, channels):
    block = channels // 8
    taps = [part.reshape(8, block, LANES) for part in reduced]
    return jnp.stack([part[:KSIZE] for part in taps]), jnp.stack([part[KSIZE] for part in taps])


def fast_device(
    incoming_samples,
    sample_extents,
    chosen_entries,
    encoder_dilated_kernels,
    encoder_dilated_biases,
    encoder_pointwise_tables,
    encoder_pointwise_offsets,
    reducing_filter,
    reducing_offset,
    quantizer_tables,
    widening_filter,
    widening_offset,
    decoder_dilated_filters,
    decoder_dilated_offsets,
    decoder_pointwise_tables,
    decoder_pointwise_offsets,
    result_cotangent,
):
    f32, bf16 = jnp.float32, jnp.bfloat16
    segment = lax.axis_index("tm")
    member = lax.axis_index("clip")
    clips, frames, channels = incoming_samples.shape
    latents = frames // HOP_FACTOR
    all_frames = frames * lax.axis_size("tm")
    first_frame = segment * frames
    group_width = channels // GROUPS

    def bounds(reach):
        return jnp.stack([reach - first_frame, all_frames - first_frame + reach])

    coordinates = jnp.stack(
        [member % 2, (member // 2) % 2, (member // 4) % 2, segment]
    ).astype(jnp.int32)

    def placed(reach):
        return jnp.concatenate([bounds(reach).astype(jnp.int32), coordinates])

    reach = LATENT_REACH * HOP_FACTOR
    grad_reach = GRAD_REACH * HOP_FACTOR
    where = bounds(reach).astype(jnp.int32)
    places = {frames + 2 * r: placed(r) for r in (grad_reach, 16)}
    place = places[frames + 32]

    codes = with_neighbours(chosen_entries, LATENT_REACH)
    cotangent = with_neighbours(result_cotangent, grad_reach)
    samples = with_neighbours(incoming_samples, reach)

    code_range = jnp.arange(quantizer_tables.shape[2], dtype=jnp.int32)
    picked = [
        [
            jnp.einsum(
                "cnk,kd->cnd",
                (codes[:, :, g * LEVELS + l][..., None] == code_range).astype(bf16),
                quantizer_tables[g, l],
                preferred_element_type=f32,
            )
            for l in range(LEVELS)
        ]
        for g in range(GROUPS)
    ]
    quantized_wide = jnp.concatenate([sum(rows) for rows in picked], axis=2).astype(bf16)
    mid = slice(LATENT_REACH, LATENT_REACH + latents)
    quantized = quantized_wide[:, mid]
    widened = jnp.einsum("cnd,de->cne", quantized_wide, widening_filter, preferred_element_type=f32)
    start = (
        widened.reshape(clips, frames + 2 * reach, channels) + widening_offset.astype(f32)
    ).astype(bf16)

    decoded, decoder_kept = forward_stack(
        where,
        start,
        decoder_dilated_filters,
        decoder_dilated_offsets,
        decoder_pointwise_tables,
        decoder_pointwise_offsets,
        frames,
    )
    output = decoded[:, grad_reach : grad_reach + frames].astype(bf16)
    grad_start, decoder_work, decoder_sums = backward_stack(
        places, cotangent, decoder_kept, decoder_dilated_filters, decoder_pointwise_tables, frames
    )
    decoder_reduced = unit_scatters(place, decoder_work, frames, clips)

    widened_grad = grad_start.astype(bf16)
    spreading = jnp.sum(widened_grad.astype(f32), axis=(0, 1))
    folded = widened_grad.reshape(clips * latents, HOP_FACTOR * channels)
    up_send = jnp.concatenate([quantized.reshape(clips * latents, channels), folded], axis=1)
    up_reduced = scatter(up_gradient(place, up_send, swap(up_send, 1), channels))
    latent_grad = lax.dot_general(
        folded, widening_filter, NT, preferred_element_type=f32
    ).reshape(clips, latents, channels)

    encoded, encoder_kept = forward_stack(
        where,
        samples,
        encoder_dilated_kernels,
        encoder_dilated_biases,
        encoder_pointwise_tables,
        encoder_pointwise_offsets,
        frames,
    )
    pooled_wide = elu(encoded).astype(bf16)
    pooled = pooled_wide[:, grad_reach : grad_reach + frames].reshape(
        clips * latents, HOP_FACTOR * channels
    )
    latent = (
        jnp.dot(pooled, reducing_filter, preferred_element_type=f32) + reducing_offset.astype(f32)
    ).reshape(clips, latents, channels)
    validity = (
        (first_frame + HOP_FACTOR * jnp.arange(latents, dtype=jnp.int32))[None, :]
        < sample_extents[:, None]
    ).astype(f32)
    masked = validity[..., None]
    loss_local = jnp.float32(0.0)
    commits, book_rows = [], []
    for g in range(GROUPS):
        residue = latent[:, :, g * group_width : (g + 1) * group_width]
        commit_sum = jnp.zeros_like(residue)
        for l in range(LEVELS):
            residue = residue - picked[g][l][:, mid]
            loss_local = loss_local + jnp.sum(masked * residue * residue)
            commit_sum = commit_sum + residue
            gap = (-2.0 * masked * residue).astype(bf16)
            gap = gap.reshape(clips * latents, 4, 1, group_width // 4)
            book_rows.append(
                jnp.broadcast_to(gap, (clips * latents, 4, 2, group_width // 4)).reshape(
                    clips * latents, 2 * group_width
                )
            )
        commits.append(2.0 * commit_weight * masked * commit_sum)
    glatent = (latent_grad + jnp.concatenate(commits, axis=2)).astype(bf16)
    pooling = jnp.sum(glatent.astype(f32), axis=(0, 1))
    glatent_wide = with_neighbours(glatent, GRAD_REACH)
    down_send = jnp.concatenate(
        [pooled, glatent.reshape(clips * latents, channels)] + book_rows, axis=1
    )
    own_codes = chosen_entries.reshape(clips * latents, GROUPS * LEVELS).T
    pair_codes = jnp.concatenate([own_codes, swap(own_codes, 1)], axis=1)
    down = down_gradient(place, pair_codes, down_send, swap(down_send, 1), channels)
    down_reduced = scatter(down[:4])
    book_reduced = scatter(down[4:])

    pooled_grad = lax.dot_general(
        glatent_wide.reshape(-1, channels), reducing_filter, NT, preferred_element_type=f32
    ).reshape(clips, frames + 2 * grad_reach, channels) * slope_from_elu(pooled_wide.astype(f32))
    grad_samples, encoder_work, encoder_sums = backward_stack(
        places,
        pooled_grad,
        encoder_kept,
        encoder_dilated_kernels,
        encoder_pointwise_tables,
        frames,
    )
    input_grad = grad_samples.astype(bf16)
    encoder_reduced = unit_scatters(place, encoder_work, frames, clips)

    count_local = jnp.sum((sample_extents + HOP_FACTOR - 1) // HOP_FACTOR).astype(f32)
    scalars = jnp.zeros((2, channels), f32).at[0, 0].set(loss_local).at[0, 1].set(count_local)
    small = jnp.concatenate(
        [t[:2] for t in encoder_sums]
        + [t[:2] for t in decoder_sums]
        + [pooling[None], spreading[None], scalars],
        axis=0,
    )
    for bit in (1, 2, 4):
        small = small + swap(small, bit)
    for bit in (1, 2):
        pairs = [(i, i ^ bit) for i in range(lax.axis_size("tm"))]
        small = small + lax.ppermute(small, "tm", pairs)
    loss_sum = (1.0 + commit_weight) * small[14, 0]
    total_count = small[14, 1] / lax.axis_size("tm")
    masked_loss = loss_sum / (total_count * channels)

    analysis, mixers = split_units(encoder_reduced, channels)
    synthesis, remixers = split_units(decoder_reduced, channels)
    block = channels // 8
    upsample = up_reduced.reshape(8, block, LANES).transpose(1, 0, 2).reshape(block, 8 * LANES)
    downsample = down_reduced.reshape(8 * block, LANES)
    codebooks = (
        book_reduced.reshape(GROUPS, LEVELS, 64, 2, 64)
        .transpose(0, 1, 3, 2, 4)
        .reshape(GROUPS, LEVELS, 128, 64)
    )
    return (
        output,
        quantized,
        masked_loss,
        input_grad,
        analysis,
        small[0:6:2],
        mixers,
        small[1:6:2],
        downsample,
        small[12],
        codebooks,
        upsample,
        small[13],
        synthesis,
        small[6:12:2],
        remixers,
        small[7:12:2],
    )


def solution(mesh):
    placed = (
        P("clip", "tm", None),
        P("clip"),
        P("clip", "tm", None),
        P(),
        P(),
        P(),
        P(),
        P(),
        P(),
        P(),
        P(),
        P(),
        P(),
        P(),
        P(),
        P(),
        P("clip", "tm", None),
    )
    matched = mesh.shape["clip"] == 8 and mesh.shape["tm"] == 4
    return jax.shard_map(
        fast_device if matched else on_device,
        mesh=mesh,
        in_specs=placed,
        out_specs=(
            P("clip", "tm", None),
            P("clip", "tm", None),
            P(),
            P("clip", "tm", None),
            P(None, None, "clip", "tm"),
            P(),
            P(None, "clip", "tm"),
            P(),
            P("clip", "tm"),
            P(),
            P(None, None, "clip", "tm"),
            P("clip", "tm"),
            P(),
            P(None, None, "clip", "tm"),
            P(),
            P(None, "clip", "tm"),
            P(),
        ),
        check_vma=False,
    )
```

```python
import functools

import jax
import jax.numpy as jnp
from jax import lax
from jax.experimental import pallas as pl
from jax.experimental.pallas import tpu as pltpu
from jax.sharding import PartitionSpec as P

GROUPS = 2
LEVELS = 2
KSIZE = 7
UNITS = 3
HOP_FACTOR = 8


commit_weight = 0.25


def from_behind(block, axis, distance):
    devices = range(lax.axis_size(axis))
    route = [(i - distance, i) for i in devices if i - distance in devices]
    return lax.ppermute(block, axis, route)


def padded(cells, sides, width):
    for axis, dim in sides:
        count = lax.axis_size(axis)
        ends = count - 1
        head = lax.slice_in_dim(cells, 0, width, axis=dim)
        tail = lax.slice_in_dim(cells, cells.shape[dim] - width, cells.shape[dim], axis=dim)
        cells = jnp.concatenate(
            [
                lax.ppermute(tail, axis, [(i, (i + 1) % count) for i in range(ends)]),
                cells,
                lax.ppermute(head, axis, [((i + 1) % count, i) for i in range(ends)]),
            ],
            axis=dim,
        )
    return cells


def elu_slope(values):
    return jnp.where(values > 0, 1.0, jnp.exp(jnp.minimum(values, 0.0)))


def gather_taps(source, dilation, frames):
    return jnp.concatenate(
        [
            source[:, tap_index * dilation : tap_index * dilation + frames]
            for tap_index in range(KSIZE)
        ],
        axis=2,
    )


def dilated(source, kernel, dilation):
    frames = source.shape[1] - (KSIZE - 1) * dilation
    stacked = gather_taps(source, dilation, frames)
    flattened = kernel.reshape(KSIZE * kernel.shape[1], kernel.shape[2])
    return jnp.einsum("cti,io->cto", stacked, flattened, preferred_element_type=jnp.float32)


def dilated_back(source, kernel, dilation, grad_out):
    frames = grad_out.shape[1]
    stacked = gather_taps(source, dilation, frames)
    flattened = kernel.reshape(KSIZE * kernel.shape[1], kernel.shape[2])
    kernel_grad = jnp.einsum(
        "cti,cto->io", stacked, grad_out, preferred_element_type=jnp.float32
    ).reshape(kernel.shape)
    spread = jnp.einsum("cto,io->cti", grad_out, flattened, preferred_element_type=jnp.float32)
    channels = kernel.shape[1]
    source_grad = jnp.zeros(source.shape, jnp.float32)
    for tap_index in range(KSIZE):
        source_grad = source_grad.at[:, tap_index * dilation : tap_index * dilation + frames].add(
            spread[:, :, tap_index * channels : (tap_index + 1) * channels]
        )
    return (kernel_grad, source_grad)


def return_rims(grad_full, margin_width):
    length = grad_full.shape[1]
    owned = grad_full[:, margin_width : length - margin_width]
    from_above = from_behind(grad_full[:, :margin_width].astype(jnp.bfloat16), "tm", -1).astype(
        jnp.float32
    )
    from_below = from_behind(
        grad_full[:, length - margin_width :].astype(jnp.bfloat16), "tm", 1
    ).astype(jnp.float32)
    owned = owned.at[:, owned.shape[1] - margin_width :].add(from_above)
    return owned.at[:, :margin_width].add(from_below)


def unit_source(stream, margin_width):
    activated = jax.nn.elu(stream)
    return padded(activated.astype(jnp.bfloat16), (("tm", 1),), margin_width)


def source_back(source_grad, margin_width):
    return return_rims(source_grad, margin_width)


def stack_forward(
    stream,
    kernels,
    encoder_dilated_biases,
    encoder_pointwise_tables,
    encoder_pointwise_offsets,
    first_frame,
    frames,
):
    kept_list = []
    for unit_index in range(UNITS):
        dilation = 3**unit_index
        margin_width = KSIZE // 2 * dilation
        extra_frames = (stream.shape[1] - frames) // 2
        positions = first_frame - extra_frames + jnp.arange(stream.shape[1], dtype=jnp.int32)
        source = unit_source(stream, margin_width)
        before = dilated(source, kernels[unit_index], dilation) + encoder_dilated_biases[
            unit_index
        ].astype(jnp.float32)
        pointed = jax.nn.elu(before).astype(jnp.bfloat16)
        branch = jnp.einsum(
            "ctd,de->cte",
            pointed,
            encoder_pointwise_tables[unit_index],
            preferred_element_type=jnp.float32,
        )
        branch = branch + encoder_pointwise_offsets[unit_index].astype(jnp.float32)
        kept_list.append((stream, source, before, pointed, positions))
        stream = stream + branch
    return (stream, kept_list)


def stack_backward(grad_stream, kept_list, kernels, encoder_pointwise_tables):
    kernel_grads, offset_grads, mixer_grads, shift_grads = ([], [], [], [])
    for unit_index in reversed(range(UNITS)):
        stream, source, before, pointed, positions = kept_list[unit_index]
        dilation = 3**unit_index
        margin_width = KSIZE // 2 * dilation
        branch_grad = grad_stream.astype(jnp.bfloat16)
        mixer_grads.insert(
            0, jnp.einsum("ctd,cte->de", pointed, branch_grad, preferred_element_type=jnp.float32)
        )
        shift_grads.insert(0, jnp.sum(branch_grad.astype(jnp.float32), axis=(0, 1)))
        pointed_grad = jnp.einsum(
            "cte,de->ctd",
            branch_grad,
            encoder_pointwise_tables[unit_index],
            preferred_element_type=jnp.float32,
        )
        before_grad = (pointed_grad * elu_slope(before)).astype(jnp.bfloat16)
        offset_grads.insert(0, jnp.sum(before_grad.astype(jnp.float32), axis=(0, 1)))
        kernel_grad, source_grad = dilated_back(source, kernels[unit_index], dilation, before_grad)
        kernel_grads.insert(0, kernel_grad)
        owned_grad = source_back(source_grad, margin_width)
        grad_stream = grad_stream + owned_grad * elu_slope(stream)
    return (
        grad_stream,
        (
            jnp.stack(kernel_grads),
            jnp.stack(offset_grads),
            jnp.stack(mixer_grads),
            jnp.stack(shift_grads),
        ),
    )


def over_clips(matrices):
    return (
        lax.psum_scatter(
            matrices[0].astype(jnp.bfloat16), "clip", scatter_dimension=2, tiled=True
        ).astype(jnp.float32),
        lax.psum_scatter(
            matrices[1].astype(jnp.bfloat16), "clip", scatter_dimension=1, tiled=True
        ).astype(jnp.float32),
        lax.psum_scatter(
            matrices[2].astype(jnp.bfloat16), "clip", scatter_dimension=0, tiled=True
        ).astype(jnp.float32),
        lax.psum_scatter(
            matrices[3].astype(jnp.bfloat16), "clip", scatter_dimension=2, tiled=True
        ).astype(jnp.float32),
        lax.psum_scatter(
            matrices[4].astype(jnp.bfloat16), "clip", scatter_dimension=0, tiled=True
        ).astype(jnp.float32),
        lax.psum_scatter(
            matrices[5].astype(jnp.bfloat16), "clip", scatter_dimension=2, tiled=True
        ).astype(jnp.float32),
        lax.psum_scatter(
            matrices[6].astype(jnp.bfloat16), "clip", scatter_dimension=1, tiled=True
        ).astype(jnp.float32),
    )


def over_segments(matrices):
    return (
        lax.psum_scatter(
            matrices[0].astype(jnp.bfloat16), "tm", scatter_dimension=3, tiled=True
        ).astype(jnp.float32),
        lax.psum_scatter(
            matrices[1].astype(jnp.bfloat16), "tm", scatter_dimension=2, tiled=True
        ).astype(jnp.float32),
        lax.psum_scatter(
            matrices[2].astype(jnp.bfloat16), "tm", scatter_dimension=1, tiled=True
        ).astype(jnp.float32),
        lax.psum_scatter(
            matrices[3].astype(jnp.bfloat16), "tm", scatter_dimension=3, tiled=True
        ).astype(jnp.float32),
        lax.psum_scatter(
            matrices[4].astype(jnp.bfloat16), "tm", scatter_dimension=1, tiled=True
        ).astype(jnp.float32),
        lax.psum_scatter(
            matrices[5].astype(jnp.bfloat16), "tm", scatter_dimension=3, tiled=True
        ).astype(jnp.float32),
        lax.psum_scatter(
            matrices[6].astype(jnp.bfloat16), "tm", scatter_dimension=2, tiled=True
        ).astype(jnp.float32),
    )


def on_device(
    incoming_samples,
    sample_extents,
    chosen_entries,
    encoder_dilated_kernels,
    encoder_dilated_biases,
    encoder_pointwise_tables,
    encoder_pointwise_offsets,
    reducing_filter,
    reducing_offset,
    quantizer_tables,
    widening_filter,
    widening_offset,
    decoder_dilated_filters,
    decoder_dilated_offsets,
    decoder_pointwise_tables,
    decoder_pointwise_offsets,
    result_cotangent,
):
    segment = lax.axis_index("tm")
    clips = incoming_samples.shape[0]
    frames = incoming_samples.shape[1]
    channels = incoming_samples.shape[2]
    first_frame = segment * frames
    latents = frames // HOP_FACTOR
    total_count = lax.psum(
        jnp.sum((sample_extents + HOP_FACTOR - 1) // HOP_FACTOR).astype(jnp.float32), "clip"
    )
    stream = incoming_samples.astype(jnp.float32)
    encoded, encoder_kept = stack_forward(
        stream,
        encoder_dilated_kernels,
        encoder_dilated_biases,
        encoder_pointwise_tables,
        encoder_pointwise_offsets,
        first_frame,
        frames,
    )
    reduced_samples = (
        jax.nn.elu(encoded).astype(jnp.bfloat16).reshape(clips, latents, HOP_FACTOR * channels)
    )
    latent = jnp.einsum(
        "kde,er->kdr", reduced_samples, reducing_filter, preferred_element_type=jnp.float32
    ) + reducing_offset.astype(jnp.float32)
    validity = (
        (first_frame + HOP_FACTOR * jnp.arange(latents, dtype=jnp.int32))[None, :]
        < sample_extents[:, None]
    ).astype(jnp.float32)
    masked = validity[..., None]
    group_width = channels // GROUPS
    code_range = jnp.arange(quantizer_tables.shape[2], dtype=jnp.int32)
    loss_local = jnp.float32(0.0)
    quant_parts, commit_parts, book_rows = ([], [], [])
    for group_index in range(GROUPS):
        residue = latent[:, :, group_index * group_width : (group_index + 1) * group_width]
        commit_sum = jnp.zeros_like(residue)
        group_code = jnp.zeros_like(residue)
        level_rows = []
        for level_index in range(LEVELS):
            column = group_index * LEVELS + level_index
            onehot = (chosen_entries[:, :, column][..., None] == code_range).astype(jnp.bfloat16)
            picked = jnp.einsum(
                "kde,er->kdr",
                onehot,
                quantizer_tables[group_index, level_index],
                preferred_element_type=jnp.float32,
            )
            residue = residue - picked
            level_rows.append(
                jnp.einsum(
                    "cnk,cnd->kd",
                    onehot.astype(jnp.float32),
                    -2.0 * masked * residue,
                    precision=lax.Precision.HIGHEST,
                    preferred_element_type=jnp.float32,
                )
            )
            commit_sum = commit_sum + residue
            loss_local = loss_local + jnp.sum(masked * residue * residue)
            group_code = group_code + picked
        book_rows.append(jnp.stack(level_rows))
        commit_parts.append(2.0 * commit_weight * masked * commit_sum)
        quant_parts.append(group_code)
    loss_local = (1.0 + commit_weight) * loss_local
    quantized = jnp.concatenate(quant_parts, axis=2).astype(jnp.bfloat16)
    loss_sum = lax.psum(loss_local, ("clip", "tm"))
    masked_loss = loss_sum / (total_count * channels)
    widened = jnp.einsum(
        "cnd,de->cne", quantized, widening_filter, preferred_element_type=jnp.float32
    )
    decoder_start = (
        widened.reshape(clips, frames, channels) + widening_offset.astype(jnp.float32)
    ).astype(jnp.bfloat16)
    stream = decoder_start.astype(jnp.float32)
    decoded, decoder_kept = stack_forward(
        stream,
        decoder_dilated_filters,
        decoder_dilated_offsets,
        decoder_pointwise_tables,
        decoder_pointwise_offsets,
        first_frame,
        frames,
    )
    output = decoded.astype(jnp.bfloat16)
    grad_decoder, decoder_grads = stack_backward(
        result_cotangent.astype(jnp.float32),
        decoder_kept,
        decoder_dilated_filters,
        decoder_pointwise_tables,
    )
    widened_grad = grad_decoder.astype(jnp.bfloat16)
    spreading_grad = jnp.sum(widened_grad.astype(jnp.float32), axis=(0, 1))
    folded_grad = widened_grad.reshape(clips, latents, HOP_FACTOR * channels)
    upsample_grad = jnp.einsum(
        "cnd,cne->de", quantized, folded_grad, preferred_element_type=jnp.float32
    )
    latent_grad = jnp.einsum(
        "cne,de->cnd", folded_grad, widening_filter, preferred_element_type=jnp.float32
    )
    hidden_first_half = (latent_grad + jnp.concatenate(commit_parts, axis=2)).astype(jnp.bfloat16)
    pooling_grad = jnp.sum(hidden_first_half.astype(jnp.float32), axis=(0, 1))
    downsampling_gradient = jnp.einsum(
        "cnk,cnd->kd", reduced_samples, hidden_first_half, preferred_element_type=jnp.float32
    )
    pooled_grad = jnp.einsum(
        "npk,xk->npx", hidden_first_half, reducing_filter, preferred_element_type=jnp.float32
    )
    pooled_grad = pooled_grad.reshape(clips, frames, channels) * elu_slope(encoded)
    grad_encoder, encoder_grads = stack_backward(
        pooled_grad, encoder_kept, encoder_dilated_kernels, encoder_pointwise_tables
    )
    input_grad = grad_encoder.astype(jnp.bfloat16)
    codebook_grad = jnp.stack(book_rows)
    matrices = (
        encoder_grads[0],
        encoder_grads[2],
        downsampling_gradient,
        codebook_grad,
        upsample_grad,
        decoder_grads[0],
        decoder_grads[2],
    )
    matrices = over_segments(over_clips(matrices))
    biases = lax.psum(
        (
            encoder_grads[1],
            encoder_grads[3],
            pooling_grad,
            spreading_grad,
            decoder_grads[1],
            decoder_grads[3],
        ),
        ("clip", "tm"),
    )
    return (
        output,
        quantized,
        masked_loss,
        input_grad,
        matrices[0],
        biases[0],
        matrices[1],
        biases[1],
        matrices[2],
        biases[2],
        matrices[3],
        matrices[4],
        biases[3],
        matrices[5],
        biases[4],
        matrices[6],
        biases[5],
    )

PAD = 32
LANES = 128
LATENT_REACH = 10
GRAD_REACH = 6
NT = (((1,), (1,)), ((), ()))
VMEM_BYTES = 60 * 1024 * 1024


def elu(values):
    return jnp.where(values > 0, values, jnp.exp(jnp.minimum(values, 0.0)) - 1.0)


def slope_from_elu(activated):
    return jnp.where(activated > 0, 1.0, activated + 1.0)


def whole(array):
    return pl.BlockSpec(array.shape, lambda i: (0,) * len(array.shape))


def smem():
    return pl.BlockSpec(memory_space=pltpu.SMEM)


def compiler_params():
    return pltpu.CompilerParams(
        vmem_limit_bytes=VMEM_BYTES, dimension_semantics=("arbitrary",)
    )


def forward_kernel(
    unit, first, rows, where_ref, h_ref, w_ref, b_ref, m_ref, s_ref, e_ref, p_ref, out_ref, lines
):
    clips, length, channels = h_ref.shape
    dilation = 3**unit
    low, high = where_ref[0], where_ref[1]
    tiles = channels // LANES
    position = lax.broadcasted_iota(jnp.int32, (length, LANES), 0)
    inside = (position >= low) & (position < high)
    for clip in range(clips):
        for tile in range(tiles):
            lanes = slice(tile * LANES, (tile + 1) * LANES)
            lines[clip, tile, :PAD, :] = jnp.zeros((PAD, LANES), jnp.float32)
            lines[clip, tile, PAD + length :, :] = jnp.zeros((PAD, LANES), jnp.float32)
            active = jnp.where(inside, elu(h_ref[clip, :, lanes].astype(jnp.float32)), 0.0)
            active = active.astype(jnp.bfloat16)
            e_ref[clip, :, lanes] = active
            lines[clip, tile, PAD : PAD + length, :] = active.astype(jnp.float32)
    kernel = w_ref[0].reshape(KSIZE * channels, channels)
    mixer = m_ref[0]
    for clip in range(clips):
        taps = []
        for tap in range(KSIZE):
            start = PAD + first + (tap - KSIZE // 2) * dilation
            for tile in range(tiles):
                taps.append(lines[clip, tile, start : start + rows, :].astype(jnp.bfloat16))
        before = jnp.dot(
            jnp.concatenate(taps, axis=1), kernel, preferred_element_type=jnp.float32
        )
        pointed = elu(before + b_ref[unit : unit + 1, :].astype(jnp.float32)).astype(jnp.bfloat16)
        p_ref[clip] = pointed
        branch = jnp.dot(pointed, mixer, preferred_element_type=jnp.float32)
        branch = branch + s_ref[unit : unit + 1, :].astype(jnp.float32)
        stream = h_ref[clip, first : first + rows, :].astype(jnp.float32)
        out_ref[clip] = (stream + branch).astype(out_ref.dtype)


def forward_unit(where, h, kernels, biases, mixers, shifts, unit, first, rows):
    clips, length, channels = h.shape
    outs = (
        jax.ShapeDtypeStruct((clips, length, channels), jnp.bfloat16),
        jax.ShapeDtypeStruct((clips, rows, channels), jnp.bfloat16),
        jax.ShapeDtypeStruct((clips, rows, channels), jnp.float32),
    )
    return pl.pallas_call(
        functools.partial(forward_kernel, unit, first, rows),
        grid=(1,),
        in_specs=[
            smem(),
            whole(h),
            pl.BlockSpec((1, KSIZE, channels, channels), lambda i: (unit, 0, 0, 0)),
            whole(biases),
            pl.BlockSpec((1, channels, channels), lambda i: (unit, 0, 0)),
            whole(shifts),
        ],
        out_specs=[whole(out) for out in outs],
        out_shape=outs,
        scratch_shapes=[
            pltpu.VMEM((clips, channels // LANES, length + 2 * PAD, LANES), jnp.float32)
        ],
        compiler_params=compiler_params(),
        name="unit_forward",
    )(where, h, kernels, biases, mixers, shifts)


def backward_kernel(
    dilation,
    rows,
    p_first,
    e_first,
    own,
    rim,
    place,
    gh_ref,
    p_ref,
    e_ref,
    w_ref,
    m_ref,
    send_ref,
    keep_ref,
    out_ref,
    sum_ref,
    lines,
    turned,
):
    clips, length, channels = gh_ref.shape
    tiles = channels // LANES
    own_first = (length - own) // 2
    shift = (length - rows) // 2
    wide = own + 2 * rim
    low, high, core = place[0], place[1], place[2]
    mixer = m_ref[0]
    position = lax.broadcasted_iota(jnp.int32, (length, channels), 0)
    inside = (position >= low) & (position < high)
    for clip in range(clips):
        gc = gh_ref[clip].astype(jnp.bfloat16)
        send_ref[clips * wide + clip * own : clips * wide + (clip + 1) * own, :] = gc[
            own_first : own_first + own
        ]
        gp = lax.dot_general(gc, mixer, NT, preferred_element_type=jnp.float32)
        pointed = p_ref[clip, p_first : p_first + length, :].astype(jnp.float32)
        ga = jnp.where(inside, gp * slope_from_elu(pointed), 0.0).astype(jnp.bfloat16)
        send_ref[clip * wide : (clip + 1) * wide, :] = ga[
            own_first - rim : own_first + own + rim
        ]
        ga = ga.astype(jnp.float32)
        a_sum = jnp.sum(ga[own_first : own_first + own], axis=0, keepdims=True)
        c_sum = jnp.sum(
            gc[own_first : own_first + own].astype(jnp.float32), axis=0, keepdims=True
        )
        if clip == 0:
            sum_ref[0:1, :] = a_sum
            sum_ref[1:2, :] = c_sum
        else:
            sum_ref[0:1, :] = sum_ref[0:1, :] + a_sum
            sum_ref[1:2, :] = sum_ref[1:2, :] + c_sum
        for tile in range(tiles):
            lines[clip, tile, :PAD, :] = jnp.zeros((PAD, LANES), jnp.float32)
            lines[clip, tile, PAD + length :, :] = jnp.zeros((PAD, LANES), jnp.float32)
            lines[clip, tile, PAD : PAD + length, :] = ga[:, tile * LANES : (tile + 1) * LANES]
    total = None
    for tap in range(KSIZE):
        start = PAD + shift - (tap - KSIZE // 2) * dilation
        moved = jnp.concatenate(
            [
                jnp.concatenate(
                    [
                        lines[clip, tile, start : start + rows, :].astype(jnp.bfloat16)
                        for tile in range(tiles)
                    ],
                    axis=1,
                )
                for clip in range(clips)
            ],
            axis=0,
        )
        part = lax.dot_general(moved, w_ref[0, tap], NT, preferred_element_type=jnp.float32)
        total = part if total is None else total + part
    for clip in range(clips):
        active = e_ref[clip, e_first : e_first + rows, :].astype(jnp.float32)
        out_ref[clip] = gh_ref[clip, shift : shift + rows, :].astype(jnp.float32) + total[
            clip * rows : (clip + 1) * rows
        ] * slope_from_elu(active)
    base = clips * (wide + own)
    block = channels // 8
    sources = ((e_ref, e_first + (rows - own) // 2), (p_ref, p_first + own_first))
    for which, (ref, start) in enumerate(sources):
        for clip in range(clips):
            turned[...] = jnp.transpose(ref[clip, start : start + own, :])
            for rx in range(2):
                for ry in range(2):
                    pair = jnp.bitwise_xor(place[4], ry) * 4 + jnp.bitwise_xor(place[3], rx) * 2
                    to = (which * clips + clip) * (channels // 2) + (rx * 2 + ry) * block
                    mine = pl.multiple_of((pair + core) * block, block)
                    other = pl.multiple_of((pair + 1 - core) * block, block)
                    keep_ref[to : to + block, :] = turned[pl.ds(mine, block), :]
                    send_ref[base + to : base + to + block, :] = turned[pl.ds(other, block), :]


def backward_unit(place, gh, p, e, kernels, mixers, unit, rows, p_first, e_first, own, rim):
    clips, length, channels = gh.shape
    payload = clips * (2 * own + 2 * rim + channels)
    outs = (
        jax.ShapeDtypeStruct((payload, channels), jnp.bfloat16),
        jax.ShapeDtypeStruct((clips * channels, own), jnp.bfloat16),
        jax.ShapeDtypeStruct((clips, rows, channels), jnp.float32),
        jax.ShapeDtypeStruct((8, channels), jnp.float32),
    )
    return pl.pallas_call(
        functools.partial(backward_kernel, 3**unit, rows, p_first, e_first, own, rim),
        grid=(1,),
        in_specs=[
            smem(),
            whole(gh),
            whole(p),
            whole(e),
            pl.BlockSpec((1, KSIZE, channels, channels), lambda i: (unit, 0, 0, 0)),
            pl.BlockSpec((1, channels, channels), lambda i: (unit, 0, 0)),
        ],
        out_specs=[whole(out) for out in outs],
        out_shape=outs,
        scratch_shapes=[
            pltpu.VMEM((clips, channels // LANES, length + 2 * PAD, LANES), jnp.float32),
            pltpu.VMEM((channels, own), jnp.bfloat16),
        ],
        compiler_params=compiler_params(),
        name="unit_backward",
    )(place, gh, p, e, kernels, mixers)


def emit(result, z, start, tap_rows, first_axis, send_ref, keep_ref):
    result = result.astype(jnp.bfloat16)
    quarter = result.shape[0] // 4
    for rx in range(2):
        for ry in range(2):
            first, second = (rx, ry) if first_axis == 0 else (ry, rx)
            target = send_ref if first == 1 else keep_ref
            rows = slice((rx * 2 + ry) * quarter, (rx * 2 + ry + 1) * quarter)
            for segment in range(4):
                relative = lax.rem(segment - z + 4, 4)
                target[second, relative, start : start + tap_rows, :] = result[
                    rows, segment * LANES : (segment + 1) * LANES
                ]


def emit_outputs(rows):
    out = jax.ShapeDtypeStruct((2, 4, rows, LANES), jnp.bfloat16)
    return (out,) * 4


def weights_kernel(
    dilation, own, rim, clips, place, mine_ref, other_ref, keep_ref, sx, kx, sy, ky, lines
):
    channels = mine_ref.shape[1]
    tiles = channels // LANES
    half = channels // 2
    wide = own + 2 * rim
    c_base = clips * wide
    base = c_base + clips * own
    sources = (mine_ref, other_ref)
    step = pl.program_id(0)

    @pl.when(step == 0)
    def _():
        for source in range(2):
            for clip in range(clips):
                for tile in range(tiles):
                    lines[source * clips + clip, tile, :, :] = sources[source][
                        clip * wide : (clip + 1) * wide, tile * LANES : (tile + 1) * LANES
                    ].astype(jnp.float32)

    def left(which):
        pieces = [
            keep_ref[(which * clips + clip) * half : (which * clips + clip + 1) * half, :]
            for clip in range(clips)
        ] + [
            other_ref[
                base + (which * clips + clip) * half : base + (which * clips + clip + 1) * half, :
            ]
            for clip in range(clips)
        ]
        return jnp.concatenate(pieces, axis=1)

    for tap in range(KSIZE + 1):

        @pl.when(step == tap)
        def _(tap=tap):
            if tap < KSIZE:
                start = rim - (tap - KSIZE // 2) * dilation
                right = jnp.concatenate(
                    [
                        jnp.concatenate(
                            [
                                lines[item, tile, start : start + own, :].astype(jnp.bfloat16)
                                for tile in range(tiles)
                            ],
                            axis=1,
                        )
                        for item in range(2 * clips)
                    ],
                    axis=0,
                )
                result = jnp.dot(left(0), right, preferred_element_type=jnp.float32)
            else:
                right = jnp.concatenate(
                    [
                        source[c_base + clip * own : c_base + (clip + 1) * own, :]
                        for source in sources
                        for clip in range(clips)
                    ],
                    axis=0,
                )
                result = jnp.dot(left(1), right, preferred_element_type=jnp.float32)
            if tap < 4:
                emit(result, place[5], tap * (channels // 8), channels // 8, 0, sx, kx)
            else:
                emit(result, place[5], (tap - 4) * (channels // 8), channels // 8, 1, sy, ky)


def weights_unit(place, mine, other, keep, unit, own, rim, clips):
    channels = mine.shape[1]
    outs = emit_outputs(channels // 2)
    return pl.pallas_call(
        functools.partial(weights_kernel, 3**unit, own, rim, clips),
        grid=(KSIZE + 1,),
        in_specs=[smem(), whole(mine), whole(other), whole(keep)],
        out_specs=[whole(out) for out in outs],
        out_shape=outs,
        scratch_shapes=[
            pltpu.VMEM((2 * clips, channels // LANES, own + 2 * rim, LANES), jnp.float32)
        ],
        compiler_params=compiler_params(),
        name="unit_weights",
    )(place, mine, other, keep)


def relative_rows(place, ref, block, start, count):
    pieces = []
    for rx in range(2):
        for ry in range(2):
            pair = jnp.bitwise_xor(place[4], ry) * 4 + jnp.bitwise_xor(place[3], rx) * 2
            first = pl.multiple_of((pair + place[2]) * block + start, 16)
            pieces.append(ref[pl.ds(first, count), :])
    return jnp.concatenate(pieces, axis=0)


def up_kernel(place, mine_ref, other_ref, sx, kx, sy, ky, turned):
    latents = mine_ref.shape[0]
    channels = turned.shape[0]
    for source, ref in enumerate((mine_ref, other_ref)):
        turned[:, source * latents : (source + 1) * latents] = jnp.transpose(ref[:, :channels])
    left = relative_rows(place, turned, channels // 8, 0, channels // 8)
    for tap in range(8):
        right = jnp.concatenate(
            [
                jnp.concatenate(
                    [
                        ref[:, channels + (z * 8 + tap) * LANES : channels + (z * 8 + tap + 1) * LANES]
                        for z in range(4)
                    ],
                    axis=1,
                )
                for ref in (mine_ref, other_ref)
            ],
            axis=0,
        )
        result = jnp.dot(left, right, preferred_element_type=jnp.float32)
        if tap < 4:
            emit(result, place[5], tap * (channels // 8), channels // 8, 0, sx, kx)
        else:
            emit(result, place[5], (tap - 4) * (channels // 8), channels // 8, 1, sy, ky)


def up_gradient(place, mine, other, channels):
    outs = emit_outputs(channels // 2)
    return pl.pallas_call(
        up_kernel,
        grid=(1,),
        in_specs=[smem(), whole(mine), whole(other)],
        out_specs=[whole(out) for out in outs],
        out_shape=outs,
        scratch_shapes=[pltpu.VMEM((channels, 2 * mine.shape[0]), jnp.bfloat16)],
        compiler_params=compiler_params(),
        name="upsample_weights",
    )(place, mine, other)


def down_kernel(place, codes_ref, mine_ref, other_ref, sx, kx, sy, ky, turned):
    latents = mine_ref.shape[0]
    long = turned.shape[0]
    channels = long // 8
    refs = (mine_ref, other_ref)
    for source, ref in enumerate(refs):
        turned[:, source * latents : (source + 1) * latents] = jnp.transpose(ref[:, :long])
    right = jnp.concatenate([ref[:, long : long + channels] for ref in refs], axis=0)
    block = channels // 8
    for tap in range(8):
        left = relative_rows(place, turned, channels, tap * block, block)
        result = jnp.dot(left, right, preferred_element_type=jnp.float32)
        if tap < 4:
            emit(result, place[5], tap * block, block, 0, sx, kx)
        else:
            emit(result, place[5], (tap - 4) * block, block, 1, sy, ky)
    lane = lax.broadcasted_iota(jnp.int32, (4 * 64, channels), 1)
    row = lax.broadcasted_iota(jnp.int32, (64, 2 * latents), 0)
    for book in range(4):
        gaps = jnp.concatenate(
            [
                ref[:, long + channels + book * channels : long + channels + (book + 1) * channels]
                for ref in refs
            ],
            axis=0,
        )
        codes = codes_ref[book : book + 1, :]
        parts = []
        for part in range(2):
            pieces = []
            for rx in range(2):
                for ry in range(2):
                    pair = jnp.bitwise_xor(place[4], ry) * 4 + jnp.bitwise_xor(place[3], rx) * 2
                    first = (pair + place[2]) * 128 + part * 64
                    pieces.append(jnp.where(codes == row + first, 1.0, 0.0).astype(jnp.bfloat16))
            parts.append(
                jnp.dot(
                    jnp.concatenate(pieces, axis=0), gaps, preferred_element_type=jnp.float32
                )
            )
        result = jnp.where(lax.rem(lane, LANES) < 64, parts[0], parts[1])
        if book < 2:
            emit(result, place[5], 4 * block + book * 64, 64, 0, sx, kx)
        else:
            emit(result, place[5], 4 * block + (book - 2) * 64, 64, 1, sy, ky)


def down_gradient(place, codes, mine, other, channels):
    outs = emit_outputs(channels // 2 + 128)
    return pl.pallas_call(
        down_kernel,
        grid=(1,),
        in_specs=[smem(), whole(codes), whole(mine), whole(other)],
        out_specs=[whole(out) for out in outs],
        out_shape=outs,
        scratch_shapes=[pltpu.VMEM((8 * channels, 2 * mine.shape[0]), jnp.bfloat16)],
        compiler_params=compiler_params(),
        name="downsample_weights",
    )(place, codes, mine, other)


def swap(block, bit):
    return lax.ppermute(block, "clip", [(i, i ^ bit) for i in range(lax.axis_size("clip"))])


def turn(block, distance):
    count = lax.axis_size("tm")
    return lax.ppermute(block, "tm", [(i, (i + distance) % count) for i in range(count)])


def added(*parts):
    total = parts[0].astype(jnp.float32)
    for part in parts[1:]:
        total = total + part.astype(jnp.float32)
    return total


def after(value, *others):
    return lax.optimization_barrier((value,) + others)[0]


class Lane:
    def __init__(self):
        self.clock = None
        self.ready = ()
        self.pending = []

    def run(self, kernel, first, *others):
        if self.clock is not None:
            first = after(first, self.clock, *self.ready)
        outs = kernel(first, *others)
        self.clock = outs[0]
        self.ready = ()
        waiting, self.pending = self.pending, []
        for stage in waiting:
            stage()
        return outs

    def scatter(self, pieces, done):
        sx, kx, sy, ky = pieces
        rx, ry = swap(sx, 2), swap(sy, 4)

        def second():
            ax, ay, _ = lax.optimization_barrier((rx, ry, self.clock))
            bx = added(kx[1], ax[1]).astype(jnp.bfloat16)
            by = added(ky[1], ay[1]).astype(jnp.bfloat16)
            self.ready += (bx, by)
            rx2, ry2 = swap(bx, 4), swap(by, 2)

            def third():
                cx, cy, _ = lax.optimization_barrier((rx2, ry2, self.clock))
                done(
                    jnp.concatenate(
                        [
                            added(kx[0], ax[0], cx).astype(jnp.bfloat16),
                            added(ky[0], ay[0], cy).astype(jnp.bfloat16),
                        ],
                        axis=1,
                    )
                )

            self.pending.append(third)

        self.pending.append(second)

    def segments(self, groups, done):
        blocks = jnp.concatenate(groups, axis=1) if len(groups) > 1 else groups[0]
        self.ready += (blocks,)
        arrived = [turn(blocks[distance], distance) for distance in range(1, 4)]

        def last():
            total = added(blocks[0], *arrived)
            start = 0
            for group in groups:
                done.append(total[start : start + group.shape[1]])
                start += group.shape[1]

        self.pending.append(last)

    def finish(self):
        while self.pending:
            waiting, self.pending = self.pending, []
            for stage in waiting:
                stage()


def with_neighbours(block, reach):
    count = lax.axis_size("tm")
    ends = count - 1
    head = block[:, :reach]
    tail = block[:, block.shape[1] - reach :]
    return jnp.concatenate(
        [
            lax.ppermute(tail, "tm", [(i, i + 1) for i in range(ends)]),
            block,
            lax.ppermute(head, "tm", [(i + 1, i) for i in range(ends)]),
        ],
        axis=1,
    )


def with_both(one, reach_one, two, reach_two):
    ends = lax.axis_size("tm") - 1
    tail = jnp.concatenate(
        [one[:, one.shape[1] - reach_one :], two[:, two.shape[1] - reach_two :]], axis=1
    )
    head = jnp.concatenate([one[:, :reach_one], two[:, :reach_two]], axis=1)
    below = lax.ppermute(tail, "tm", [(i, i + 1) for i in range(ends)])
    above = lax.ppermute(head, "tm", [(i + 1, i) for i in range(ends)])
    return (
        jnp.concatenate([below[:, :reach_one], one, above[:, :reach_one]], axis=1),
        jnp.concatenate([below[:, reach_one:], two, above[:, reach_one:]], axis=1),
    )


def forward_stack(lane, where, start, kernels, biases, mixers, shifts, own, between=None):
    length = start.shape[1]
    rim = (length - own) // 2 - GRAD_REACH * HOP_FACTOR
    stream = start
    kept = []
    for unit in range(UNITS):
        last = unit == UNITS - 1
        first, rows = (rim, length - 2 * rim) if last else (0, length)
        e, p, stream = lane.run(
            lambda h: forward_unit(where, h, kernels, biases, mixers, shifts, unit, first, rows),
            stream,
        )
        kept.append((e, p))
        if between is not None and unit in between:
            between[unit]()
    return stream, kept


RIMS = (16, 16, 32)


def backward_one(lane, places, grad, kept, kernels, mixers, unit, own):
    reach = kept[0][0].shape[1]
    e, p = kept[unit]
    rows = own if unit == 0 else own + 32
    length = grad.shape[1]
    send, keep, grad, total = lane.run(
        lambda g: backward_unit(
            places[length],
            g,
            p,
            e,
            kernels,
            mixers,
            unit,
            rows,
            (p.shape[1] - length) // 2,
            (reach - rows) // 2,
            own,
            RIMS[unit],
        ),
        grad,
    )
    return grad, (send, swap(send, 1), keep), total


def weights_one(lane, place, result, unit, own, clips, done):
    send, other, keep = result
    pieces = lane.run(
        lambda mine: weights_unit(place, mine, other, keep, unit, own, RIMS[unit], clips), send
    )
    lane.scatter(pieces, done)


def split_units(reduced, channels):
    block = channels // 8
    taps = [part.reshape(8, block, LANES) for part in reduced]
    return jnp.stack([part[:KSIZE] for part in taps]), jnp.stack([part[KSIZE] for part in taps])


def fast_device(
    incoming_samples,
    sample_extents,
    chosen_entries,
    encoder_dilated_kernels,
    encoder_dilated_biases,
    encoder_pointwise_tables,
    encoder_pointwise_offsets,
    reducing_filter,
    reducing_offset,
    quantizer_tables,
    widening_filter,
    widening_offset,
    decoder_dilated_filters,
    decoder_dilated_offsets,
    decoder_pointwise_tables,
    decoder_pointwise_offsets,
    result_cotangent,
):
    f32, bf16 = jnp.float32, jnp.bfloat16
    segment = lax.axis_index("tm")
    member = lax.axis_index("clip")
    clips, frames, channels = incoming_samples.shape
    latents = frames // HOP_FACTOR
    all_frames = frames * lax.axis_size("tm")
    first_frame = segment * frames
    group_width = channels // GROUPS

    def bounds(reach):
        return jnp.stack([reach - first_frame, all_frames - first_frame + reach])

    coordinates = jnp.stack(
        [member % 2, (member // 2) % 2, (member // 4) % 2, segment]
    ).astype(jnp.int32)

    def placed(reach):
        return jnp.concatenate([bounds(reach).astype(jnp.int32), coordinates])

    reach = LATENT_REACH * HOP_FACTOR
    grad_reach = GRAD_REACH * HOP_FACTOR
    where = bounds(reach).astype(jnp.int32)
    places = {frames + 2 * r: placed(r) for r in (grad_reach, 16)}
    place = places[frames + 32]

    lane = Lane()
    codes = with_neighbours(chosen_entries, LATENT_REACH)
    cotangent, samples = with_both(result_cotangent, grad_reach, incoming_samples, reach)

    code_range = jnp.arange(quantizer_tables.shape[2], dtype=jnp.int32)
    picked = [
        [
            jnp.einsum(
                "cnk,kd->cnd",
                (codes[:, :, g * LEVELS + l][..., None] == code_range).astype(bf16),
                quantizer_tables[g, l],
                preferred_element_type=f32,
            )
            for l in range(LEVELS)
        ]
        for g in range(GROUPS)
    ]
    quantized_wide = jnp.concatenate([sum(rows) for rows in picked], axis=2).astype(bf16)
    mid = slice(LATENT_REACH, LATENT_REACH + latents)
    quantized = quantized_wide[:, mid]
    widened = jnp.einsum("cnd,de->cne", quantized_wide, widening_filter, preferred_element_type=f32)
    start = (
        widened.reshape(clips, frames + 2 * reach, channels) + widening_offset.astype(f32)
    ).astype(bf16)

    decoded, decoder_kept = forward_stack(
        lane,
        where,
        start,
        decoder_dilated_filters,
        decoder_dilated_offsets,
        decoder_pointwise_tables,
        decoder_pointwise_offsets,
        frames,
    )
    output = decoded[:, grad_reach : grad_reach + frames].astype(bf16)

    decoder_work, decoder_sums = [None] * UNITS, [None] * UNITS
    reduced = {}
    batches = {"a": [], "b": [], "c": [], "d": []}
    sizes = {"a": 3, "b": 2, "c": 2, "d": 1}
    order = {"a": [], "b": [], "c": [], "d": []}

    def into(batch, name):
        def done(blocks):
            batches[batch].append(blocks)
            order[batch].append(name)
            if len(batches[batch]) == sizes[batch]:
                reduced[batch] = []
                lane.segments(batches[batch], reduced[batch])

        return done

    def decoder_backward(unit, grad):
        grad, decoder_work[unit], decoder_sums[unit] = backward_one(
            lane,
            places,
            grad,
            decoder_kept,
            decoder_dilated_filters,
            decoder_pointwise_tables,
            unit,
            frames,
        )
        return grad

    def decoder_weights(unit, batch):
        weights_one(
            lane, place, decoder_work[unit], unit, frames, clips, into(batch, ("d", unit))
        )

    grad_start = decoder_backward(1, decoder_backward(2, cotangent))
    decoder_weights(2, "a")
    grad_start = decoder_backward(0, grad_start)
    decoder_weights(1, "a")

    widened_grad = grad_start.astype(bf16)
    spreading = jnp.sum(widened_grad.astype(f32), axis=(0, 1))
    folded = widened_grad.reshape(clips * latents, HOP_FACTOR * channels)
    up_send = jnp.concatenate([quantized.reshape(clips * latents, channels), folded], axis=1)
    up_other = swap(up_send, 1)
    latent_grad = lax.dot_general(
        folded, widening_filter, NT, preferred_element_type=f32
    ).reshape(clips, latents, channels)

    def up_weights():
        pieces = lane.run(lambda mine: up_gradient(place, mine, up_other, channels), up_send)
        lane.scatter(pieces, into("a", "up"))

    encoded, encoder_kept = forward_stack(
        lane,
        where,
        samples,
        encoder_dilated_kernels,
        encoder_dilated_biases,
        encoder_pointwise_tables,
        encoder_pointwise_offsets,
        frames,
        {0: up_weights},
    )
    pooled_wide = elu(encoded).astype(bf16)
    pooled = pooled_wide[:, grad_reach : grad_reach + frames].reshape(
        clips * latents, HOP_FACTOR * channels
    )
    latent = (
        jnp.dot(pooled, reducing_filter, preferred_element_type=f32) + reducing_offset.astype(f32)
    ).reshape(clips, latents, channels)
    validity = (
        (first_frame + HOP_FACTOR * jnp.arange(latents, dtype=jnp.int32))[None, :]
        < sample_extents[:, None]
    ).astype(f32)
    masked = validity[..., None]
    loss_local = jnp.float32(0.0)
    commits, book_rows = [], []
    for g in range(GROUPS):
        residue = latent[:, :, g * group_width : (g + 1) * group_width]
        commit_sum = jnp.zeros_like(residue)
        for l in range(LEVELS):
            residue = residue - picked[g][l][:, mid]
            loss_local = loss_local + jnp.sum(masked * residue * residue)
            commit_sum = commit_sum + residue
            gap = (-2.0 * masked * residue).astype(bf16)
            gap = gap.reshape(clips * latents, 4, 1, group_width // 4)
            book_rows.append(
                jnp.broadcast_to(gap, (clips * latents, 4, 2, group_width // 4)).reshape(
                    clips * latents, 2 * group_width
                )
            )
        commits.append(2.0 * commit_weight * masked * commit_sum)
    glatent = (latent_grad + jnp.concatenate(commits, axis=2)).astype(bf16)
    pooling = jnp.sum(glatent.astype(f32), axis=(0, 1))
    glatent_wide = with_neighbours(glatent, GRAD_REACH)
    down_send = jnp.concatenate(
        [pooled, glatent.reshape(clips * latents, channels)] + book_rows, axis=1
    )
    own_codes = chosen_entries.reshape(clips * latents, GROUPS * LEVELS).T
    pair_codes = jnp.concatenate([own_codes, swap(own_codes, 1)], axis=1)
    down_other = swap(down_send, 1)
    decoder_weights(0, "b")

    pooled_grad = lax.dot_general(
        glatent_wide.reshape(-1, channels), reducing_filter, NT, preferred_element_type=f32
    ).reshape(clips, frames + 2 * grad_reach, channels) * slope_from_elu(pooled_wide.astype(f32))
    encoder_work, encoder_sums = [None] * UNITS, [None] * UNITS

    def encoder_backward(unit, grad):
        grad, encoder_work[unit], encoder_sums[unit] = backward_one(
            lane,
            places,
            grad,
            encoder_kept,
            encoder_dilated_kernels,
            encoder_pointwise_tables,
            unit,
            frames,
        )
        return grad

    def encoder_weights(unit, batch):
        weights_one(
            lane, place, encoder_work[unit], unit, frames, clips, into(batch, ("e", unit))
        )

    grad_samples = encoder_backward(2, pooled_grad)
    pieces = lane.run(
        lambda mine: down_gradient(place, pair_codes, mine, down_other, channels), down_send
    )
    lane.scatter(pieces, into("b", "down"))
    grad_samples = encoder_backward(1, grad_samples)
    encoder_weights(2, "c")
    grad_samples = encoder_backward(0, grad_samples)
    encoder_weights(1, "c")
    encoder_weights(0, "d")
    lane.finish()
    input_grad = grad_samples.astype(bf16)
    result = {}
    for batch in order:
        for name, part in zip(order[batch], reduced[batch]):
            result[name] = part

    count_local = jnp.sum((sample_extents + HOP_FACTOR - 1) // HOP_FACTOR).astype(f32)
    scalars = jnp.zeros((2, channels), f32).at[0, 0].set(loss_local).at[0, 1].set(count_local)
    small = jnp.concatenate(
        [t[:2] for t in encoder_sums]
        + [t[:2] for t in decoder_sums]
        + [pooling[None], spreading[None], scalars],
        axis=0,
    )
    for bit in (1, 2, 4):
        small = small + swap(small, bit)
    for bit in (1, 2):
        pairs = [(i, i ^ bit) for i in range(lax.axis_size("tm"))]
        small = small + lax.ppermute(small, "tm", pairs)
    loss_sum = (1.0 + commit_weight) * small[14, 0]
    total_count = small[14, 1] / lax.axis_size("tm")
    masked_loss = loss_sum / (total_count * channels)

    analysis, mixers = split_units([result["e", unit] for unit in range(UNITS)], channels)
    synthesis, remixers = split_units([result["d", unit] for unit in range(UNITS)], channels)
    block = channels // 8
    up_rows = result["up"].reshape(8, block, LANES)
    upsample = up_rows.transpose(1, 0, 2).reshape(block, 8 * LANES)
    halves = result["down"].reshape(2, channels // 2 + 128, LANES)
    downsample = halves[:, : channels // 2].reshape(8 * block, LANES)
    codebooks = (
        halves[:, channels // 2 :]
        .reshape(GROUPS, LEVELS, 64, 2, 64)
        .transpose(0, 1, 3, 2, 4)
        .reshape(GROUPS, LEVELS, 128, 64)
    )
    return (
        output,
        quantized,
        masked_loss,
        input_grad,
        analysis,
        small[0:6:2],
        mixers,
        small[1:6:2],
        downsample,
        small[12],
        codebooks,
        upsample,
        small[13],
        synthesis,
        small[6:12:2],
        remixers,
        small[7:12:2],
    )


def solution(mesh):
    placed = (
        P("clip", "tm", None),
        P("clip"),
        P("clip", "tm", None),
        P(),
        P(),
        P(),
        P(),
        P(),
        P(),
        P(),
        P(),
        P(),
        P(),
        P(),
        P(),
        P(),
        P("clip", "tm", None),
    )
    matched = mesh.shape["clip"] == 8 and mesh.shape["tm"] == 4
    return jax.shard_map(
        fast_device if matched else on_device,
        mesh=mesh,
        in_specs=placed,
        out_specs=(
            P("clip", "tm", None),
            P("clip", "tm", None),
            P(),
            P("clip", "tm", None),
            P(None, None, "clip", "tm"),
            P(),
            P(None, "clip", "tm"),
            P(),
            P("clip", "tm"),
            P(),
            P(None, None, "clip", "tm"),
            P("clip", "tm"),
            P(),
            P(None, None, "clip", "tm"),
            P(),
            P(None, "clip", "tm"),
            P(),
        ),
        check_vma=False,
    )
```

```python
import functools

import jax
import jax.numpy as jnp
from jax import lax
from jax.experimental import pallas as pl
from jax.experimental.pallas import tpu as pltpu
from jax.sharding import PartitionSpec as P

GROUPS = 2
LEVELS = 2
KSIZE = 7
UNITS = 3
HOP_FACTOR = 8


commit_weight = 0.25


def from_behind(block, axis, distance):
    devices = range(lax.axis_size(axis))
    route = [(i - distance, i) for i in devices if i - distance in devices]
    return lax.ppermute(block, axis, route)


def padded(cells, sides, width):
    for axis, dim in sides:
        count = lax.axis_size(axis)
        ends = count - 1
        head = lax.slice_in_dim(cells, 0, width, axis=dim)
        tail = lax.slice_in_dim(cells, cells.shape[dim] - width, cells.shape[dim], axis=dim)
        cells = jnp.concatenate(
            [
                lax.ppermute(tail, axis, [(i, (i + 1) % count) for i in range(ends)]),
                cells,
                lax.ppermute(head, axis, [((i + 1) % count, i) for i in range(ends)]),
            ],
            axis=dim,
        )
    return cells


def elu_slope(values):
    return jnp.where(values > 0, 1.0, jnp.exp(jnp.minimum(values, 0.0)))


def gather_taps(source, dilation, frames):
    return jnp.concatenate(
        [
            source[:, tap_index * dilation : tap_index * dilation + frames]
            for tap_index in range(KSIZE)
        ],
        axis=2,
    )


def dilated(source, kernel, dilation):
    frames = source.shape[1] - (KSIZE - 1) * dilation
    stacked = gather_taps(source, dilation, frames)
    flattened = kernel.reshape(KSIZE * kernel.shape[1], kernel.shape[2])
    return jnp.einsum("cti,io->cto", stacked, flattened, preferred_element_type=jnp.float32)


def dilated_back(source, kernel, dilation, grad_out):
    frames = grad_out.shape[1]
    stacked = gather_taps(source, dilation, frames)
    flattened = kernel.reshape(KSIZE * kernel.shape[1], kernel.shape[2])
    kernel_grad = jnp.einsum(
        "cti,cto->io", stacked, grad_out, preferred_element_type=jnp.float32
    ).reshape(kernel.shape)
    spread = jnp.einsum("cto,io->cti", grad_out, flattened, preferred_element_type=jnp.float32)
    channels = kernel.shape[1]
    source_grad = jnp.zeros(source.shape, jnp.float32)
    for tap_index in range(KSIZE):
        source_grad = source_grad.at[:, tap_index * dilation : tap_index * dilation + frames].add(
            spread[:, :, tap_index * channels : (tap_index + 1) * channels]
        )
    return (kernel_grad, source_grad)


def return_rims(grad_full, margin_width):
    length = grad_full.shape[1]
    owned = grad_full[:, margin_width : length - margin_width]
    from_above = from_behind(grad_full[:, :margin_width].astype(jnp.bfloat16), "tm", -1).astype(
        jnp.float32
    )
    from_below = from_behind(
        grad_full[:, length - margin_width :].astype(jnp.bfloat16), "tm", 1
    ).astype(jnp.float32)
    owned = owned.at[:, owned.shape[1] - margin_width :].add(from_above)
    return owned.at[:, :margin_width].add(from_below)


def unit_source(stream, margin_width):
    activated = jax.nn.elu(stream)
    return padded(activated.astype(jnp.bfloat16), (("tm", 1),), margin_width)


def source_back(source_grad, margin_width):
    return return_rims(source_grad, margin_width)


def stack_forward(
    stream,
    kernels,
    encoder_dilated_biases,
    encoder_pointwise_tables,
    encoder_pointwise_offsets,
    first_frame,
    frames,
):
    kept_list = []
    for unit_index in range(UNITS):
        dilation = 3**unit_index
        margin_width = KSIZE // 2 * dilation
        extra_frames = (stream.shape[1] - frames) // 2
        positions = first_frame - extra_frames + jnp.arange(stream.shape[1], dtype=jnp.int32)
        source = unit_source(stream, margin_width)
        before = dilated(source, kernels[unit_index], dilation) + encoder_dilated_biases[
            unit_index
        ].astype(jnp.float32)
        pointed = jax.nn.elu(before).astype(jnp.bfloat16)
        branch = jnp.einsum(
            "ctd,de->cte",
            pointed,
            encoder_pointwise_tables[unit_index],
            preferred_element_type=jnp.float32,
        )
        branch = branch + encoder_pointwise_offsets[unit_index].astype(jnp.float32)
        kept_list.append((stream, source, before, pointed, positions))
        stream = stream + branch
    return (stream, kept_list)


def stack_backward(grad_stream, kept_list, kernels, encoder_pointwise_tables):
    kernel_grads, offset_grads, mixer_grads, shift_grads = ([], [], [], [])
    for unit_index in reversed(range(UNITS)):
        stream, source, before, pointed, positions = kept_list[unit_index]
        dilation = 3**unit_index
        margin_width = KSIZE // 2 * dilation
        branch_grad = grad_stream.astype(jnp.bfloat16)
        mixer_grads.insert(
            0, jnp.einsum("ctd,cte->de", pointed, branch_grad, preferred_element_type=jnp.float32)
        )
        shift_grads.insert(0, jnp.sum(branch_grad.astype(jnp.float32), axis=(0, 1)))
        pointed_grad = jnp.einsum(
            "cte,de->ctd",
            branch_grad,
            encoder_pointwise_tables[unit_index],
            preferred_element_type=jnp.float32,
        )
        before_grad = (pointed_grad * elu_slope(before)).astype(jnp.bfloat16)
        offset_grads.insert(0, jnp.sum(before_grad.astype(jnp.float32), axis=(0, 1)))
        kernel_grad, source_grad = dilated_back(source, kernels[unit_index], dilation, before_grad)
        kernel_grads.insert(0, kernel_grad)
        owned_grad = source_back(source_grad, margin_width)
        grad_stream = grad_stream + owned_grad * elu_slope(stream)
    return (
        grad_stream,
        (
            jnp.stack(kernel_grads),
            jnp.stack(offset_grads),
            jnp.stack(mixer_grads),
            jnp.stack(shift_grads),
        ),
    )


def over_clips(matrices):
    return (
        lax.psum_scatter(
            matrices[0].astype(jnp.bfloat16), "clip", scatter_dimension=2, tiled=True
        ).astype(jnp.float32),
        lax.psum_scatter(
            matrices[1].astype(jnp.bfloat16), "clip", scatter_dimension=1, tiled=True
        ).astype(jnp.float32),
        lax.psum_scatter(
            matrices[2].astype(jnp.bfloat16), "clip", scatter_dimension=0, tiled=True
        ).astype(jnp.float32),
        lax.psum_scatter(
            matrices[3].astype(jnp.bfloat16), "clip", scatter_dimension=2, tiled=True
        ).astype(jnp.float32),
        lax.psum_scatter(
            matrices[4].astype(jnp.bfloat16), "clip", scatter_dimension=0, tiled=True
        ).astype(jnp.float32),
        lax.psum_scatter(
            matrices[5].astype(jnp.bfloat16), "clip", scatter_dimension=2, tiled=True
        ).astype(jnp.float32),
        lax.psum_scatter(
            matrices[6].astype(jnp.bfloat16), "clip", scatter_dimension=1, tiled=True
        ).astype(jnp.float32),
    )


def over_segments(matrices):
    return (
        lax.psum_scatter(
            matrices[0].astype(jnp.bfloat16), "tm", scatter_dimension=3, tiled=True
        ).astype(jnp.float32),
        lax.psum_scatter(
            matrices[1].astype(jnp.bfloat16), "tm", scatter_dimension=2, tiled=True
        ).astype(jnp.float32),
        lax.psum_scatter(
            matrices[2].astype(jnp.bfloat16), "tm", scatter_dimension=1, tiled=True
        ).astype(jnp.float32),
        lax.psum_scatter(
            matrices[3].astype(jnp.bfloat16), "tm", scatter_dimension=3, tiled=True
        ).astype(jnp.float32),
        lax.psum_scatter(
            matrices[4].astype(jnp.bfloat16), "tm", scatter_dimension=1, tiled=True
        ).astype(jnp.float32),
        lax.psum_scatter(
            matrices[5].astype(jnp.bfloat16), "tm", scatter_dimension=3, tiled=True
        ).astype(jnp.float32),
        lax.psum_scatter(
            matrices[6].astype(jnp.bfloat16), "tm", scatter_dimension=2, tiled=True
        ).astype(jnp.float32),
    )


def on_device(
    incoming_samples,
    sample_extents,
    chosen_entries,
    encoder_dilated_kernels,
    encoder_dilated_biases,
    encoder_pointwise_tables,
    encoder_pointwise_offsets,
    reducing_filter,
    reducing_offset,
    quantizer_tables,
    widening_filter,
    widening_offset,
    decoder_dilated_filters,
    decoder_dilated_offsets,
    decoder_pointwise_tables,
    decoder_pointwise_offsets,
    result_cotangent,
):
    segment = lax.axis_index("tm")
    clips = incoming_samples.shape[0]
    frames = incoming_samples.shape[1]
    channels = incoming_samples.shape[2]
    first_frame = segment * frames
    latents = frames // HOP_FACTOR
    total_count = lax.psum(
        jnp.sum((sample_extents + HOP_FACTOR - 1) // HOP_FACTOR).astype(jnp.float32), "clip"
    )
    stream = incoming_samples.astype(jnp.float32)
    encoded, encoder_kept = stack_forward(
        stream,
        encoder_dilated_kernels,
        encoder_dilated_biases,
        encoder_pointwise_tables,
        encoder_pointwise_offsets,
        first_frame,
        frames,
    )
    reduced_samples = (
        jax.nn.elu(encoded).astype(jnp.bfloat16).reshape(clips, latents, HOP_FACTOR * channels)
    )
    latent = jnp.einsum(
        "kde,er->kdr", reduced_samples, reducing_filter, preferred_element_type=jnp.float32
    ) + reducing_offset.astype(jnp.float32)
    validity = (
        (first_frame + HOP_FACTOR * jnp.arange(latents, dtype=jnp.int32))[None, :]
        < sample_extents[:, None]
    ).astype(jnp.float32)
    masked = validity[..., None]
    group_width = channels // GROUPS
    code_range = jnp.arange(quantizer_tables.shape[2], dtype=jnp.int32)
    loss_local = jnp.float32(0.0)
    quant_parts, commit_parts, book_rows = ([], [], [])
    for group_index in range(GROUPS):
        residue = latent[:, :, group_index * group_width : (group_index + 1) * group_width]
        commit_sum = jnp.zeros_like(residue)
        group_code = jnp.zeros_like(residue)
        level_rows = []
        for level_index in range(LEVELS):
            column = group_index * LEVELS + level_index
            onehot = (chosen_entries[:, :, column][..., None] == code_range).astype(jnp.bfloat16)
            picked = jnp.einsum(
                "kde,er->kdr",
                onehot,
                quantizer_tables[group_index, level_index],
                preferred_element_type=jnp.float32,
            )
            residue = residue - picked
            level_rows.append(
                jnp.einsum(
                    "cnk,cnd->kd",
                    onehot.astype(jnp.float32),
                    -2.0 * masked * residue,
                    precision=lax.Precision.HIGHEST,
                    preferred_element_type=jnp.float32,
                )
            )
            commit_sum = commit_sum + residue
            loss_local = loss_local + jnp.sum(masked * residue * residue)
            group_code = group_code + picked
        book_rows.append(jnp.stack(level_rows))
        commit_parts.append(2.0 * commit_weight * masked * commit_sum)
        quant_parts.append(group_code)
    loss_local = (1.0 + commit_weight) * loss_local
    quantized = jnp.concatenate(quant_parts, axis=2).astype(jnp.bfloat16)
    loss_sum = lax.psum(loss_local, ("clip", "tm"))
    masked_loss = loss_sum / (total_count * channels)
    widened = jnp.einsum(
        "cnd,de->cne", quantized, widening_filter, preferred_element_type=jnp.float32
    )
    decoder_start = (
        widened.reshape(clips, frames, channels) + widening_offset.astype(jnp.float32)
    ).astype(jnp.bfloat16)
    stream = decoder_start.astype(jnp.float32)
    decoded, decoder_kept = stack_forward(
        stream,
        decoder_dilated_filters,
        decoder_dilated_offsets,
        decoder_pointwise_tables,
        decoder_pointwise_offsets,
        first_frame,
        frames,
    )
    output = decoded.astype(jnp.bfloat16)
    grad_decoder, decoder_grads = stack_backward(
        result_cotangent.astype(jnp.float32),
        decoder_kept,
        decoder_dilated_filters,
        decoder_pointwise_tables,
    )
    widened_grad = grad_decoder.astype(jnp.bfloat16)
    spreading_grad = jnp.sum(widened_grad.astype(jnp.float32), axis=(0, 1))
    folded_grad = widened_grad.reshape(clips, latents, HOP_FACTOR * channels)
    upsample_grad = jnp.einsum(
        "cnd,cne->de", quantized, folded_grad, preferred_element_type=jnp.float32
    )
    latent_grad = jnp.einsum(
        "cne,de->cnd", folded_grad, widening_filter, preferred_element_type=jnp.float32
    )
    hidden_first_half = (latent_grad + jnp.concatenate(commit_parts, axis=2)).astype(jnp.bfloat16)
    pooling_grad = jnp.sum(hidden_first_half.astype(jnp.float32), axis=(0, 1))
    downsampling_gradient = jnp.einsum(
        "cnk,cnd->kd", reduced_samples, hidden_first_half, preferred_element_type=jnp.float32
    )
    pooled_grad = jnp.einsum(
        "npk,xk->npx", hidden_first_half, reducing_filter, preferred_element_type=jnp.float32
    )
    pooled_grad = pooled_grad.reshape(clips, frames, channels) * elu_slope(encoded)
    grad_encoder, encoder_grads = stack_backward(
        pooled_grad, encoder_kept, encoder_dilated_kernels, encoder_pointwise_tables
    )
    input_grad = grad_encoder.astype(jnp.bfloat16)
    codebook_grad = jnp.stack(book_rows)
    matrices = (
        encoder_grads[0],
        encoder_grads[2],
        downsampling_gradient,
        codebook_grad,
        upsample_grad,
        decoder_grads[0],
        decoder_grads[2],
    )
    matrices = over_segments(over_clips(matrices))
    biases = lax.psum(
        (
            encoder_grads[1],
            encoder_grads[3],
            pooling_grad,
            spreading_grad,
            decoder_grads[1],
            decoder_grads[3],
        ),
        ("clip", "tm"),
    )
    return (
        output,
        quantized,
        masked_loss,
        input_grad,
        matrices[0],
        biases[0],
        matrices[1],
        biases[1],
        matrices[2],
        biases[2],
        matrices[3],
        matrices[4],
        biases[3],
        matrices[5],
        biases[4],
        matrices[6],
        biases[5],
    )

PAD = 32
RIM = 32
STRIP = 16
CHUNKS = 2
HALO = 16
LANES = 128
LATENT_REACH = 10
GRAD_REACH = 6
NT = (((1,), (1,)), ((), ()))
VMEM_BYTES = 60 * 1024 * 1024


def elu(values):
    return jnp.where(values > 0, values, jnp.exp(jnp.minimum(values, 0.0)) - 1.0)


def slope_from_elu(activated):
    return jnp.where(activated > 0, 1.0, activated + 1.0)


def whole(array):
    return pl.BlockSpec(array.shape, lambda *i: (0,) * len(array.shape))


def smem():
    return pl.BlockSpec(memory_space=pltpu.SMEM)


def compiler_params(axes=1):
    return pltpu.CompilerParams(
        vmem_limit_bytes=VMEM_BYTES, dimension_semantics=("arbitrary",) * axes
    )


def spread(block, lines, first, reach, step):
    own = block.shape[0] - 2 * HALO
    for tile in range(lines.shape[0]):
        lanes = slice(tile * LANES, (tile + 1) * LANES)
        for start, count, row in (
            (0, own, first + reach),
            (own, reach, first),
            (own + HALO, reach, first + reach + own),
        ):
            lines[tile, pl.ds(HOP_FACTOR * row + step, count, HOP_FACTOR), :] = block[
                start : start + count, lanes
            ]


def start_kernel(codes_ref, tables_ref, filter_ref, offset_ref, q_ref, start_ref, picked_ref, lines):
    clips, count = codes_ref.shape[:2]
    own = count - 2 * HALO
    channels = start_ref.shape[2]
    entries = tables_ref.shape[2]
    entry = lax.broadcasted_iota(jnp.int32, (count, entries), 1)
    offset = offset_ref[...].astype(jnp.float32)
    for clip in range(clips):
        groups = []
        for group in range(GROUPS):
            total = None
            for level in range(LEVELS):
                column = group * LEVELS + level
                onehot = jnp.where(codes_ref[clip, :, column : column + 1] == entry, 1.0, 0.0)
                rows = jnp.dot(
                    onehot.astype(jnp.bfloat16),
                    tables_ref[group, level],
                    preferred_element_type=jnp.float32,
                )
                picked_ref[column, clip] = rows[:own]
                total = rows if total is None else total + rows
            groups.append(total)
        quantized = jnp.concatenate(groups, axis=1).astype(jnp.bfloat16)
        q_ref[clip] = quantized[:own]
        for step in range(HOP_FACTOR):
            block = jnp.dot(
                quantized,
                filter_ref[:, step * channels : (step + 1) * channels],
                preferred_element_type=jnp.float32,
            )
            spread(block + offset, lines, 0, LATENT_REACH, step)
        for tile in range(channels // LANES):
            start_ref[clip, :, tile * LANES : (tile + 1) * LANES] = lines[tile].astype(
                jnp.bfloat16
            )


def start_frames(codes, tables, widening, offset):
    clips, count, _ = codes.shape
    own = count - 2 * HALO
    channels = widening.shape[0]
    frames = HOP_FACTOR * (own + 2 * LATENT_REACH)
    outs = (
        jax.ShapeDtypeStruct((clips, own, channels), jnp.bfloat16),
        jax.ShapeDtypeStruct((clips, frames, channels), jnp.bfloat16),
        jax.ShapeDtypeStruct((GROUPS * LEVELS, clips, own, channels // GROUPS), jnp.float32),
    )
    offset = offset.reshape(1, channels)
    return pl.pallas_call(
        start_kernel,
        grid=(1,),
        in_specs=[whole(codes), whole(tables), whole(widening), whole(offset)],
        out_specs=[whole(out) for out in outs],
        out_shape=outs,
        scratch_shapes=[pltpu.VMEM((channels // LANES, frames, LANES), jnp.float32)],
        compiler_params=compiler_params(),
        name="decoder_start",
    )(codes, tables, widening, offset)


def latent_kernel(
    extents, pooled_ref, filter_ref, offset_ref, picked_ref, grad_ref, g_ref, send_ref, sum_ref, lines
):
    clips, length, channels = pooled_ref.shape
    latents = g_ref.shape[1]
    own = HOP_FACTOR * latents
    first = (length - own) // 2
    width = channels // GROUPS
    tiles = channels // LANES
    long = HOP_FACTOR * channels
    for clip in range(clips):
        for tile in range(tiles):
            lines[tile] = pooled_ref[
                clip, first : first + own, tile * LANES : (tile + 1) * LANES
            ].astype(jnp.float32)
        rows = slice(clip * latents, (clip + 1) * latents)
        for step in range(HOP_FACTOR):
            for tile in range(tiles):
                column = step * channels + tile * LANES
                send_ref[rows, column : column + LANES] = lines[
                    tile, pl.ds(step, latents, HOP_FACTOR), :
                ].astype(jnp.bfloat16)
    latent = jnp.dot(
        send_ref[:, :long], filter_ref[...], preferred_element_type=jnp.float32
    ) + offset_ref[...].astype(jnp.float32)
    position = extents[0] + HOP_FACTOR * lax.broadcasted_iota(jnp.int32, (latents, width), 0)
    lane = lax.broadcasted_iota(jnp.int32, (latents, LANES), 1)
    pooling = jnp.zeros((1, channels), jnp.float32)
    losses = [jnp.zeros((1, width), jnp.float32) for _ in range(GROUPS)]
    for clip in range(clips):
        rows = slice(clip * latents, (clip + 1) * latents)
        masked = jnp.where(position < extents[1 + clip], 1.0, 0.0)
        for group in range(GROUPS):
            columns = slice(group * width, (group + 1) * width)
            residue = latent[rows, columns]
            commit = jnp.zeros_like(residue)
            for level in range(LEVELS):
                book = group * LEVELS + level
                residue = residue - picked_ref[book, clip]
                losses[group] = losses[group] + jnp.sum(
                    masked * residue * residue, axis=0, keepdims=True
                )
                commit = commit + residue
                gap = -2.0 * masked * residue
                for tile in range(width // LANES):
                    part = gap[:, tile * LANES : (tile + 1) * LANES]
                    turned = pltpu.roll(part, LANES // 2, 1)
                    to = long + channels + book * 2 * width + tile * 2 * LANES
                    send_ref[rows, to : to + LANES] = jnp.where(
                        lane < LANES // 2, part, turned
                    ).astype(jnp.bfloat16)
                    send_ref[rows, to + LANES : to + 2 * LANES] = jnp.where(
                        lane < LANES // 2, turned, part
                    ).astype(jnp.bfloat16)
            glatent = grad_ref[rows, columns] + 2.0 * commit_weight * masked * commit
            glatent = glatent.astype(jnp.bfloat16)
            g_ref[clip, :, columns] = glatent
            send_ref[rows, long + group * width : long + (group + 1) * width] = glatent
    for clip in range(clips):
        pooling = pooling + jnp.sum(g_ref[clip].astype(jnp.float32), axis=0, keepdims=True)
    sum_ref[0:1, :] = pooling
    sum_ref[1:2, :] = jnp.concatenate(losses, axis=1)
    count = 0
    for clip in range(clips):
        count = count + (extents[1 + clip] + HOP_FACTOR - 1) // HOP_FACTOR
    sum_ref[2:3, :] = jnp.full((1, channels), count, jnp.int32).astype(jnp.float32)


def latent_frames(extents, pooled, reducing, offset, picked, latent_grad, own):
    clips, _, channels = pooled.shape
    latents = own // HOP_FACTOR
    offset = offset.reshape(1, channels)
    outs = (
        jax.ShapeDtypeStruct((clips, latents, channels), jnp.bfloat16),
        jax.ShapeDtypeStruct((clips * latents, (HOP_FACTOR + 5) * channels), jnp.bfloat16),
        jax.ShapeDtypeStruct((8, channels), jnp.float32),
    )
    return pl.pallas_call(
        latent_kernel,
        grid=(1,),
        in_specs=[
            smem(),
            whole(pooled),
            whole(reducing),
            whole(offset),
            whole(picked),
            whole(latent_grad),
        ],
        out_specs=[whole(out) for out in outs],
        out_shape=outs,
        scratch_shapes=[pltpu.VMEM((channels // LANES, own, LANES), jnp.float32)],
        compiler_params=compiler_params(),
        name="latent_frames",
    )(extents, pooled, reducing, offset, picked, latent_grad)


def pooled_kernel(g_ref, filter_ref, pooled_ref, out_ref, lines):
    channels = out_ref.shape[2]
    for step in range(HOP_FACTOR):
        block = lax.dot_general(
            g_ref[0],
            filter_ref[step * channels : (step + 1) * channels, :],
            NT,
            preferred_element_type=jnp.float32,
        )
        spread(block, lines, 0, GRAD_REACH, step)
    for tile in range(channels // LANES):
        lanes = slice(tile * LANES, (tile + 1) * LANES)
        pooled = pooled_ref[0, :, lanes].astype(jnp.float32)
        out_ref[0, :, lanes] = lines[tile] * slope_from_elu(pooled)


def pooled_gradient(glatent, reducing, pooled):
    clips, length, channels = pooled.shape
    clip_spec = pl.BlockSpec((1, length, channels), lambda c: (c, 0, 0))
    return pl.pallas_call(
        pooled_kernel,
        grid=(clips,),
        in_specs=[
            pl.BlockSpec((1,) + glatent.shape[1:], lambda c: (c, 0, 0)),
            whole(reducing),
            clip_spec,
        ],
        out_specs=clip_spec,
        out_shape=jax.ShapeDtypeStruct(pooled.shape, jnp.float32),
        scratch_shapes=[pltpu.VMEM((channels // LANES, length, LANES), jnp.float32)],
        compiler_params=compiler_params(),
        name="pooled_gradient",
    )(glatent, reducing, pooled)


def dilation_of(unit):
    return jnp.where(unit == 0, 1, jnp.where(unit == 1, 3, 9)).astype(jnp.int32)


def row_of(unit, ref):
    rows = ref[...].astype(jnp.float32)
    return jnp.where(unit == 0, rows[0:1], jnp.where(unit == 1, rows[1:2], rows[2:3]))


def forward_kernel(
    out_first,
    activate,
    where_ref,
    h_ref,
    w_ref,
    b_ref,
    m_ref,
    s_ref,
    e_ref,
    p_ref,
    out_ref,
    stream,
    lines,
):
    clips, length, channels = h_ref.shape
    unit, clip = pl.program_id(0), pl.program_id(1)
    dilation = dilation_of(unit)
    low, high = where_ref[0], where_ref[1]
    tiles = channels // LANES
    rows = length // CHUNKS

    @pl.when(jnp.logical_and(unit == 0, clip == 0))
    def _():
        for tile in range(tiles):
            lines[tile, :PAD, :] = jnp.zeros((PAD, LANES), jnp.float32)
            lines[tile, PAD + length :, :] = jnp.zeros((PAD, LANES), jnp.float32)

    @pl.when(unit == 0)
    def _():
        stream[clip] = h_ref[clip].astype(jnp.float32)

    position = lax.broadcasted_iota(jnp.int32, (length, LANES), 0)
    inside = (position >= low) & (position < high)
    for tile in range(tiles):
        lanes = slice(tile * LANES, (tile + 1) * LANES)
        active = jnp.where(inside, elu(stream[clip, :, lanes]), 0.0).astype(jnp.bfloat16)
        e_ref[0, 0, :, lanes] = active
        lines[tile, PAD : PAD + length, :] = active.astype(jnp.float32)
    kernel = w_ref[0].reshape(KSIZE * channels, channels)
    mixer = m_ref[0]
    bias = row_of(unit, b_ref)
    shift = row_of(unit, s_ref)
    for chunk in range(CHUNKS):
        taps = []
        for tap in range(KSIZE):
            start = PAD + chunk * rows + (tap - KSIZE // 2) * dilation
            for tile in range(tiles):
                taps.append(lines[tile, pl.ds(start, rows), :].astype(jnp.bfloat16))
        before = jnp.dot(
            jnp.concatenate(taps, axis=1), kernel, preferred_element_type=jnp.float32
        )
        pointed = elu(before + bias).astype(jnp.bfloat16)
        span = slice(chunk * rows, (chunk + 1) * rows)
        p_ref[0, 0, span, :] = pointed
        branch = jnp.dot(pointed, mixer, preferred_element_type=jnp.float32) + shift
        stream[clip, span, :] = stream[clip, span, :] + branch

    @pl.when(unit == UNITS - 1)
    def _():
        final = stream[clip, out_first : out_first + out_ref.shape[1], :]
        out_ref[0] = (elu(final) if activate else final).astype(out_ref.dtype)


def forward_units(where, h, kernels, biases, mixers, shifts, out_rows, activate):
    clips, length, channels = h.shape
    kept = jax.ShapeDtypeStruct((UNITS, clips, length, channels), jnp.bfloat16)
    kept_spec = pl.BlockSpec((1, 1, length, channels), lambda u, c: (u, c, 0, 0))
    return pl.pallas_call(
        functools.partial(forward_kernel, (length - out_rows) // 2, activate),
        grid=(UNITS, clips),
        in_specs=[
            smem(),
            whole(h),
            pl.BlockSpec((1, KSIZE, channels, channels), lambda u, c: (u, 0, 0, 0)),
            whole(biases),
            pl.BlockSpec((1, channels, channels), lambda u, c: (u, 0, 0)),
            whole(shifts),
        ],
        out_specs=[
            kept_spec,
            kept_spec,
            pl.BlockSpec(
                (1, out_rows, channels), lambda u, c: (jnp.where(u == UNITS - 1, c, 0), 0, 0)
            ),
        ],
        out_shape=(
            kept,
            kept,
            jax.ShapeDtypeStruct((clips, out_rows, channels), jnp.bfloat16),
        ),
        scratch_shapes=[
            pltpu.VMEM((clips, length, channels), jnp.float32),
            pltpu.VMEM((channels // LANES, length + 2 * PAD, LANES), jnp.float32),
        ],
        compiler_params=compiler_params(2),
        name="units_forward",
    )(where, h, kernels, biases, mixers, shifts)


def backward_kernel(
    unit_first,
    units,
    own,
    final,
    data,
    place,
    gh_ref,
    p_ref,
    e_ref,
    m_ref,
    *rest,
):
    if data:
        w_ref, send_ref, keep_ref, sum_ref, out_ref, grad, lines, turned = rest
    else:
        send_ref, keep_ref, sum_ref, grad, turned = rest
    clips, length, channels = gh_ref.shape
    step, clip = pl.program_id(0), pl.program_id(1)
    dilation = dilation_of(unit_first - step)
    tiles = channels // LANES
    kept_length = p_ref.shape[2]
    kept_first = (kept_length - length) // 2
    own_first = (length - own) // 2
    wide = own + 2 * RIM
    rows = own + 2 * STRIP
    first = own_first - STRIP
    low, high, core = place[0], place[1], place[2]

    if data:

        @pl.when(jnp.logical_and(step == 0, clip == 0))
        def _():
            for tile in range(tiles):
                lines[tile, :PAD, :] = jnp.zeros((PAD, LANES), jnp.float32)
                lines[tile, PAD + length :, :] = jnp.zeros((PAD, LANES), jnp.float32)

    @pl.when(step == 0)
    def _():
        grad[clip] = gh_ref[clip].astype(jnp.float32)

    gc = grad[clip].astype(jnp.bfloat16)
    send_ref[0, 0, wide : wide + own, :] = gc[own_first : own_first + own]
    gp = lax.dot_general(gc, m_ref[0], NT, preferred_element_type=jnp.float32)
    pointed = p_ref[0, 0, kept_first : kept_first + length, :].astype(jnp.float32)
    position = lax.broadcasted_iota(jnp.int32, (length, channels), 0)
    inside = (position >= low) & (position < high)
    ga = jnp.where(inside, gp * slope_from_elu(pointed), 0.0).astype(jnp.bfloat16)
    send_ref[0, 0, :wide, :] = ga[own_first - RIM : own_first + own + RIM]
    ga = ga.astype(jnp.float32)
    a_sum = jnp.sum(ga[own_first : own_first + own], axis=0, keepdims=True)
    c_sum = jnp.sum(gc[own_first : own_first + own].astype(jnp.float32), axis=0, keepdims=True)
    o_sum = jnp.zeros_like(a_sum)
    if data:
        for tile in range(tiles):
            lines[tile, PAD : PAD + length, :] = ga[:, tile * LANES : (tile + 1) * LANES]
        kernel = jnp.concatenate([w_ref[0, tap] for tap in range(KSIZE)], axis=1)
        size = rows // CHUNKS
        for chunk in range(CHUNKS):
            begin = first + chunk * size
            moved = jnp.concatenate(
                [
                    lines[
                        tile, pl.ds(PAD + begin - (tap - KSIZE // 2) * dilation, size), :
                    ].astype(jnp.bfloat16)
                    for tap in range(KSIZE)
                    for tile in range(tiles)
                ],
                axis=1,
            )
            total = lax.dot_general(moved, kernel, NT, preferred_element_type=jnp.float32)
            active = e_ref[0, 0, kept_first + begin : kept_first + begin + size, :]
            grad[clip, begin : begin + size, :] = grad[
                clip, begin : begin + size, :
            ] + total * slope_from_elu(active.astype(jnp.float32))

        if final:
            own_grad = grad[clip, own_first : own_first + own, :].astype(jnp.bfloat16)
            o_sum = jnp.sum(own_grad.astype(jnp.float32), axis=0, keepdims=True)

            @pl.when(step == units - 1)
            def _():
                out_ref[0] = own_grad
        else:

            @pl.when(step == units - 1)
            def _():
                out_ref[0] = grad[clip]

    sums = jnp.concatenate([a_sum, c_sum, o_sum], axis=0)

    @pl.when(clip == 0)
    def _():
        sum_ref[0, :3, :] = sums

    @pl.when(clip > 0)
    def _():
        sum_ref[0, :3, :] = sum_ref[0, :3, :] + sums

    base = wide + own
    block = channels // 8
    start = (kept_length - own) // 2
    for which, ref in enumerate((e_ref, p_ref)):
        turned[...] = jnp.transpose(ref[0, 0, start : start + own, :])
        for rx in range(2):
            for ry in range(2):
                pair = jnp.bitwise_xor(place[4], ry) * 4 + jnp.bitwise_xor(place[3], rx) * 2
                to = which * (channels // 2) + (rx * 2 + ry) * block
                mine = pl.multiple_of((pair + core) * block, block)
                other = pl.multiple_of((pair + 1 - core) * block, block)
                keep_ref[0, 0, to : to + block, :] = turned[pl.ds(mine, block), :]
                send_ref[0, 0, base + to : base + to + block, :] = turned[pl.ds(other, block), :]


def backward_units(place, gh, p, e, kernels, mixers, unit_first, units, own, data=True):
    clips, length, channels = gh.shape
    kept_length = p.shape[2]
    payload = 2 * own + 2 * RIM + channels
    final = unit_first - units + 1 == 0
    kept_spec = pl.BlockSpec(
        (1, 1, kept_length, channels), lambda u, c: (unit_first - u, c, 0, 0)
    )
    out = (
        jax.ShapeDtypeStruct((clips, own, channels), jnp.bfloat16)
        if final
        else jax.ShapeDtypeStruct((clips, length, channels), jnp.float32)
    )
    tiles = channels // LANES
    operands = [place, gh, p, e, mixers]
    in_specs = [
        smem(),
        whole(gh),
        kept_spec,
        kept_spec,
        pl.BlockSpec((1, channels, channels), lambda u, c: (unit_first - u, 0, 0)),
    ]
    out_specs = [
        pl.BlockSpec((1, 1, payload, channels), lambda u, c: (u, c, 0, 0)),
        pl.BlockSpec((1, 1, channels, own), lambda u, c: (u, c, 0, 0)),
        pl.BlockSpec((1, 8, channels), lambda u, c: (u, 0, 0)),
    ]
    outs = [
        jax.ShapeDtypeStruct((units, clips, payload, channels), jnp.bfloat16),
        jax.ShapeDtypeStruct((units, clips, channels, own), jnp.bfloat16),
        jax.ShapeDtypeStruct((units, 8, channels), jnp.float32),
    ]
    scratch = [pltpu.VMEM((clips, length, channels), jnp.float32)]
    if data:
        operands.append(kernels)
        in_specs.append(
            pl.BlockSpec((1, KSIZE, channels, channels), lambda u, c: (unit_first - u, 0, 0, 0))
        )
        outs.append(out)
        out_specs.append(
            pl.BlockSpec(
                (1,) + out.shape[1:], lambda u, c: (jnp.where(u == units - 1, c, 0), 0, 0)
            )
        )
        scratch.append(pltpu.VMEM((tiles, length + 2 * PAD, LANES), jnp.float32))
    return pl.pallas_call(
        functools.partial(backward_kernel, unit_first, units, own, final, data),
        grid=(units, clips),
        in_specs=in_specs,
        out_specs=out_specs,
        out_shape=outs,
        scratch_shapes=scratch + [pltpu.VMEM((channels, own), jnp.bfloat16)],
        compiler_params=compiler_params(2),
        name="units_backward",
    )(*operands)


def stream_kernel(own, gh_ref, send_ref, e_ref, w_ref, out_ref, lines):
    length, channels = gh_ref.shape[1:]
    tiles = channels // LANES
    first = (length - own) // 2
    kept_first = (e_ref.shape[2] - own) // 2
    wide = own + 2 * RIM
    for tile in range(tiles):
        lanes = slice(tile * LANES, (tile + 1) * LANES)
        lines[tile] = send_ref[0, 0, :wide, lanes].astype(jnp.float32)
    kernel = jnp.concatenate([w_ref[0, tap] for tap in range(KSIZE)], axis=1)
    size = own // CHUNKS
    for chunk in range(CHUNKS):
        begin = chunk * size
        moved = jnp.concatenate(
            [
                lines[tile, start : start + size, :].astype(jnp.bfloat16)
                for start in (RIM + begin - tap + KSIZE // 2 for tap in range(KSIZE))
                for tile in range(tiles)
            ],
            axis=1,
        )
        total = lax.dot_general(moved, kernel, NT, preferred_element_type=jnp.float32)
        active = e_ref[0, 0, kept_first + begin : kept_first + begin + size, :]
        stream = gh_ref[0, first + begin : first + begin + size, :]
        out_ref[0, begin : begin + size, :] = (
            stream + total * slope_from_elu(active.astype(jnp.float32))
        ).astype(out_ref.dtype)


def stream_gradient(gh, send, e, kernels, own):
    clips, length, channels = gh.shape
    payload, kept_length = send.shape[2], e.shape[2]
    return pl.pallas_call(
        functools.partial(stream_kernel, own),
        grid=(clips,),
        in_specs=[
            pl.BlockSpec((1, length, channels), lambda c: (c, 0, 0)),
            pl.BlockSpec((1, 1, payload, channels), lambda c: (0, c, 0, 0)),
            pl.BlockSpec((1, 1, kept_length, channels), lambda c: (0, c, 0, 0)),
            pl.BlockSpec((1, KSIZE, channels, channels), lambda c: (0, 0, 0, 0)),
        ],
        out_specs=pl.BlockSpec((1, own, channels), lambda c: (c, 0, 0)),
        out_shape=jax.ShapeDtypeStruct((clips, own, channels), jnp.bfloat16),
        scratch_shapes=[
            pltpu.VMEM((channels // LANES, own + 2 * RIM, LANES), jnp.float32)
        ],
        compiler_params=compiler_params(),
        name="stream_gradient",
    )(gh, send, e, kernels)


def emit(result, start, tap_rows, first_axis, send_ref, keep_ref):
    result = result.astype(jnp.bfloat16)
    quarter = result.shape[0] // 4
    for rx in range(2):
        for ry in range(2):
            first, second = (rx, ry) if first_axis == 0 else (ry, rx)
            target = send_ref if first == 1 else keep_ref
            rows = slice((rx * 2 + ry) * quarter, (rx * 2 + ry + 1) * quarter)
            for segment in range(4):
                target[second, segment, pl.ds(start, tap_rows), :] = result[
                    rows, segment * LANES : (segment + 1) * LANES
                ]


def emit_outputs(rows):
    out = jax.ShapeDtypeStruct((2, 4, rows, LANES), jnp.bfloat16)
    return (out,) * 4


def weights_kernel(
    unit_first, units, own, with_up, place, mine_ref, other_ref, keep_ref, *rest
):
    if with_up:
        up_mine, up_other, filter_ref, sx, kx, sy, ky, latent_ref, lines, turned = rest
    else:
        sx, kx, sy, ky, lines = rest
    clips, channels = mine_ref.shape[1], mine_ref.shape[3]
    tiles = channels // LANES
    half = channels // 2
    block = channels // 8
    wide = own + 2 * RIM
    base = wide + own
    sources = (mine_ref, other_ref)
    step = pl.program_id(0)
    unit = unit_first - step // (KSIZE + 1)
    tap = lax.rem(step, KSIZE + 1)
    dilation = dilation_of(unit)
    normal = step < units * (KSIZE + 1)

    @pl.when(jnp.logical_and(normal, tap == 0))
    def _():
        for source in range(2):
            for clip in range(clips):
                for tile in range(tiles):
                    lines[source * clips + clip, tile, :, :] = sources[source][
                        0, clip, :wide, tile * LANES : (tile + 1) * LANES
                    ].astype(jnp.float32)

    def left(which):
        pieces = [
            keep_ref[0, clip, which * half : (which + 1) * half, :] for clip in range(clips)
        ] + [
            other_ref[0, clip, base + which * half : base + (which + 1) * half, :]
            for clip in range(clips)
        ]
        return jnp.concatenate(pieces, axis=1)

    def right():
        start = RIM - (tap - KSIZE // 2) * dilation
        return jnp.concatenate(
            [
                jnp.concatenate(
                    [
                        lines[item, tile, pl.ds(start, own), :].astype(jnp.bfloat16)
                        for tile in range(tiles)
                    ],
                    axis=1,
                )
                for item in range(2 * clips)
            ],
            axis=0,
        )

    half_taps = (KSIZE + 1) // 2

    @pl.when(jnp.logical_and(normal, tap < half_taps))
    def _():
        result = jnp.dot(left(0), right(), preferred_element_type=jnp.float32)
        emit(result, pl.multiple_of(tap * block, block), block, 0, sx, kx)

    @pl.when(jnp.logical_and(normal, jnp.logical_and(tap >= half_taps, tap < KSIZE)))
    def _():
        result = jnp.dot(left(0), right(), preferred_element_type=jnp.float32)
        start = pl.multiple_of((tap - half_taps) * block, block)
        emit(result, start, block, 1, sy, ky)

    @pl.when(jnp.logical_and(normal, tap == KSIZE))
    def _():
        grads = jnp.concatenate(
            [source[0, clip, wide:base, :] for source in sources for clip in range(clips)], axis=0
        )
        result = jnp.dot(left(1), grads, preferred_element_type=jnp.float32)
        emit(result, (half_taps - 1) * block, block, 1, sy, ky)

    if with_up:

        @pl.when(jnp.logical_not(normal))
        def _():
            up_kernel(place, up_mine, up_other, sx, kx, sy, ky, turned)
            latent_ref[...] = lax.dot_general(
                up_mine[:, channels:], filter_ref[...], NT, preferred_element_type=jnp.float32
            )


def weights_units(place, mine, other, keep, unit_first, own, up=None):
    units, clips, payload, channels = mine.shape
    steps = units * (KSIZE + 1)
    taps = KSIZE + 1
    rows = channels // 2
    groups = units + (0 if up is None else 1)
    out = jax.ShapeDtypeStruct((2, 4, groups * rows, LANES), jnp.bfloat16)
    out_spec = pl.BlockSpec((2, 4, rows, LANES), lambda i: (0, 0, i // taps, 0))

    def of_unit(array):
        return pl.BlockSpec(
            (1,) + array.shape[1:], lambda i: (jnp.minimum(i // taps, units - 1), 0, 0, 0)
        )

    scratch = [pltpu.VMEM((2 * clips, channels // LANES, own + 2 * RIM, LANES), jnp.float32)]
    more = ()
    out_specs, outs = [out_spec] * 4, (out,) * 4
    if up is not None:
        more = tuple(up)
        outs += (jax.ShapeDtypeStruct((up[0].shape[0], channels), jnp.float32),)
        out_specs.append(whole(outs[4]))
        scratch.append(pltpu.VMEM((channels, 2 * up[0].shape[0]), jnp.bfloat16))
    return pl.pallas_call(
        functools.partial(weights_kernel, unit_first, units, own, up is not None),
        grid=(steps + (0 if up is None else 1),),
        in_specs=[smem(), of_unit(mine), of_unit(other), of_unit(keep)]
        + [whole(array) for array in more],
        out_specs=out_specs,
        out_shape=outs,
        scratch_shapes=scratch,
        compiler_params=compiler_params(),
        name="units_weights",
    )(place, mine, other, keep, *more)


def relative_rows(place, ref, block, start, count):
    pieces = []
    for rx in range(2):
        for ry in range(2):
            pair = jnp.bitwise_xor(place[4], ry) * 4 + jnp.bitwise_xor(place[3], rx) * 2
            first = pl.multiple_of((pair + place[2]) * block + start, 16)
            pieces.append(ref[pl.ds(first, count), :])
    return jnp.concatenate(pieces, axis=0)


def up_kernel(place, mine_ref, other_ref, sx, kx, sy, ky, turned):
    latents = mine_ref.shape[0]
    channels = turned.shape[0]
    for source, ref in enumerate((mine_ref, other_ref)):
        turned[:, source * latents : (source + 1) * latents] = jnp.transpose(ref[:, :channels])
    left = relative_rows(place, turned, channels // 8, 0, channels // 8)
    for tap in range(8):
        right = jnp.concatenate(
            [
                jnp.concatenate(
                    [
                        ref[:, channels + (z * 8 + tap) * LANES : channels + (z * 8 + tap + 1) * LANES]
                        for z in range(4)
                    ],
                    axis=1,
                )
                for ref in (mine_ref, other_ref)
            ],
            axis=0,
        )
        result = jnp.dot(left, right, preferred_element_type=jnp.float32)
        if tap < 4:
            emit(result, tap * (channels // 8), channels // 8, 0, sx, kx)
        else:
            emit(result, (tap - 4) * (channels // 8), channels // 8, 1, sy, ky)


def down_kernel(place, codes_ref, mine_ref, other_ref, sx, kx, sy, ky, turned):
    latents = mine_ref.shape[0]
    long = turned.shape[0]
    channels = long // 8
    refs = (mine_ref, other_ref)
    for source, ref in enumerate(refs):
        turned[:, source * latents : (source + 1) * latents] = jnp.transpose(ref[:, :long])
    right = jnp.concatenate([ref[:, long : long + channels] for ref in refs], axis=0)
    block = channels // 8
    for tap in range(8):
        left = relative_rows(place, turned, channels, tap * block, block)
        result = jnp.dot(left, right, preferred_element_type=jnp.float32)
        if tap < 4:
            emit(result, tap * block, block, 0, sx, kx)
        else:
            emit(result, (tap - 4) * block, block, 1, sy, ky)
    lane = lax.broadcasted_iota(jnp.int32, (4 * 64, channels), 1)
    row = lax.broadcasted_iota(jnp.int32, (64, 2 * latents), 0)
    for book in range(4):
        gaps = jnp.concatenate(
            [
                ref[:, long + channels + book * channels : long + channels + (book + 1) * channels]
                for ref in refs
            ],
            axis=0,
        )
        codes = codes_ref[book : book + 1, :]
        parts = []
        for part in range(2):
            pieces = []
            for rx in range(2):
                for ry in range(2):
                    pair = jnp.bitwise_xor(place[4], ry) * 4 + jnp.bitwise_xor(place[3], rx) * 2
                    first = (pair + place[2]) * 128 + part * 64
                    pieces.append(jnp.where(codes == row + first, 1.0, 0.0).astype(jnp.bfloat16))
            parts.append(
                jnp.dot(
                    jnp.concatenate(pieces, axis=0), gaps, preferred_element_type=jnp.float32
                )
            )
        result = jnp.where(lax.rem(lane, LANES) < 64, parts[0], parts[1])
        if book < 2:
            emit(result, 4 * block + book * 64, 64, 0, sx, kx)
        else:
            emit(result, 4 * block + (book - 2) * 64, 64, 1, sy, ky)


def down_gradient(place, codes, mine, other, channels):
    outs = emit_outputs(channels // 2 + 128)
    return pl.pallas_call(
        down_kernel,
        grid=(1,),
        in_specs=[smem(), whole(codes), whole(mine), whole(other)],
        out_specs=[whole(out) for out in outs],
        out_shape=outs,
        scratch_shapes=[pltpu.VMEM((8 * channels, 2 * mine.shape[0]), jnp.bfloat16)],
        compiler_params=compiler_params(),
        name="downsample_weights",
    )(place, codes, mine, other)


def swap(block, bit):
    return lax.ppermute(block, "clip", [(i, i ^ bit) for i in range(lax.axis_size("clip"))])


def turn(block, distance):
    count = lax.axis_size("tm")
    return lax.ppermute(block, "tm", [(i, (i + distance) % count) for i in range(count)])


def added(*parts):
    total = parts[0].astype(jnp.float32)
    for part in parts[1:]:
        total = total + part.astype(jnp.float32)
    return total


def after(value, *others):
    return lax.optimization_barrier((value,) + others)[0]


class Lane:
    def __init__(self):
        self.clock = None
        self.ready = ()
        self.flights = []

    def fly(self, arrays, then, kernels=1):
        self.flights.append([kernels, arrays, then])

    def land(self, outs):
        arrived = [flight for flight in self.flights if flight[0] <= 1]
        self.flights = [[n - 1, arrays, then] for n, arrays, then in self.flights if n > 1]
        flat = [array for _, arrays, _ in arrived for array in arrays]
        held = lax.optimization_barrier(tuple(outs) + tuple(flat))
        outs, flat = held[: len(outs)], held[len(outs) :]
        self.clock = outs[0]
        self.ready = ()
        for _, arrays, then in arrived:
            then(*flat[: len(arrays)])
            flat = flat[len(arrays) :]
        return outs

    def run(self, kernel, first, *others):
        if self.clock is not None:
            first = after(first, self.clock, *self.ready)
        return self.land(kernel(first, *others))

    def scatter(self, pieces, done, kernels=(1, 1)):
        sx, kx, sy, ky = pieces

        def second(ax, ay):
            bx = added(kx[1], ax[1]).astype(jnp.bfloat16)
            by = added(ky[1], ay[1]).astype(jnp.bfloat16)
            self.ready += (bx, by)

            def third(cx, cy):
                blocks = jnp.concatenate(
                    [
                        added(kx[0], ax[0], cx).astype(jnp.bfloat16),
                        added(ky[0], ay[0], cy).astype(jnp.bfloat16),
                    ],
                    axis=1,
                )
                self.ready += (blocks,)
                done(blocks)

            self.fly((swap(bx, 4), swap(by, 2)), third, kernels[1])

        self.fly((swap(sx, 2), swap(sy, 4)), second, kernels[0])

    def segments(self, groups, done):
        blocks = jnp.concatenate(groups, axis=1) if len(groups) > 1 else groups[0]
        self.ready += (blocks,)
        total = lax.psum_scatter(blocks, "tm", scatter_dimension=0).astype(jnp.float32)
        start = 0
        for group in groups:
            done.append(total[start : start + group.shape[1]])
            start += group.shape[1]

    def everywhere(self, value, split, done):
        steps = [("tm", bit) for bit in (1, 2)] + [("clip", bit) for bit in (1, 2, 4)]

        def step(value, index):
            if index == len(steps):
                parts = split(value)
                self.ready += parts
                done.extend(parts)
                return
            axis, bit = steps[index]
            pairs = [(i, i ^ bit) for i in range(lax.axis_size(axis))]
            self.ready += (value,)
            self.fly(
                (lax.ppermute(value, axis, pairs),), lambda other: step(value + other, index + 1)
            )

        step(value, 0)

    def finish(self):
        while self.flights:
            tick = self.ready or (self.clock,)
            self.land(tick)


def neighbours(block, reach):
    ends = lax.axis_size("tm") - 1
    head = block[:, :reach]
    tail = block[:, block.shape[1] - reach :]
    return (
        lax.ppermute(tail, "tm", [(i, i + 1) for i in range(ends)]),
        lax.ppermute(head, "tm", [(i + 1, i) for i in range(ends)]),
    )


def latent_rows(block, below, above):
    widths = ((0, 0), (0, HALO - below.shape[1]), (0, 0))
    return jnp.concatenate([block, jnp.pad(below, widths), jnp.pad(above, widths)], axis=1)


def with_both(one, reach_one, two, reach_two):
    ends = lax.axis_size("tm") - 1
    tail = jnp.concatenate(
        [one[:, one.shape[1] - reach_one :], two[:, two.shape[1] - reach_two :]], axis=1
    )
    head = jnp.concatenate([one[:, :reach_one], two[:, :reach_two]], axis=1)
    below = lax.ppermute(tail, "tm", [(i, i + 1) for i in range(ends)])
    above = lax.ppermute(head, "tm", [(i + 1, i) for i in range(ends)])
    return (
        jnp.concatenate([below[:, :reach_one], one, above[:, :reach_one]], axis=1),
        jnp.concatenate([below[:, reach_one:], two, above[:, reach_one:]], axis=1),
    )


def split_units(reduced, channels):
    block = channels // 8
    taps = [part.reshape(8, block, LANES) for part in reduced]
    return jnp.stack([part[:KSIZE] for part in taps]), jnp.stack([part[KSIZE] for part in taps])


def fast_device(
    incoming_samples,
    sample_extents,
    chosen_entries,
    encoder_dilated_kernels,
    encoder_dilated_biases,
    encoder_pointwise_tables,
    encoder_pointwise_offsets,
    reducing_filter,
    reducing_offset,
    quantizer_tables,
    widening_filter,
    widening_offset,
    decoder_dilated_filters,
    decoder_dilated_offsets,
    decoder_pointwise_tables,
    decoder_pointwise_offsets,
    result_cotangent,
):
    f32, bf16 = jnp.float32, jnp.bfloat16
    segment = lax.axis_index("tm")
    member = lax.axis_index("clip")
    clips, frames, channels = incoming_samples.shape
    latents = frames // HOP_FACTOR
    all_frames = frames * lax.axis_size("tm")
    first_frame = segment * frames
    group_width = channels // GROUPS

    def bounds(reach):
        return jnp.stack([reach - first_frame, all_frames - first_frame + reach])

    coordinates = jnp.stack(
        [member % 2, (member // 2) % 2, (member // 4) % 2, segment]
    ).astype(jnp.int32)

    def placed(reach):
        return jnp.concatenate([bounds(reach).astype(jnp.int32), coordinates])

    reach = LATENT_REACH * HOP_FACTOR
    grad_reach = GRAD_REACH * HOP_FACTOR
    where = bounds(reach).astype(jnp.int32)
    place = placed(grad_reach)

    lane = Lane()
    codes = latent_rows(chosen_entries, *neighbours(chosen_entries, LATENT_REACH))
    cotangent, samples = with_both(result_cotangent, grad_reach, incoming_samples, reach)
    own_codes = chosen_entries.reshape(clips * latents, GROUPS * LEVELS).T
    pair_codes = []
    lane.fly(
        (swap(own_codes, 1),),
        lambda other: pair_codes.append(jnp.concatenate([own_codes, other], axis=1)),
        2,
    )

    quantized, start, picked = lane.run(
        lambda c: start_frames(c, quantizer_tables, widening_filter, widening_offset), codes
    )

    e_decoder, p_decoder, output = lane.run(
        lambda h: forward_units(
            where,
            h,
            decoder_dilated_filters,
            decoder_dilated_offsets,
            decoder_pointwise_tables,
            decoder_pointwise_offsets,
            frames,
            False,
        ),
        start,
    )

    reduced = {}
    sizes = {"a": 2, "b": 2, "c": 2}
    batches = {name: [] for name in sizes}
    order = {name: [] for name in sizes}

    def into(batch, name):
        def done(blocks):
            batches[batch].append(blocks)
            order[batch].append(name)
            if len(batches[batch]) == sizes[batch]:
                reduced[batch] = []
                lane.segments(batches[batch], reduced[batch])

        return done

    def backward(grad, p, e, kernels, tables, unit, units, data=True, kernels_between=1):
        send, keep, sums, *grad = lane.run(
            lambda g: backward_units(place, g, p, e, kernels, tables, unit, units, frames, data),
            grad,
        )
        grad = grad[0] if data else None
        work = [send, None, keep]

        def arrived(other):
            work[1] = other

        lane.fly((swap(send, 1),), arrived, kernels_between)
        return grad, work, sums

    def weights(work, unit, batch, name, up=None, kernels=(1, 1)):
        send, other, keep = work
        pieces = lane.run(
            lambda mine: weights_units(place, mine, other, keep, unit, frames, up), send
        )
        lane.scatter(pieces[:4], into(batch, name), kernels)
        return pieces[4:]

    decoder = (p_decoder, e_decoder, decoder_dilated_filters, decoder_pointwise_tables)
    grad_start, decoder_last, sums_last = backward(cotangent, *decoder, 2, 1)
    grad_start, decoder_rest, sums_rest = backward(grad_start, *decoder, 1, 2)

    widened_grad = grad_start
    folded = widened_grad.reshape(clips * latents, HOP_FACTOR * channels)
    up_send = jnp.concatenate([quantized.reshape(clips * latents, channels), folded], axis=1)
    up = (up_send, swap(up_send, 1), widening_filter)
    weights(decoder_last, 2, "a", "d2", None, (1, 2))
    (latent_grad,) = weights(decoder_rest, 1, "a", "d10up", up, (2, 2))

    e_encoder, p_encoder, pooled_wide = lane.run(
        lambda h: forward_units(
            where,
            h,
            encoder_dilated_kernels,
            encoder_dilated_biases,
            encoder_pointwise_tables,
            encoder_pointwise_offsets,
            frames + 2 * grad_reach,
            True,
        ),
        samples,
    )
    extents = jnp.concatenate([jnp.reshape(first_frame, (1,)), sample_extents]).astype(jnp.int32)
    glatent, down_send, latent_sums = lane.run(
        lambda p: latent_frames(
            extents, p, reducing_filter, reducing_offset, picked, latent_grad, frames
        ),
        pooled_wide,
    )
    glatent_wide = latent_rows(glatent, *neighbours(glatent, GRAD_REACH))
    down_other = []
    lane.fly((swap(down_send, 1),), down_other.append)
    (pooled_grad,) = lane.run(
        lambda g: (pooled_gradient(g, reducing_filter, pooled_wide),), glatent_wide
    )

    encoder = (p_encoder, e_encoder, encoder_dilated_kernels, encoder_pointwise_tables)
    grad, work_2, sums_2 = backward(pooled_grad, *encoder, 2, 1)
    pieces = lane.run(
        lambda mine: down_gradient(place, pair_codes[0], mine, down_other[0], channels), down_send
    )
    lane.scatter(pieces, into("b", "down"), (2, 1))
    grad, work_1, sums_1 = backward(grad, *encoder, 1, 1)
    weights(work_2, 2, "b", "e2")
    _, work_0, sums_0 = backward(grad, *encoder, 0, 1, False)
    small = jnp.concatenate(
        [
            sums.reshape(-1, channels)
            for sums in (sums_0, sums_1, sums_2, sums_rest, sums_last, latent_sums)
        ],
        axis=0,
    )
    summed = []

    def parts(small):
        rows = small.reshape(7, 8, channels)
        loss_sum = (1.0 + commit_weight) * jnp.sum(rows[6, 1])
        total_count = rows[6, 2, 0] / lax.axis_size("tm")
        decoder_rows = jnp.stack([rows[4], rows[3], rows[5]])
        return (
            loss_sum / (total_count * channels),
            rows[:3, 0],
            rows[:3, 1],
            rows[6, 0],
            rows[4, 2],
            decoder_rows[:, 0],
            decoder_rows[:, 1],
        )

    lane.everywhere(small, parts, summed)
    weights(work_1, 1, "c", "e1")
    weights(work_0, 0, "c", "e0")
    (input_grad,) = lane.run(
        lambda g: (stream_gradient(g, work_0[0], e_encoder, encoder_dilated_kernels, frames),),
        grad,
    )
    lane.finish()
    result = {}
    for batch in order:
        for name, part in zip(order[batch], reduced[batch]):
            result[name] = part

    block = channels // 8
    rest = result["d10up"].reshape(2, UNITS, channels // 2, LANES)
    decoder_parts = [rest[:, 1], rest[:, 0], result["d2"]]
    encoder_parts = [result["e0"], result["e1"], result["e2"]]
    analysis, mixers = split_units(encoder_parts, channels)
    synthesis, remixers = split_units(decoder_parts, channels)
    up_rows = rest[:, 2].reshape(8, block, LANES)
    upsample = up_rows.transpose(1, 0, 2).reshape(block, 8 * LANES)
    halves = result["down"].reshape(2, channels // 2 + 128, LANES)
    downsample = halves[:, : channels // 2].reshape(8 * block, LANES)
    codebooks = (
        halves[:, channels // 2 :]
        .reshape(GROUPS, LEVELS, 64, 2, 64)
        .transpose(0, 1, 3, 2, 4)
        .reshape(GROUPS, LEVELS, 128, 64)
    )
    masked_loss, offsets, shifts, pooling, spreading, biasing, tilting = summed
    return (
        output,
        quantized,
        masked_loss,
        input_grad,
        analysis,
        offsets,
        mixers,
        shifts,
        downsample,
        pooling,
        codebooks,
        upsample,
        spreading,
        synthesis,
        biasing,
        remixers,
        tilting,
    )


def solution(mesh):
    placed = (
        P("clip", "tm", None),
        P("clip"),
        P("clip", "tm", None),
        P(),
        P(),
        P(),
        P(),
        P(),
        P(),
        P(),
        P(),
        P(),
        P(),
        P(),
        P(),
        P(),
        P("clip", "tm", None),
    )
    matched = mesh.shape["clip"] == 8 and mesh.shape["tm"] == 4
    return jax.shard_map(
        fast_device if matched else on_device,
        mesh=mesh,
        in_specs=placed,
        out_specs=(
            P("clip", "tm", None),
            P("clip", "tm", None),
            P(),
            P("clip", "tm", None),
            P(None, None, "clip", "tm"),
            P(),
            P(None, "clip", "tm"),
            P(),
            P("clip", "tm"),
            P(),
            P(None, None, "clip", "tm"),
            P("clip", "tm"),
            P(),
            P(None, None, "clip", "tm"),
            P(),
            P(None, "clip", "tm"),
            P(),
        ),
        check_vma=False,
    )
```

```python
import functools

import jax
import jax.numpy as jnp
from jax import lax
from jax.experimental import pallas as pl
from jax.experimental.pallas import tpu as pltpu
from jax.sharding import PartitionSpec as P

GROUPS = 2
LEVELS = 2
KSIZE = 7
UNITS = 3
HOP_FACTOR = 8


commit_weight = 0.25


def from_behind(block, axis, distance):
    devices = range(lax.axis_size(axis))
    route = [(i - distance, i) for i in devices if i - distance in devices]
    return lax.ppermute(block, axis, route)


def padded(cells, sides, width):
    for axis, dim in sides:
        count = lax.axis_size(axis)
        ends = count - 1
        head = lax.slice_in_dim(cells, 0, width, axis=dim)
        tail = lax.slice_in_dim(cells, cells.shape[dim] - width, cells.shape[dim], axis=dim)
        cells = jnp.concatenate(
            [
                lax.ppermute(tail, axis, [(i, (i + 1) % count) for i in range(ends)]),
                cells,
                lax.ppermute(head, axis, [((i + 1) % count, i) for i in range(ends)]),
            ],
            axis=dim,
        )
    return cells


def elu_slope(values):
    return jnp.where(values > 0, 1.0, jnp.exp(jnp.minimum(values, 0.0)))


def gather_taps(source, dilation, frames):
    return jnp.concatenate(
        [
            source[:, tap_index * dilation : tap_index * dilation + frames]
            for tap_index in range(KSIZE)
        ],
        axis=2,
    )


def dilated(source, kernel, dilation):
    frames = source.shape[1] - (KSIZE - 1) * dilation
    stacked = gather_taps(source, dilation, frames)
    flattened = kernel.reshape(KSIZE * kernel.shape[1], kernel.shape[2])
    return jnp.einsum("cti,io->cto", stacked, flattened, preferred_element_type=jnp.float32)


def dilated_back(source, kernel, dilation, grad_out):
    frames = grad_out.shape[1]
    stacked = gather_taps(source, dilation, frames)
    flattened = kernel.reshape(KSIZE * kernel.shape[1], kernel.shape[2])
    kernel_grad = jnp.einsum(
        "cti,cto->io", stacked, grad_out, preferred_element_type=jnp.float32
    ).reshape(kernel.shape)
    spread = jnp.einsum("cto,io->cti", grad_out, flattened, preferred_element_type=jnp.float32)
    channels = kernel.shape[1]
    source_grad = jnp.zeros(source.shape, jnp.float32)
    for tap_index in range(KSIZE):
        source_grad = source_grad.at[:, tap_index * dilation : tap_index * dilation + frames].add(
            spread[:, :, tap_index * channels : (tap_index + 1) * channels]
        )
    return (kernel_grad, source_grad)


def return_rims(grad_full, margin_width):
    length = grad_full.shape[1]
    owned = grad_full[:, margin_width : length - margin_width]
    from_above = from_behind(grad_full[:, :margin_width].astype(jnp.bfloat16), "tm", -1).astype(
        jnp.float32
    )
    from_below = from_behind(
        grad_full[:, length - margin_width :].astype(jnp.bfloat16), "tm", 1
    ).astype(jnp.float32)
    owned = owned.at[:, owned.shape[1] - margin_width :].add(from_above)
    return owned.at[:, :margin_width].add(from_below)


def unit_source(stream, margin_width):
    activated = jax.nn.elu(stream)
    return padded(activated.astype(jnp.bfloat16), (("tm", 1),), margin_width)


def source_back(source_grad, margin_width):
    return return_rims(source_grad, margin_width)


def stack_forward(
    stream,
    kernels,
    encoder_dilated_biases,
    encoder_pointwise_tables,
    encoder_pointwise_offsets,
    first_frame,
    frames,
):
    kept_list = []
    for unit_index in range(UNITS):
        dilation = 3**unit_index
        margin_width = KSIZE // 2 * dilation
        extra_frames = (stream.shape[1] - frames) // 2
        positions = first_frame - extra_frames + jnp.arange(stream.shape[1], dtype=jnp.int32)
        source = unit_source(stream, margin_width)
        before = dilated(source, kernels[unit_index], dilation) + encoder_dilated_biases[
            unit_index
        ].astype(jnp.float32)
        pointed = jax.nn.elu(before).astype(jnp.bfloat16)
        branch = jnp.einsum(
            "ctd,de->cte",
            pointed,
            encoder_pointwise_tables[unit_index],
            preferred_element_type=jnp.float32,
        )
        branch = branch + encoder_pointwise_offsets[unit_index].astype(jnp.float32)
        kept_list.append((stream, source, before, pointed, positions))
        stream = stream + branch
    return (stream, kept_list)


def stack_backward(grad_stream, kept_list, kernels, encoder_pointwise_tables):
    kernel_grads, offset_grads, mixer_grads, shift_grads = ([], [], [], [])
    for unit_index in reversed(range(UNITS)):
        stream, source, before, pointed, positions = kept_list[unit_index]
        dilation = 3**unit_index
        margin_width = KSIZE // 2 * dilation
        branch_grad = grad_stream.astype(jnp.bfloat16)
        mixer_grads.insert(
            0, jnp.einsum("ctd,cte->de", pointed, branch_grad, preferred_element_type=jnp.float32)
        )
        shift_grads.insert(0, jnp.sum(branch_grad.astype(jnp.float32), axis=(0, 1)))
        pointed_grad = jnp.einsum(
            "cte,de->ctd",
            branch_grad,
            encoder_pointwise_tables[unit_index],
            preferred_element_type=jnp.float32,
        )
        before_grad = (pointed_grad * elu_slope(before)).astype(jnp.bfloat16)
        offset_grads.insert(0, jnp.sum(before_grad.astype(jnp.float32), axis=(0, 1)))
        kernel_grad, source_grad = dilated_back(source, kernels[unit_index], dilation, before_grad)
        kernel_grads.insert(0, kernel_grad)
        owned_grad = source_back(source_grad, margin_width)
        grad_stream = grad_stream + owned_grad * elu_slope(stream)
    return (
        grad_stream,
        (
            jnp.stack(kernel_grads),
            jnp.stack(offset_grads),
            jnp.stack(mixer_grads),
            jnp.stack(shift_grads),
        ),
    )


def over_clips(matrices):
    return (
        lax.psum_scatter(
            matrices[0].astype(jnp.bfloat16), "clip", scatter_dimension=2, tiled=True
        ).astype(jnp.float32),
        lax.psum_scatter(
            matrices[1].astype(jnp.bfloat16), "clip", scatter_dimension=1, tiled=True
        ).astype(jnp.float32),
        lax.psum_scatter(
            matrices[2].astype(jnp.bfloat16), "clip", scatter_dimension=0, tiled=True
        ).astype(jnp.float32),
        lax.psum_scatter(
            matrices[3].astype(jnp.bfloat16), "clip", scatter_dimension=2, tiled=True
        ).astype(jnp.float32),
        lax.psum_scatter(
            matrices[4].astype(jnp.bfloat16), "clip", scatter_dimension=0, tiled=True
        ).astype(jnp.float32),
        lax.psum_scatter(
            matrices[5].astype(jnp.bfloat16), "clip", scatter_dimension=2, tiled=True
        ).astype(jnp.float32),
        lax.psum_scatter(
            matrices[6].astype(jnp.bfloat16), "clip", scatter_dimension=1, tiled=True
        ).astype(jnp.float32),
    )


def over_segments(matrices):
    return (
        lax.psum_scatter(
            matrices[0].astype(jnp.bfloat16), "tm", scatter_dimension=3, tiled=True
        ).astype(jnp.float32),
        lax.psum_scatter(
            matrices[1].astype(jnp.bfloat16), "tm", scatter_dimension=2, tiled=True
        ).astype(jnp.float32),
        lax.psum_scatter(
            matrices[2].astype(jnp.bfloat16), "tm", scatter_dimension=1, tiled=True
        ).astype(jnp.float32),
        lax.psum_scatter(
            matrices[3].astype(jnp.bfloat16), "tm", scatter_dimension=3, tiled=True
        ).astype(jnp.float32),
        lax.psum_scatter(
            matrices[4].astype(jnp.bfloat16), "tm", scatter_dimension=1, tiled=True
        ).astype(jnp.float32),
        lax.psum_scatter(
            matrices[5].astype(jnp.bfloat16), "tm", scatter_dimension=3, tiled=True
        ).astype(jnp.float32),
        lax.psum_scatter(
            matrices[6].astype(jnp.bfloat16), "tm", scatter_dimension=2, tiled=True
        ).astype(jnp.float32),
    )


def on_device(
    incoming_samples,
    sample_extents,
    chosen_entries,
    encoder_dilated_kernels,
    encoder_dilated_biases,
    encoder_pointwise_tables,
    encoder_pointwise_offsets,
    reducing_filter,
    reducing_offset,
    quantizer_tables,
    widening_filter,
    widening_offset,
    decoder_dilated_filters,
    decoder_dilated_offsets,
    decoder_pointwise_tables,
    decoder_pointwise_offsets,
    result_cotangent,
):
    segment = lax.axis_index("tm")
    clips = incoming_samples.shape[0]
    frames = incoming_samples.shape[1]
    channels = incoming_samples.shape[2]
    first_frame = segment * frames
    latents = frames // HOP_FACTOR
    total_count = lax.psum(
        jnp.sum((sample_extents + HOP_FACTOR - 1) // HOP_FACTOR).astype(jnp.float32), "clip"
    )
    stream = incoming_samples.astype(jnp.float32)
    encoded, encoder_kept = stack_forward(
        stream,
        encoder_dilated_kernels,
        encoder_dilated_biases,
        encoder_pointwise_tables,
        encoder_pointwise_offsets,
        first_frame,
        frames,
    )
    reduced_samples = (
        jax.nn.elu(encoded).astype(jnp.bfloat16).reshape(clips, latents, HOP_FACTOR * channels)
    )
    latent = jnp.einsum(
        "kde,er->kdr", reduced_samples, reducing_filter, preferred_element_type=jnp.float32
    ) + reducing_offset.astype(jnp.float32)
    validity = (
        (first_frame + HOP_FACTOR * jnp.arange(latents, dtype=jnp.int32))[None, :]
        < sample_extents[:, None]
    ).astype(jnp.float32)
    masked = validity[..., None]
    group_width = channels // GROUPS
    code_range = jnp.arange(quantizer_tables.shape[2], dtype=jnp.int32)
    loss_local = jnp.float32(0.0)
    quant_parts, commit_parts, book_rows = ([], [], [])
    for group_index in range(GROUPS):
        residue = latent[:, :, group_index * group_width : (group_index + 1) * group_width]
        commit_sum = jnp.zeros_like(residue)
        group_code = jnp.zeros_like(residue)
        level_rows = []
        for level_index in range(LEVELS):
            column = group_index * LEVELS + level_index
            onehot = (chosen_entries[:, :, column][..., None] == code_range).astype(jnp.bfloat16)
            picked = jnp.einsum(
                "kde,er->kdr",
                onehot,
                quantizer_tables[group_index, level_index],
                preferred_element_type=jnp.float32,
            )
            residue = residue - picked
            level_rows.append(
                jnp.einsum(
                    "cnk,cnd->kd",
                    onehot.astype(jnp.float32),
                    -2.0 * masked * residue,
                    precision=lax.Precision.HIGHEST,
                    preferred_element_type=jnp.float32,
                )
            )
            commit_sum = commit_sum + residue
            loss_local = loss_local + jnp.sum(masked * residue * residue)
            group_code = group_code + picked
        book_rows.append(jnp.stack(level_rows))
        commit_parts.append(2.0 * commit_weight * masked * commit_sum)
        quant_parts.append(group_code)
    loss_local = (1.0 + commit_weight) * loss_local
    quantized = jnp.concatenate(quant_parts, axis=2).astype(jnp.bfloat16)
    loss_sum = lax.psum(loss_local, ("clip", "tm"))
    masked_loss = loss_sum / (total_count * channels)
    widened = jnp.einsum(
        "cnd,de->cne", quantized, widening_filter, preferred_element_type=jnp.float32
    )
    decoder_start = (
        widened.reshape(clips, frames, channels) + widening_offset.astype(jnp.float32)
    ).astype(jnp.bfloat16)
    stream = decoder_start.astype(jnp.float32)
    decoded, decoder_kept = stack_forward(
        stream,
        decoder_dilated_filters,
        decoder_dilated_offsets,
        decoder_pointwise_tables,
        decoder_pointwise_offsets,
        first_frame,
        frames,
    )
    output = decoded.astype(jnp.bfloat16)
    grad_decoder, decoder_grads = stack_backward(
        result_cotangent.astype(jnp.float32),
        decoder_kept,
        decoder_dilated_filters,
        decoder_pointwise_tables,
    )
    widened_grad = grad_decoder.astype(jnp.bfloat16)
    spreading_grad = jnp.sum(widened_grad.astype(jnp.float32), axis=(0, 1))
    folded_grad = widened_grad.reshape(clips, latents, HOP_FACTOR * channels)
    upsample_grad = jnp.einsum(
        "cnd,cne->de", quantized, folded_grad, preferred_element_type=jnp.float32
    )
    latent_grad = jnp.einsum(
        "cne,de->cnd", folded_grad, widening_filter, preferred_element_type=jnp.float32
    )
    hidden_first_half = (latent_grad + jnp.concatenate(commit_parts, axis=2)).astype(jnp.bfloat16)
    pooling_grad = jnp.sum(hidden_first_half.astype(jnp.float32), axis=(0, 1))
    downsampling_gradient = jnp.einsum(
        "cnk,cnd->kd", reduced_samples, hidden_first_half, preferred_element_type=jnp.float32
    )
    pooled_grad = jnp.einsum(
        "npk,xk->npx", hidden_first_half, reducing_filter, preferred_element_type=jnp.float32
    )
    pooled_grad = pooled_grad.reshape(clips, frames, channels) * elu_slope(encoded)
    grad_encoder, encoder_grads = stack_backward(
        pooled_grad, encoder_kept, encoder_dilated_kernels, encoder_pointwise_tables
    )
    input_grad = grad_encoder.astype(jnp.bfloat16)
    codebook_grad = jnp.stack(book_rows)
    matrices = (
        encoder_grads[0],
        encoder_grads[2],
        downsampling_gradient,
        codebook_grad,
        upsample_grad,
        decoder_grads[0],
        decoder_grads[2],
    )
    matrices = over_segments(over_clips(matrices))
    biases = lax.psum(
        (
            encoder_grads[1],
            encoder_grads[3],
            pooling_grad,
            spreading_grad,
            decoder_grads[1],
            decoder_grads[3],
        ),
        ("clip", "tm"),
    )
    return (
        output,
        quantized,
        masked_loss,
        input_grad,
        matrices[0],
        biases[0],
        matrices[1],
        biases[1],
        matrices[2],
        biases[2],
        matrices[3],
        matrices[4],
        biases[3],
        matrices[5],
        biases[4],
        matrices[6],
        biases[5],
    )

PAD = 32
RIM = 32
STRIP = 16
CHUNKS = 1
HALO = 16
LANES = 128
LATENT_REACH = 10
GRAD_REACH = 6
NT = (((1,), (1,)), ((), ()))
VMEM_BYTES = 60 * 1024 * 1024


def elu(values):
    return jnp.where(values > 0, values, jnp.exp(jnp.minimum(values, 0.0)) - 1.0)


def slope_from_elu(activated):
    return jnp.where(activated > 0, 1.0, activated + 1.0)


def whole(array):
    return pl.BlockSpec(array.shape, lambda *i: (0,) * len(array.shape))


def smem():
    return pl.BlockSpec(memory_space=pltpu.SMEM)


def compiler_params(axes=1):
    return pltpu.CompilerParams(
        vmem_limit_bytes=VMEM_BYTES, dimension_semantics=("arbitrary",) * axes
    )


def spread(block, lines, pieces, step):
    for tile in range(lines.shape[0]):
        lanes = slice(tile * LANES, (tile + 1) * LANES)
        for start, count, row in pieces:
            lines[tile, pl.ds(HOP_FACTOR * row + step, count, HOP_FACTOR), :] = block[
                start : start + count, lanes
            ]


def start_kernel(codes_ref, tables_ref, filter_ref, offset_ref, q_ref, start_ref, picked_ref, lines):
    clips, count = codes_ref.shape[:2]
    own = count - 2 * HALO
    channels = start_ref.shape[2]
    entries = tables_ref.shape[2]
    entry = lax.broadcasted_iota(jnp.int32, (count, entries), 1)
    offset = offset_ref[...].astype(jnp.float32)
    far = LATENT_REACH - GRAD_REACH
    pieces = (
        (0, own, LATENT_REACH),
        (own, GRAD_REACH, far),
        (own + GRAD_REACH, far, 0),
        (own + HALO, LATENT_REACH, LATENT_REACH + own),
    )
    for clip in range(clips):
        groups = []
        for group in range(GROUPS):
            total = None
            for level in range(LEVELS):
                column = group * LEVELS + level
                onehot = jnp.where(codes_ref[clip, :, column : column + 1] == entry, 1.0, 0.0)
                rows = jnp.dot(
                    onehot.astype(jnp.bfloat16),
                    tables_ref[group, level],
                    preferred_element_type=jnp.float32,
                )
                picked_ref[column, clip] = rows
                total = rows if total is None else total + rows
            groups.append(total)
        quantized = jnp.concatenate(groups, axis=1).astype(jnp.bfloat16)
        q_ref[clip] = quantized[:own]
        for step in range(HOP_FACTOR):
            block = jnp.dot(
                quantized,
                filter_ref[:, step * channels : (step + 1) * channels],
                preferred_element_type=jnp.float32,
            )
            spread(block + offset, lines, pieces, step)
        for tile in range(channels // LANES):
            start_ref[clip, :, tile * LANES : (tile + 1) * LANES] = lines[tile].astype(
                jnp.bfloat16
            )


def start_frames(codes, tables, widening, offset):
    clips, count, _ = codes.shape
    own = count - 2 * HALO
    channels = widening.shape[0]
    frames = HOP_FACTOR * (own + 2 * LATENT_REACH)
    outs = (
        jax.ShapeDtypeStruct((clips, own, channels), jnp.bfloat16),
        jax.ShapeDtypeStruct((clips, frames, channels), jnp.bfloat16),
        jax.ShapeDtypeStruct((GROUPS * LEVELS, clips, count, channels // GROUPS), jnp.float32),
    )
    offset = offset.reshape(1, channels)
    return pl.pallas_call(
        start_kernel,
        grid=(1,),
        in_specs=[whole(codes), whole(tables), whole(widening), whole(offset)],
        out_specs=[whole(out) for out in outs],
        out_shape=outs,
        scratch_shapes=[pltpu.VMEM((channels // LANES, frames, LANES), jnp.float32)],
        compiler_params=compiler_params(),
        name="decoder_start",
    )(codes, tables, widening, offset)


def latent_kernel(
    extents,
    pooled_ref,
    filter_ref,
    offset_ref,
    picked_ref,
    grad_ref,
    send_ref,
    sum_ref,
    out_ref,
    lines,
    pool,
):
    clips, length, channels = pooled_ref.shape
    count = grad_ref.shape[1]
    latents = count - 2 * HALO
    own = HOP_FACTOR * latents
    first = (length - own) // 2
    width = channels // GROUPS
    tiles = channels // LANES
    long = HOP_FACTOR * channels
    for tile in range(tiles):
        lines[tile, length:, :] = jnp.zeros((lines.shape[1] - length, LANES), jnp.float32)
    for clip in range(clips):
        for tile in range(tiles):
            lines[tile, :length, :] = pooled_ref[
                clip, :, tile * LANES : (tile + 1) * LANES
            ].astype(jnp.float32)
        rows = slice(clip * latents, (clip + 1) * latents)
        for step in range(HOP_FACTOR):
            for tile in range(tiles):
                columns = slice(step * channels + tile * LANES, step * channels + (tile + 1) * LANES)
                for to, size, start in (
                    (0, latents, first),
                    (latents, HALO, 0),
                    (latents + HALO, HALO, first + own),
                ):
                    part = lines[tile, pl.ds(start + step, size, HOP_FACTOR), :]
                    part = part.astype(jnp.bfloat16)
                    pool[clip * count + to : clip * count + to + size, columns] = part
                    if to == 0:
                        send_ref[rows, columns] = part
    latent = jnp.dot(
        pool[...], filter_ref[...], preferred_element_type=jnp.float32
    ) + offset_ref[...].astype(jnp.float32)
    row = lax.broadcasted_iota(jnp.int32, (count, width), 0)
    frame = jnp.where(
        row < latents,
        row,
        jnp.where(row < latents + HALO, row - latents - GRAD_REACH, row - HALO),
    )
    position = extents[0] + HOP_FACTOR * frame
    lane = lax.broadcasted_iota(jnp.int32, (latents, LANES), 1)
    pooling = jnp.zeros((1, channels), jnp.float32)
    losses = [jnp.zeros((1, width), jnp.float32) for _ in range(GROUPS)]
    pieces = (
        (0, latents, GRAD_REACH),
        (latents, GRAD_REACH, 0),
        (latents + HALO, GRAD_REACH, GRAD_REACH + latents),
    )
    for clip in range(clips):
        rows = slice(clip * latents, (clip + 1) * latents)
        masked = jnp.where(position < extents[1 + clip], 1.0, 0.0)
        halves = []
        for group in range(GROUPS):
            columns = slice(group * width, (group + 1) * width)
            residue = latent[clip * count : (clip + 1) * count, columns]
            commit = jnp.zeros_like(residue)
            for level in range(LEVELS):
                book = group * LEVELS + level
                residue = residue - picked_ref[book, clip]
                square = (masked * residue * residue)[:latents]
                losses[group] = losses[group] + jnp.sum(square, axis=0, keepdims=True)
                commit = commit + residue
                gap = (-2.0 * masked * residue)[:latents]
                for tile in range(width // LANES):
                    part = gap[:, tile * LANES : (tile + 1) * LANES]
                    turned = pltpu.roll(part, LANES // 2, 1)
                    to = long + channels + book * 2 * width + tile * 2 * LANES
                    send_ref[rows, to : to + LANES] = jnp.where(
                        lane < LANES // 2, part, turned
                    ).astype(jnp.bfloat16)
                    send_ref[rows, to + LANES : to + 2 * LANES] = jnp.where(
                        lane < LANES // 2, turned, part
                    ).astype(jnp.bfloat16)
            glatent = grad_ref[clip, :, columns] + 2.0 * commit_weight * masked * commit
            halves.append(glatent.astype(jnp.bfloat16))
        glatent = jnp.concatenate(halves, axis=1)
        send_ref[rows, long : long + channels] = glatent[:latents]
        pooling = pooling + jnp.sum(
            glatent[:latents].astype(jnp.float32), axis=0, keepdims=True
        )
        for step in range(HOP_FACTOR):
            block = lax.dot_general(
                glatent,
                filter_ref[step * channels : (step + 1) * channels, :],
                NT,
                preferred_element_type=jnp.float32,
            )
            spread(block, lines, pieces, step)
        for tile in range(tiles):
            lanes = slice(tile * LANES, (tile + 1) * LANES)
            pooled = pooled_ref[clip, :, lanes].astype(jnp.float32)
            out_ref[clip, :, lanes] = lines[tile, :length, :] * slope_from_elu(pooled)
    sum_ref[0:1, :] = pooling
    sum_ref[1:2, :] = jnp.concatenate(losses, axis=1)
    total = 0
    for clip in range(clips):
        total = total + (extents[1 + clip] + HOP_FACTOR - 1) // HOP_FACTOR
    sum_ref[2:3, :] = jnp.full((1, channels), total, jnp.int32).astype(jnp.float32)


def latent_frames(extents, pooled, reducing, offset, picked, latent_grad):
    clips, length, channels = pooled.shape
    count = latent_grad.shape[1]
    latents = count - 2 * HALO
    offset = offset.reshape(1, channels)
    outs = (
        jax.ShapeDtypeStruct((clips * latents, (HOP_FACTOR + 5) * channels), jnp.bfloat16),
        jax.ShapeDtypeStruct((8, channels), jnp.float32),
        jax.ShapeDtypeStruct(pooled.shape, jnp.float32),
    )
    rows = length + HOP_FACTOR * HALO
    return pl.pallas_call(
        latent_kernel,
        grid=(1,),
        in_specs=[
            smem(),
            whole(pooled),
            whole(reducing),
            whole(offset),
            whole(picked),
            whole(latent_grad),
        ],
        out_specs=[whole(out) for out in outs],
        out_shape=outs,
        scratch_shapes=[
            pltpu.VMEM((channels // LANES, rows, LANES), jnp.float32),
            pltpu.VMEM((clips * count, HOP_FACTOR * channels), jnp.bfloat16),
        ],
        compiler_params=compiler_params(),
        name="latent_frames",
    )(extents, pooled, reducing, offset, picked, latent_grad)


def dilation_of(unit):
    return jnp.where(unit == 0, 1, jnp.where(unit == 1, 3, 9)).astype(jnp.int32)


def row_of(unit, ref):
    rows = ref[...].astype(jnp.float32)
    return jnp.where(unit == 0, rows[0:1], jnp.where(unit == 1, rows[1:2], rows[2:3]))


def forward_kernel(
    out_first,
    activate,
    where_ref,
    h_ref,
    w_ref,
    b_ref,
    m_ref,
    s_ref,
    e_ref,
    p_ref,
    out_ref,
    stream,
    lines,
):
    clips, length, channels = h_ref.shape
    unit, clip = pl.program_id(0), pl.program_id(1)
    dilation = dilation_of(unit)
    low, high = where_ref[0], where_ref[1]
    tiles = channels // LANES
    rows = length // CHUNKS

    @pl.when(jnp.logical_and(unit == 0, clip == 0))
    def _():
        for tile in range(tiles):
            lines[tile, :PAD, :] = jnp.zeros((PAD, LANES), jnp.float32)
            lines[tile, PAD + length :, :] = jnp.zeros((PAD, LANES), jnp.float32)

    @pl.when(unit == 0)
    def _():
        stream[clip] = h_ref[clip].astype(jnp.float32)

    position = lax.broadcasted_iota(jnp.int32, (length, LANES), 0)
    inside = (position >= low) & (position < high)
    for tile in range(tiles):
        lanes = slice(tile * LANES, (tile + 1) * LANES)
        active = jnp.where(inside, elu(stream[clip, :, lanes]), 0.0).astype(jnp.bfloat16)
        e_ref[0, 0, :, lanes] = active
        lines[tile, PAD : PAD + length, :] = active.astype(jnp.float32)
    kernel = w_ref[0].reshape(KSIZE * channels, channels)
    mixer = m_ref[0]
    bias = row_of(unit, b_ref)
    shift = row_of(unit, s_ref)
    for chunk in range(CHUNKS):
        taps = []
        for tap in range(KSIZE):
            start = PAD + chunk * rows + (tap - KSIZE // 2) * dilation
            for tile in range(tiles):
                taps.append(lines[tile, pl.ds(start, rows), :].astype(jnp.bfloat16))
        before = jnp.dot(
            jnp.concatenate(taps, axis=1), kernel, preferred_element_type=jnp.float32
        )
        pointed = elu(before + bias).astype(jnp.bfloat16)
        span = slice(chunk * rows, (chunk + 1) * rows)
        p_ref[0, 0, span, :] = pointed
        branch = jnp.dot(pointed, mixer, preferred_element_type=jnp.float32) + shift
        stream[clip, span, :] = stream[clip, span, :] + branch

    @pl.when(unit == UNITS - 1)
    def _():
        final = stream[clip, out_first : out_first + out_ref.shape[1], :]
        out_ref[0] = (elu(final) if activate else final).astype(out_ref.dtype)


def forward_units(where, h, kernels, biases, mixers, shifts, out_rows, activate):
    clips, length, channels = h.shape
    kept = jax.ShapeDtypeStruct((UNITS, clips, length, channels), jnp.bfloat16)
    kept_spec = pl.BlockSpec((1, 1, length, channels), lambda u, c: (u, c, 0, 0))
    return pl.pallas_call(
        functools.partial(forward_kernel, (length - out_rows) // 2, activate),
        grid=(UNITS, clips),
        in_specs=[
            smem(),
            whole(h),
            pl.BlockSpec((1, KSIZE, channels, channels), lambda u, c: (u, 0, 0, 0)),
            whole(biases),
            pl.BlockSpec((1, channels, channels), lambda u, c: (u, 0, 0)),
            whole(shifts),
        ],
        out_specs=[
            kept_spec,
            kept_spec,
            pl.BlockSpec(
                (1, out_rows, channels), lambda u, c: (jnp.where(u == UNITS - 1, c, 0), 0, 0)
            ),
        ],
        out_shape=(
            kept,
            kept,
            jax.ShapeDtypeStruct((clips, out_rows, channels), jnp.bfloat16),
        ),
        scratch_shapes=[
            pltpu.VMEM((clips, length, channels), jnp.float32),
            pltpu.VMEM((channels // LANES, length + 2 * PAD, LANES), jnp.float32),
        ],
        compiler_params=compiler_params(2),
        name="units_forward",
    )(where, h, kernels, biases, mixers, shifts)


def backward_kernel(
    unit_first,
    units,
    own,
    final,
    data,
    place,
    gh_ref,
    p_ref,
    e_ref,
    m_ref,
    *rest,
):
    if data:
        w_ref, send_ref, keep_ref, sum_ref, out_ref, grad, lines, turned = rest
    else:
        send_ref, keep_ref, sum_ref, grad, turned = rest
    clips, length, channels = gh_ref.shape
    step, clip = pl.program_id(0), pl.program_id(1)
    dilation = dilation_of(unit_first - step)
    tiles = channels // LANES
    kept_length = p_ref.shape[2]
    kept_first = (kept_length - length) // 2
    own_first = (length - own) // 2
    wide = own + 2 * RIM
    rows = own + 2 * STRIP
    first = own_first - STRIP
    low, high, core = place[0], place[1], place[2]

    if data:

        @pl.when(jnp.logical_and(step == 0, clip == 0))
        def _():
            for tile in range(tiles):
                lines[tile, :PAD, :] = jnp.zeros((PAD, LANES), jnp.float32)
                lines[tile, PAD + length :, :] = jnp.zeros((PAD, LANES), jnp.float32)

    @pl.when(step == 0)
    def _():
        grad[clip] = gh_ref[clip].astype(jnp.float32)

    gc = grad[clip].astype(jnp.bfloat16)
    send_ref[0, 0, wide : wide + own, :] = gc[own_first : own_first + own]
    gp = lax.dot_general(gc, m_ref[0], NT, preferred_element_type=jnp.float32)
    pointed = p_ref[0, 0, kept_first : kept_first + length, :].astype(jnp.float32)
    position = lax.broadcasted_iota(jnp.int32, (length, channels), 0)
    inside = (position >= low) & (position < high)
    ga = jnp.where(inside, gp * slope_from_elu(pointed), 0.0).astype(jnp.bfloat16)
    send_ref[0, 0, :wide, :] = ga[own_first - RIM : own_first + own + RIM]
    ga = ga.astype(jnp.float32)
    a_sum = jnp.sum(ga[own_first : own_first + own], axis=0, keepdims=True)
    c_sum = jnp.sum(gc[own_first : own_first + own].astype(jnp.float32), axis=0, keepdims=True)
    o_sum = jnp.zeros_like(a_sum)
    if data:
        for tile in range(tiles):
            lines[tile, PAD : PAD + length, :] = ga[:, tile * LANES : (tile + 1) * LANES]
        kernel = jnp.concatenate([w_ref[0, tap] for tap in range(KSIZE)], axis=1)
        size = rows // CHUNKS
        for chunk in range(CHUNKS):
            begin = first + chunk * size
            moved = jnp.concatenate(
                [
                    lines[
                        tile, pl.ds(PAD + begin - (tap - KSIZE // 2) * dilation, size), :
                    ].astype(jnp.bfloat16)
                    for tap in range(KSIZE)
                    for tile in range(tiles)
                ],
                axis=1,
            )
            total = lax.dot_general(moved, kernel, NT, preferred_element_type=jnp.float32)
            active = e_ref[0, 0, kept_first + begin : kept_first + begin + size, :]
            grad[clip, begin : begin + size, :] = grad[
                clip, begin : begin + size, :
            ] + total * slope_from_elu(active.astype(jnp.float32))

        if final:
            own_grad = grad[clip, own_first : own_first + own, :].astype(jnp.bfloat16)
            o_sum = jnp.sum(own_grad.astype(jnp.float32), axis=0, keepdims=True)

            @pl.when(step == units - 1)
            def _():
                out_ref[0] = own_grad
        else:

            @pl.when(step == units - 1)
            def _():
                out_ref[0] = grad[clip]

    sums = jnp.concatenate([a_sum, c_sum, o_sum], axis=0)

    @pl.when(clip == 0)
    def _():
        sum_ref[0, :3, :] = sums

    @pl.when(clip > 0)
    def _():
        sum_ref[0, :3, :] = sum_ref[0, :3, :] + sums

    base = wide + own
    block = channels // 8
    start = (kept_length - own) // 2
    for which, ref in enumerate((e_ref, p_ref)):
        turned[...] = jnp.transpose(ref[0, 0, start : start + own, :])
        for rx in range(2):
            for ry in range(2):
                pair = jnp.bitwise_xor(place[4], ry) * 4 + jnp.bitwise_xor(place[3], rx) * 2
                to = which * (channels // 2) + (rx * 2 + ry) * block
                mine = pl.multiple_of((pair + core) * block, block)
                other = pl.multiple_of((pair + 1 - core) * block, block)
                keep_ref[0, 0, to : to + block, :] = turned[pl.ds(mine, block), :]
                send_ref[0, 0, base + to : base + to + block, :] = turned[pl.ds(other, block), :]


def backward_units(place, gh, p, e, kernels, mixers, unit_first, units, own, data=True):
    clips, length, channels = gh.shape
    kept_length = p.shape[2]
    payload = 2 * own + 2 * RIM + channels
    final = unit_first - units + 1 == 0
    kept_spec = pl.BlockSpec(
        (1, 1, kept_length, channels), lambda u, c: (unit_first - u, c, 0, 0)
    )
    out = (
        jax.ShapeDtypeStruct((clips, own, channels), jnp.bfloat16)
        if final
        else jax.ShapeDtypeStruct((clips, length, channels), jnp.float32)
    )
    tiles = channels // LANES
    operands = [place, gh, p, e, mixers]
    in_specs = [
        smem(),
        whole(gh),
        kept_spec,
        kept_spec,
        pl.BlockSpec((1, channels, channels), lambda u, c: (unit_first - u, 0, 0)),
    ]
    out_specs = [
        pl.BlockSpec((1, 1, payload, channels), lambda u, c: (u, c, 0, 0)),
        pl.BlockSpec((1, 1, channels, own), lambda u, c: (u, c, 0, 0)),
        pl.BlockSpec((1, 8, channels), lambda u, c: (u, 0, 0)),
    ]
    outs = [
        jax.ShapeDtypeStruct((units, clips, payload, channels), jnp.bfloat16),
        jax.ShapeDtypeStruct((units, clips, channels, own), jnp.bfloat16),
        jax.ShapeDtypeStruct((units, 8, channels), jnp.float32),
    ]
    scratch = [pltpu.VMEM((clips, length, channels), jnp.float32)]
    if data:
        operands.append(kernels)
        in_specs.append(
            pl.BlockSpec((1, KSIZE, channels, channels), lambda u, c: (unit_first - u, 0, 0, 0))
        )
        outs.append(out)
        out_specs.append(
            pl.BlockSpec(
                (1,) + out.shape[1:], lambda u, c: (jnp.where(u == units - 1, c, 0), 0, 0)
            )
        )
        scratch.append(pltpu.VMEM((tiles, length + 2 * PAD, LANES), jnp.float32))
    return pl.pallas_call(
        functools.partial(backward_kernel, unit_first, units, own, final, data),
        grid=(units, clips),
        in_specs=in_specs,
        out_specs=out_specs,
        out_shape=outs,
        scratch_shapes=scratch + [pltpu.VMEM((channels, own), jnp.bfloat16)],
        compiler_params=compiler_params(2),
        name="units_backward",
    )(*operands)


def stream_kernel(own, gh_ref, send_ref, e_ref, w_ref, out_ref, lines):
    length, channels = gh_ref.shape[1:]
    tiles = channels // LANES
    first = (length - own) // 2
    kept_first = (e_ref.shape[2] - own) // 2
    wide = own + 2 * RIM
    for tile in range(tiles):
        lanes = slice(tile * LANES, (tile + 1) * LANES)
        lines[tile] = send_ref[0, 0, :wide, lanes].astype(jnp.float32)
    kernel = jnp.concatenate([w_ref[0, tap] for tap in range(KSIZE)], axis=1)
    size = own // CHUNKS
    for chunk in range(CHUNKS):
        begin = chunk * size
        moved = jnp.concatenate(
            [
                lines[tile, start : start + size, :].astype(jnp.bfloat16)
                for start in (RIM + begin - tap + KSIZE // 2 for tap in range(KSIZE))
                for tile in range(tiles)
            ],
            axis=1,
        )
        total = lax.dot_general(moved, kernel, NT, preferred_element_type=jnp.float32)
        active = e_ref[0, 0, kept_first + begin : kept_first + begin + size, :]
        stream = gh_ref[0, first + begin : first + begin + size, :]
        out_ref[0, begin : begin + size, :] = (
            stream + total * slope_from_elu(active.astype(jnp.float32))
        ).astype(out_ref.dtype)


def stream_gradient(gh, send, e, kernels, own):
    clips, length, channels = gh.shape
    payload, kept_length = send.shape[2], e.shape[2]
    return pl.pallas_call(
        functools.partial(stream_kernel, own),
        grid=(clips,),
        in_specs=[
            pl.BlockSpec((1, length, channels), lambda c: (c, 0, 0)),
            pl.BlockSpec((1, 1, payload, channels), lambda c: (0, c, 0, 0)),
            pl.BlockSpec((1, 1, kept_length, channels), lambda c: (0, c, 0, 0)),
            pl.BlockSpec((1, KSIZE, channels, channels), lambda c: (0, 0, 0, 0)),
        ],
        out_specs=pl.BlockSpec((1, own, channels), lambda c: (c, 0, 0)),
        out_shape=jax.ShapeDtypeStruct((clips, own, channels), jnp.bfloat16),
        scratch_shapes=[
            pltpu.VMEM((channels // LANES, own + 2 * RIM, LANES), jnp.float32)
        ],
        compiler_params=compiler_params(),
        name="stream_gradient",
    )(gh, send, e, kernels)


def emit(result, start, tap_rows, first_axis, send_ref, keep_ref):
    result = result.astype(jnp.bfloat16)
    quarter = result.shape[0] // 4
    for rx in range(2):
        for ry in range(2):
            first, second = (rx, ry) if first_axis == 0 else (ry, rx)
            target = send_ref if first == 1 else keep_ref
            rows = slice((rx * 2 + ry) * quarter, (rx * 2 + ry + 1) * quarter)
            for segment in range(4):
                target[second, segment, pl.ds(start, tap_rows), :] = result[
                    rows, segment * LANES : (segment + 1) * LANES
                ]


def emit_outputs(rows):
    out = jax.ShapeDtypeStruct((2, 4, rows, LANES), jnp.bfloat16)
    return (out,) * 4


def weights_kernel(
    unit_first, units, own, with_up, place, mine_ref, other_ref, keep_ref, *rest
):
    if with_up:
        up_mine, up_other, filter_ref, sx, kx, sy, ky, latent_ref, lines, turned = rest
    else:
        sx, kx, sy, ky, lines = rest
    clips, channels = mine_ref.shape[1], mine_ref.shape[3]
    tiles = channels // LANES
    half = channels // 2
    block = channels // 8
    wide = own + 2 * RIM
    base = wide + own
    sources = (mine_ref, other_ref)
    step = pl.program_id(0)
    unit = unit_first - step // (KSIZE + 1)
    tap = lax.rem(step, KSIZE + 1)
    dilation = dilation_of(unit)
    normal = step < units * (KSIZE + 1)

    @pl.when(jnp.logical_and(normal, tap == 0))
    def _():
        for source in range(2):
            for clip in range(clips):
                for tile in range(tiles):
                    lines[source * clips + clip, tile, :, :] = sources[source][
                        0, clip, :wide, tile * LANES : (tile + 1) * LANES
                    ].astype(jnp.float32)

    def left(which):
        pieces = [
            keep_ref[0, clip, which * half : (which + 1) * half, :] for clip in range(clips)
        ] + [
            other_ref[0, clip, base + which * half : base + (which + 1) * half, :]
            for clip in range(clips)
        ]
        return jnp.concatenate(pieces, axis=1)

    def right():
        start = RIM - (tap - KSIZE // 2) * dilation
        return jnp.concatenate(
            [
                jnp.concatenate(
                    [
                        lines[item, tile, pl.ds(start, own), :].astype(jnp.bfloat16)
                        for tile in range(tiles)
                    ],
                    axis=1,
                )
                for item in range(2 * clips)
            ],
            axis=0,
        )

    half_taps = (KSIZE + 1) // 2

    @pl.when(jnp.logical_and(normal, tap < half_taps))
    def _():
        result = jnp.dot(left(0), right(), preferred_element_type=jnp.float32)
        emit(result, pl.multiple_of(tap * block, block), block, 0, sx, kx)

    @pl.when(jnp.logical_and(normal, jnp.logical_and(tap >= half_taps, tap < KSIZE)))
    def _():
        result = jnp.dot(left(0), right(), preferred_element_type=jnp.float32)
        start = pl.multiple_of((tap - half_taps) * block, block)
        emit(result, start, block, 1, sy, ky)

    @pl.when(jnp.logical_and(normal, tap == KSIZE))
    def _():
        grads = jnp.concatenate(
            [source[0, clip, wide:base, :] for source in sources for clip in range(clips)], axis=0
        )
        result = jnp.dot(left(1), grads, preferred_element_type=jnp.float32)
        emit(result, (half_taps - 1) * block, block, 1, sy, ky)

    if with_up:

        @pl.when(jnp.logical_not(normal))
        def _():
            up_kernel(place, up_mine, up_other, sx, kx, sy, ky, turned)
            latent_ref[...] = lax.dot_general(
                up_mine[:, channels:], filter_ref[...], NT, preferred_element_type=jnp.float32
            )


def weights_units(place, mine, other, keep, unit_first, own, up=None):
    units, clips, payload, channels = mine.shape
    steps = units * (KSIZE + 1)
    taps = KSIZE + 1
    rows = channels // 2
    groups = units + (0 if up is None else 1)
    out = jax.ShapeDtypeStruct((2, 4, groups * rows, LANES), jnp.bfloat16)
    out_spec = pl.BlockSpec((2, 4, rows, LANES), lambda i: (0, 0, i // taps, 0))

    def of_unit(array):
        return pl.BlockSpec(
            (1,) + array.shape[1:], lambda i: (jnp.minimum(i // taps, units - 1), 0, 0, 0)
        )

    scratch = [pltpu.VMEM((2 * clips, channels // LANES, own + 2 * RIM, LANES), jnp.float32)]
    more = ()
    out_specs, outs = [out_spec] * 4, (out,) * 4
    if up is not None:
        more = tuple(up)
        outs += (jax.ShapeDtypeStruct((up[0].shape[0], channels), jnp.float32),)
        out_specs.append(whole(outs[4]))
        scratch.append(pltpu.VMEM((channels, 2 * up[0].shape[0]), jnp.bfloat16))
    return pl.pallas_call(
        functools.partial(weights_kernel, unit_first, units, own, up is not None),
        grid=(steps + (0 if up is None else 1),),
        in_specs=[smem(), of_unit(mine), of_unit(other), of_unit(keep)]
        + [whole(array) for array in more],
        out_specs=out_specs,
        out_shape=outs,
        scratch_shapes=scratch,
        compiler_params=compiler_params(),
        name="units_weights",
    )(place, mine, other, keep, *more)


def relative_rows(place, ref, block, start, count):
    pieces = []
    for rx in range(2):
        for ry in range(2):
            pair = jnp.bitwise_xor(place[4], ry) * 4 + jnp.bitwise_xor(place[3], rx) * 2
            first = pl.multiple_of((pair + place[2]) * block + start, 16)
            pieces.append(ref[pl.ds(first, count), :])
    return jnp.concatenate(pieces, axis=0)


def up_kernel(place, mine_ref, other_ref, sx, kx, sy, ky, turned):
    latents = mine_ref.shape[0]
    channels = turned.shape[0]
    for source, ref in enumerate((mine_ref, other_ref)):
        turned[:, source * latents : (source + 1) * latents] = jnp.transpose(ref[:, :channels])
    left = relative_rows(place, turned, channels // 8, 0, channels // 8)
    for tap in range(8):
        right = jnp.concatenate(
            [
                jnp.concatenate(
                    [
                        ref[:, channels + (z * 8 + tap) * LANES : channels + (z * 8 + tap + 1) * LANES]
                        for z in range(4)
                    ],
                    axis=1,
                )
                for ref in (mine_ref, other_ref)
            ],
            axis=0,
        )
        result = jnp.dot(left, right, preferred_element_type=jnp.float32)
        if tap < 4:
            emit(result, tap * (channels // 8), channels // 8, 0, sx, kx)
        else:
            emit(result, (tap - 4) * (channels // 8), channels // 8, 1, sy, ky)


def down_kernel(place, codes_ref, mine_ref, other_ref, sx, kx, sy, ky, turned):
    latents = mine_ref.shape[0]
    long = turned.shape[0]
    channels = long // 8
    refs = (mine_ref, other_ref)
    for source, ref in enumerate(refs):
        turned[:, source * latents : (source + 1) * latents] = jnp.transpose(ref[:, :long])
    right = jnp.concatenate([ref[:, long : long + channels] for ref in refs], axis=0)
    block = channels // 8
    for tap in range(8):
        left = relative_rows(place, turned, channels, tap * block, block)
        result = jnp.dot(left, right, preferred_element_type=jnp.float32)
        if tap < 4:
            emit(result, tap * block, block, 0, sx, kx)
        else:
            emit(result, (tap - 4) * block, block, 1, sy, ky)
    lane = lax.broadcasted_iota(jnp.int32, (4 * 64, channels), 1)
    row = lax.broadcasted_iota(jnp.int32, (64, 2 * latents), 0)
    for book in range(4):
        gaps = jnp.concatenate(
            [
                ref[:, long + channels + book * channels : long + channels + (book + 1) * channels]
                for ref in refs
            ],
            axis=0,
        )
        codes = codes_ref[book : book + 1, :]
        parts = []
        for part in range(2):
            pieces = []
            for rx in range(2):
                for ry in range(2):
                    pair = jnp.bitwise_xor(place[4], ry) * 4 + jnp.bitwise_xor(place[3], rx) * 2
                    first = (pair + place[2]) * 128 + part * 64
                    pieces.append(jnp.where(codes == row + first, 1.0, 0.0).astype(jnp.bfloat16))
            parts.append(
                jnp.dot(
                    jnp.concatenate(pieces, axis=0), gaps, preferred_element_type=jnp.float32
                )
            )
        result = jnp.where(lax.rem(lane, LANES) < 64, parts[0], parts[1])
        if book < 2:
            emit(result, 4 * block + book * 64, 64, 0, sx, kx)
        else:
            emit(result, 4 * block + (book - 2) * 64, 64, 1, sy, ky)


def down_gradient(place, codes, mine, other, channels):
    outs = emit_outputs(channels // 2 + 128)
    return pl.pallas_call(
        down_kernel,
        grid=(1,),
        in_specs=[smem(), whole(codes), whole(mine), whole(other)],
        out_specs=[whole(out) for out in outs],
        out_shape=outs,
        scratch_shapes=[pltpu.VMEM((8 * channels, 2 * mine.shape[0]), jnp.bfloat16)],
        compiler_params=compiler_params(),
        name="downsample_weights",
    )(place, codes, mine, other)


def swap(block, bit):
    return lax.ppermute(block, "clip", [(i, i ^ bit) for i in range(lax.axis_size("clip"))])


def turn(block, distance):
    count = lax.axis_size("tm")
    return lax.ppermute(block, "tm", [(i, (i + distance) % count) for i in range(count)])


def added(*parts):
    total = parts[0].astype(jnp.float32)
    for part in parts[1:]:
        total = total + part.astype(jnp.float32)
    return total


def after(value, *others):
    return lax.optimization_barrier((value,) + others)[0]


class Lane:
    def __init__(self):
        self.clock = None
        self.ready = ()
        self.flights = []

    def fly(self, arrays, then, kernels=1):
        self.flights.append([kernels, arrays, then])

    def land(self, outs):
        arrived = [flight for flight in self.flights if flight[0] <= 1]
        self.flights = [[n - 1, arrays, then] for n, arrays, then in self.flights if n > 1]
        flat = [array for _, arrays, _ in arrived for array in arrays]
        held = lax.optimization_barrier(tuple(outs) + tuple(flat))
        outs, flat = held[: len(outs)], held[len(outs) :]
        self.clock = outs[0]
        self.ready = ()
        for _, arrays, then in arrived:
            then(*flat[: len(arrays)])
            flat = flat[len(arrays) :]
        return outs

    def run(self, kernel, first, *others):
        if self.clock is not None:
            first = after(first, self.clock, *self.ready)
        return self.land(kernel(first, *others))

    def scatter(self, pieces, done, kernels=(1, 1)):
        sx, kx, sy, ky = pieces

        def second(ax, ay):
            bx = added(kx[1], ax[1]).astype(jnp.bfloat16)
            by = added(ky[1], ay[1]).astype(jnp.bfloat16)
            self.ready += (bx, by)

            def third(cx, cy):
                blocks = jnp.concatenate(
                    [
                        added(kx[0], ax[0], cx).astype(jnp.bfloat16),
                        added(ky[0], ay[0], cy).astype(jnp.bfloat16),
                    ],
                    axis=1,
                )
                self.ready += (blocks,)
                done(blocks)

            self.fly((swap(bx, 4), swap(by, 2)), third, kernels[1])

        self.fly((swap(sx, 2), swap(sy, 4)), second, kernels[0])

    def segments(self, groups, done):
        blocks = jnp.concatenate(groups, axis=1) if len(groups) > 1 else groups[0]
        self.ready += (blocks,)
        total = lax.psum_scatter(blocks, "tm", scatter_dimension=0).astype(jnp.float32)
        start = 0
        for group in groups:
            done.append(total[start : start + group.shape[1]])
            start += group.shape[1]

    def everywhere(self, value, split, done):
        steps = [("tm", bit) for bit in (1, 2)] + [("clip", bit) for bit in (1, 2, 4)]

        def step(value, index):
            if index == len(steps):
                parts = split(value)
                self.ready += parts
                done.extend(parts)
                return
            axis, bit = steps[index]
            pairs = [(i, i ^ bit) for i in range(lax.axis_size(axis))]
            self.ready += (value,)
            self.fly(
                (lax.ppermute(value, axis, pairs),), lambda other: step(value + other, index + 1)
            )

        step(value, 0)

    def finish(self):
        while self.flights:
            tick = self.ready or (self.clock,)
            self.land(tick)


def neighbours(block, reach):
    ends = lax.axis_size("tm") - 1
    head = block[:, :reach]
    tail = block[:, block.shape[1] - reach :]
    return (
        lax.ppermute(tail, "tm", [(i, i + 1) for i in range(ends)]),
        lax.ppermute(head, "tm", [(i + 1, i) for i in range(ends)]),
    )


def latent_rows(block, below, above):
    widths = ((0, 0), (0, HALO - below.shape[1]), (0, 0))
    return jnp.concatenate([block, jnp.pad(below, widths), jnp.pad(above, widths)], axis=1)


def with_both(one, reach_one, two, reach_two):
    ends = lax.axis_size("tm") - 1
    tail = jnp.concatenate(
        [one[:, one.shape[1] - reach_one :], two[:, two.shape[1] - reach_two :]], axis=1
    )
    head = jnp.concatenate([one[:, :reach_one], two[:, :reach_two]], axis=1)
    below = lax.ppermute(tail, "tm", [(i, i + 1) for i in range(ends)])
    above = lax.ppermute(head, "tm", [(i + 1, i) for i in range(ends)])
    return (
        jnp.concatenate([below[:, :reach_one], one, above[:, :reach_one]], axis=1),
        jnp.concatenate([below[:, reach_one:], two, above[:, reach_one:]], axis=1),
    )


def split_units(reduced, channels):
    block = channels // 8
    taps = [part.reshape(8, block, LANES) for part in reduced]
    return jnp.stack([part[:KSIZE] for part in taps]), jnp.stack([part[KSIZE] for part in taps])


def fast_device(
    incoming_samples,
    sample_extents,
    chosen_entries,
    encoder_dilated_kernels,
    encoder_dilated_biases,
    encoder_pointwise_tables,
    encoder_pointwise_offsets,
    reducing_filter,
    reducing_offset,
    quantizer_tables,
    widening_filter,
    widening_offset,
    decoder_dilated_filters,
    decoder_dilated_offsets,
    decoder_pointwise_tables,
    decoder_pointwise_offsets,
    result_cotangent,
):
    f32, bf16 = jnp.float32, jnp.bfloat16
    segment = lax.axis_index("tm")
    member = lax.axis_index("clip")
    clips, frames, channels = incoming_samples.shape
    latents = frames // HOP_FACTOR
    all_frames = frames * lax.axis_size("tm")
    first_frame = segment * frames
    group_width = channels // GROUPS

    def bounds(reach):
        return jnp.stack([reach - first_frame, all_frames - first_frame + reach])

    coordinates = jnp.stack(
        [member % 2, (member // 2) % 2, (member // 4) % 2, segment]
    ).astype(jnp.int32)

    def placed(reach):
        return jnp.concatenate([bounds(reach).astype(jnp.int32), coordinates])

    reach = LATENT_REACH * HOP_FACTOR
    grad_reach = GRAD_REACH * HOP_FACTOR
    where = bounds(reach).astype(jnp.int32)
    place = placed(grad_reach)

    lane = Lane()
    below, above = neighbours(chosen_entries, LATENT_REACH)
    far = LATENT_REACH - GRAD_REACH
    below = jnp.concatenate([below[:, far:], below[:, :far]], axis=1)
    codes = latent_rows(chosen_entries, below, above)
    cotangent, samples = with_both(result_cotangent, grad_reach, incoming_samples, reach)
    own_codes = chosen_entries.reshape(clips * latents, GROUPS * LEVELS).T
    pair_codes = []
    lane.fly(
        (swap(own_codes, 1),),
        lambda other: pair_codes.append(jnp.concatenate([own_codes, other], axis=1)),
        2,
    )

    quantized, start, picked = lane.run(
        lambda c: start_frames(c, quantizer_tables, widening_filter, widening_offset), codes
    )

    e_decoder, p_decoder, output = lane.run(
        lambda h: forward_units(
            where,
            h,
            decoder_dilated_filters,
            decoder_dilated_offsets,
            decoder_pointwise_tables,
            decoder_pointwise_offsets,
            frames,
            False,
        ),
        start,
    )

    reduced = {}
    sizes = {"a": 2, "b": 2, "c": 2}
    batches = {name: [] for name in sizes}
    order = {name: [] for name in sizes}

    def into(batch, name):
        def done(blocks):
            batches[batch].append(blocks)
            order[batch].append(name)
            if len(batches[batch]) == sizes[batch]:
                reduced[batch] = []
                lane.segments(batches[batch], reduced[batch])

        return done

    def backward(grad, p, e, kernels, tables, unit, units, data=True, kernels_between=1):
        send, keep, sums, *grad = lane.run(
            lambda g: backward_units(place, g, p, e, kernels, tables, unit, units, frames, data),
            grad,
        )
        grad = grad[0] if data else None
        work = [send, None, keep]

        def arrived(other):
            work[1] = other

        lane.fly((swap(send, 1),), arrived, kernels_between)
        return grad, work, sums

    def weights(work, unit, batch, name, up=None, kernels=(1, 1)):
        send, other, keep = work
        pieces = lane.run(
            lambda mine: weights_units(place, mine, other, keep, unit, frames, up), send
        )
        lane.scatter(pieces[:4], into(batch, name), kernels)
        return pieces[4:]

    decoder = (p_decoder, e_decoder, decoder_dilated_filters, decoder_pointwise_tables)
    grad_start, decoder_last, sums_last = backward(cotangent, *decoder, 2, 1)
    grad_start, decoder_rest, sums_rest = backward(grad_start, *decoder, 1, 2)

    widened_grad = grad_start
    folded = widened_grad.reshape(clips * latents, HOP_FACTOR * channels)
    up_send = jnp.concatenate([quantized.reshape(clips * latents, channels), folded], axis=1)
    up = (up_send, swap(up_send, 1), widening_filter)
    weights(decoder_last, 2, "a", "d2", None, (1, 2))
    (latent_grad,) = weights(decoder_rest, 1, "a", "d10up", up, (2, 1))
    latent_grad = latent_grad.reshape(clips, latents, channels)
    latent_grads = []
    lane.fly(
        neighbours(latent_grad, GRAD_REACH),
        lambda below, above: latent_grads.append(latent_rows(latent_grad, below, above)),
    )

    e_encoder, p_encoder, pooled_wide = lane.run(
        lambda h: forward_units(
            where,
            h,
            encoder_dilated_kernels,
            encoder_dilated_biases,
            encoder_pointwise_tables,
            encoder_pointwise_offsets,
            frames + 2 * grad_reach,
            True,
        ),
        samples,
    )
    extents = jnp.concatenate([jnp.reshape(first_frame, (1,)), sample_extents]).astype(jnp.int32)
    down_send, latent_sums, pooled_grad = lane.run(
        lambda p: latent_frames(
            extents, p, reducing_filter, reducing_offset, picked, latent_grads[0]
        ),
        pooled_wide,
    )
    down_other = []
    lane.fly((swap(down_send, 1),), down_other.append)

    encoder = (p_encoder, e_encoder, encoder_dilated_kernels, encoder_pointwise_tables)
    grad, work_2, sums_2 = backward(pooled_grad, *encoder, 2, 1)
    pieces = lane.run(
        lambda mine: down_gradient(place, pair_codes[0], mine, down_other[0], channels), down_send
    )
    lane.scatter(pieces, into("b", "down"), (1, 1))
    grad, work_1, sums_1 = backward(grad, *encoder, 1, 1)
    weights(work_2, 2, "b", "e2")
    _, work_0, sums_0 = backward(grad, *encoder, 0, 1, False)
    small = jnp.concatenate(
        [
            sums.reshape(-1, channels)
            for sums in (sums_0, sums_1, sums_2, sums_rest, sums_last, latent_sums)
        ],
        axis=0,
    )
    summed = []

    def parts(small):
        rows = small.reshape(7, 8, channels)
        loss_sum = (1.0 + commit_weight) * jnp.sum(rows[6, 1])
        total_count = rows[6, 2, 0] / lax.axis_size("tm")
        decoder_rows = jnp.stack([rows[4], rows[3], rows[5]])
        return (
            loss_sum / (total_count * channels),
            rows[:3, 0],
            rows[:3, 1],
            rows[6, 0],
            rows[4, 2],
            decoder_rows[:, 0],
            decoder_rows[:, 1],
        )

    lane.everywhere(small, parts, summed)
    weights(work_1, 1, "c", "e1")
    weights(work_0, 0, "c", "e0")
    (input_grad,) = lane.run(
        lambda g: (stream_gradient(g, work_0[0], e_encoder, encoder_dilated_kernels, frames),),
        grad,
    )
    lane.finish()
    result = {}
    for batch in order:
        for name, part in zip(order[batch], reduced[batch]):
            result[name] = part

    block = channels // 8
    rest = result["d10up"].reshape(2, UNITS, channels // 2, LANES)
    decoder_parts = [rest[:, 1], rest[:, 0], result["d2"]]
    encoder_parts = [result["e0"], result["e1"], result["e2"]]
    analysis, mixers = split_units(encoder_parts, channels)
    synthesis, remixers = split_units(decoder_parts, channels)
    up_rows = rest[:, 2].reshape(8, block, LANES)
    upsample = up_rows.transpose(1, 0, 2).reshape(block, 8 * LANES)
    halves = result["down"].reshape(2, channels // 2 + 128, LANES)
    downsample = halves[:, : channels // 2].reshape(8 * block, LANES)
    codebooks = (
        halves[:, channels // 2 :]
        .reshape(GROUPS, LEVELS, 64, 2, 64)
        .transpose(0, 1, 3, 2, 4)
        .reshape(GROUPS, LEVELS, 128, 64)
    )
    masked_loss, offsets, shifts, pooling, spreading, biasing, tilting = summed
    return (
        output,
        quantized,
        masked_loss,
        input_grad,
        analysis,
        offsets,
        mixers,
        shifts,
        downsample,
        pooling,
        codebooks,
        upsample,
        spreading,
        synthesis,
        biasing,
        remixers,
        tilting,
    )


def solution(mesh):
    placed = (
        P("clip", "tm", None),
        P("clip"),
        P("clip", "tm", None),
        P(),
        P(),
        P(),
        P(),
        P(),
        P(),
        P(),
        P(),
        P(),
        P(),
        P(),
        P(),
        P(),
        P("clip", "tm", None),
    )
    matched = mesh.shape["clip"] == 8 and mesh.shape["tm"] == 4
    return jax.shard_map(
        fast_device if matched else on_device,
        mesh=mesh,
        in_specs=placed,
        out_specs=(
            P("clip", "tm", None),
            P("clip", "tm", None),
            P(),
            P("clip", "tm", None),
            P(None, None, "clip", "tm"),
            P(),
            P(None, "clip", "tm"),
            P(),
            P("clip", "tm"),
            P(),
            P(None, None, "clip", "tm"),
            P("clip", "tm"),
            P(),
            P(None, None, "clip", "tm"),
            P(),
            P(None, "clip", "tm"),
            P(),
        ),
        check_vma=False,
    )
```

```python
import functools

import jax
import jax.numpy as jnp
from jax import lax
from jax.experimental import pallas as pl
from jax.experimental.pallas import tpu as pltpu
from jax.sharding import PartitionSpec as P

GROUPS = 2
LEVELS = 2
KSIZE = 7
UNITS = 3
HOP_FACTOR = 8


commit_weight = 0.25


def from_behind(block, axis, distance):
    devices = range(lax.axis_size(axis))
    route = [(i - distance, i) for i in devices if i - distance in devices]
    return lax.ppermute(block, axis, route)


def padded(cells, sides, width):
    for axis, dim in sides:
        count = lax.axis_size(axis)
        ends = count - 1
        head = lax.slice_in_dim(cells, 0, width, axis=dim)
        tail = lax.slice_in_dim(cells, cells.shape[dim] - width, cells.shape[dim], axis=dim)
        cells = jnp.concatenate(
            [
                lax.ppermute(tail, axis, [(i, (i + 1) % count) for i in range(ends)]),
                cells,
                lax.ppermute(head, axis, [((i + 1) % count, i) for i in range(ends)]),
            ],
            axis=dim,
        )
    return cells


def elu_slope(values):
    return jnp.where(values > 0, 1.0, jnp.exp(jnp.minimum(values, 0.0)))


def gather_taps(source, dilation, frames):
    return jnp.concatenate(
        [
            source[:, tap_index * dilation : tap_index * dilation + frames]
            for tap_index in range(KSIZE)
        ],
        axis=2,
    )


def dilated(source, kernel, dilation):
    frames = source.shape[1] - (KSIZE - 1) * dilation
    stacked = gather_taps(source, dilation, frames)
    flattened = kernel.reshape(KSIZE * kernel.shape[1], kernel.shape[2])
    return jnp.einsum("cti,io->cto", stacked, flattened, preferred_element_type=jnp.float32)


def dilated_back(source, kernel, dilation, grad_out):
    frames = grad_out.shape[1]
    stacked = gather_taps(source, dilation, frames)
    flattened = kernel.reshape(KSIZE * kernel.shape[1], kernel.shape[2])
    kernel_grad = jnp.einsum(
        "cti,cto->io", stacked, grad_out, preferred_element_type=jnp.float32
    ).reshape(kernel.shape)
    spread = jnp.einsum("cto,io->cti", grad_out, flattened, preferred_element_type=jnp.float32)
    channels = kernel.shape[1]
    source_grad = jnp.zeros(source.shape, jnp.float32)
    for tap_index in range(KSIZE):
        source_grad = source_grad.at[:, tap_index * dilation : tap_index * dilation + frames].add(
            spread[:, :, tap_index * channels : (tap_index + 1) * channels]
        )
    return (kernel_grad, source_grad)


def return_rims(grad_full, margin_width):
    length = grad_full.shape[1]
    owned = grad_full[:, margin_width : length - margin_width]
    from_above = from_behind(grad_full[:, :margin_width].astype(jnp.bfloat16), "tm", -1).astype(
        jnp.float32
    )
    from_below = from_behind(
        grad_full[:, length - margin_width :].astype(jnp.bfloat16), "tm", 1
    ).astype(jnp.float32)
    owned = owned.at[:, owned.shape[1] - margin_width :].add(from_above)
    return owned.at[:, :margin_width].add(from_below)


def unit_source(stream, margin_width):
    activated = jax.nn.elu(stream)
    return padded(activated.astype(jnp.bfloat16), (("tm", 1),), margin_width)


def source_back(source_grad, margin_width):
    return return_rims(source_grad, margin_width)


def stack_forward(
    stream,
    kernels,
    encoder_dilated_biases,
    encoder_pointwise_tables,
    encoder_pointwise_offsets,
    first_frame,
    frames,
):
    kept_list = []
    for unit_index in range(UNITS):
        dilation = 3**unit_index
        margin_width = KSIZE // 2 * dilation
        extra_frames = (stream.shape[1] - frames) // 2
        positions = first_frame - extra_frames + jnp.arange(stream.shape[1], dtype=jnp.int32)
        source = unit_source(stream, margin_width)
        before = dilated(source, kernels[unit_index], dilation) + encoder_dilated_biases[
            unit_index
        ].astype(jnp.float32)
        pointed = jax.nn.elu(before).astype(jnp.bfloat16)
        branch = jnp.einsum(
            "ctd,de->cte",
            pointed,
            encoder_pointwise_tables[unit_index],
            preferred_element_type=jnp.float32,
        )
        branch = branch + encoder_pointwise_offsets[unit_index].astype(jnp.float32)
        kept_list.append((stream, source, before, pointed, positions))
        stream = stream + branch
    return (stream, kept_list)


def stack_backward(grad_stream, kept_list, kernels, encoder_pointwise_tables):
    kernel_grads, offset_grads, mixer_grads, shift_grads = ([], [], [], [])
    for unit_index in reversed(range(UNITS)):
        stream, source, before, pointed, positions = kept_list[unit_index]
        dilation = 3**unit_index
        margin_width = KSIZE // 2 * dilation
        branch_grad = grad_stream.astype(jnp.bfloat16)
        mixer_grads.insert(
            0, jnp.einsum("ctd,cte->de", pointed, branch_grad, preferred_element_type=jnp.float32)
        )
        shift_grads.insert(0, jnp.sum(branch_grad.astype(jnp.float32), axis=(0, 1)))
        pointed_grad = jnp.einsum(
            "cte,de->ctd",
            branch_grad,
            encoder_pointwise_tables[unit_index],
            preferred_element_type=jnp.float32,
        )
        before_grad = (pointed_grad * elu_slope(before)).astype(jnp.bfloat16)
        offset_grads.insert(0, jnp.sum(before_grad.astype(jnp.float32), axis=(0, 1)))
        kernel_grad, source_grad = dilated_back(source, kernels[unit_index], dilation, before_grad)
        kernel_grads.insert(0, kernel_grad)
        owned_grad = source_back(source_grad, margin_width)
        grad_stream = grad_stream + owned_grad * elu_slope(stream)
    return (
        grad_stream,
        (
            jnp.stack(kernel_grads),
            jnp.stack(offset_grads),
            jnp.stack(mixer_grads),
            jnp.stack(shift_grads),
        ),
    )


def over_clips(matrices):
    return (
        lax.psum_scatter(
            matrices[0].astype(jnp.bfloat16), "clip", scatter_dimension=2, tiled=True
        ).astype(jnp.float32),
        lax.psum_scatter(
            matrices[1].astype(jnp.bfloat16), "clip", scatter_dimension=1, tiled=True
        ).astype(jnp.float32),
        lax.psum_scatter(
            matrices[2].astype(jnp.bfloat16), "clip", scatter_dimension=0, tiled=True
        ).astype(jnp.float32),
        lax.psum_scatter(
            matrices[3].astype(jnp.bfloat16), "clip", scatter_dimension=2, tiled=True
        ).astype(jnp.float32),
        lax.psum_scatter(
            matrices[4].astype(jnp.bfloat16), "clip", scatter_dimension=0, tiled=True
        ).astype(jnp.float32),
        lax.psum_scatter(
            matrices[5].astype(jnp.bfloat16), "clip", scatter_dimension=2, tiled=True
        ).astype(jnp.float32),
        lax.psum_scatter(
            matrices[6].astype(jnp.bfloat16), "clip", scatter_dimension=1, tiled=True
        ).astype(jnp.float32),
    )


def over_segments(matrices):
    return (
        lax.psum_scatter(
            matrices[0].astype(jnp.bfloat16), "tm", scatter_dimension=3, tiled=True
        ).astype(jnp.float32),
        lax.psum_scatter(
            matrices[1].astype(jnp.bfloat16), "tm", scatter_dimension=2, tiled=True
        ).astype(jnp.float32),
        lax.psum_scatter(
            matrices[2].astype(jnp.bfloat16), "tm", scatter_dimension=1, tiled=True
        ).astype(jnp.float32),
        lax.psum_scatter(
            matrices[3].astype(jnp.bfloat16), "tm", scatter_dimension=3, tiled=True
        ).astype(jnp.float32),
        lax.psum_scatter(
            matrices[4].astype(jnp.bfloat16), "tm", scatter_dimension=1, tiled=True
        ).astype(jnp.float32),
        lax.psum_scatter(
            matrices[5].astype(jnp.bfloat16), "tm", scatter_dimension=3, tiled=True
        ).astype(jnp.float32),
        lax.psum_scatter(
            matrices[6].astype(jnp.bfloat16), "tm", scatter_dimension=2, tiled=True
        ).astype(jnp.float32),
    )


def on_device(
    incoming_samples,
    sample_extents,
    chosen_entries,
    encoder_dilated_kernels,
    encoder_dilated_biases,
    encoder_pointwise_tables,
    encoder_pointwise_offsets,
    reducing_filter,
    reducing_offset,
    quantizer_tables,
    widening_filter,
    widening_offset,
    decoder_dilated_filters,
    decoder_dilated_offsets,
    decoder_pointwise_tables,
    decoder_pointwise_offsets,
    result_cotangent,
):
    segment = lax.axis_index("tm")
    clips = incoming_samples.shape[0]
    frames = incoming_samples.shape[1]
    channels = incoming_samples.shape[2]
    first_frame = segment * frames
    latents = frames // HOP_FACTOR
    total_count = lax.psum(
        jnp.sum((sample_extents + HOP_FACTOR - 1) // HOP_FACTOR).astype(jnp.float32), "clip"
    )
    stream = incoming_samples.astype(jnp.float32)
    encoded, encoder_kept = stack_forward(
        stream,
        encoder_dilated_kernels,
        encoder_dilated_biases,
        encoder_pointwise_tables,
        encoder_pointwise_offsets,
        first_frame,
        frames,
    )
    reduced_samples = (
        jax.nn.elu(encoded).astype(jnp.bfloat16).reshape(clips, latents, HOP_FACTOR * channels)
    )
    latent = jnp.einsum(
        "kde,er->kdr", reduced_samples, reducing_filter, preferred_element_type=jnp.float32
    ) + reducing_offset.astype(jnp.float32)
    validity = (
        (first_frame + HOP_FACTOR * jnp.arange(latents, dtype=jnp.int32))[None, :]
        < sample_extents[:, None]
    ).astype(jnp.float32)
    masked = validity[..., None]
    group_width = channels // GROUPS
    code_range = jnp.arange(quantizer_tables.shape[2], dtype=jnp.int32)
    loss_local = jnp.float32(0.0)
    quant_parts, commit_parts, book_rows = ([], [], [])
    for group_index in range(GROUPS):
        residue = latent[:, :, group_index * group_width : (group_index + 1) * group_width]
        commit_sum = jnp.zeros_like(residue)
        group_code = jnp.zeros_like(residue)
        level_rows = []
        for level_index in range(LEVELS):
            column = group_index * LEVELS + level_index
            onehot = (chosen_entries[:, :, column][..., None] == code_range).astype(jnp.bfloat16)
            picked = jnp.einsum(
                "kde,er->kdr",
                onehot,
                quantizer_tables[group_index, level_index],
                preferred_element_type=jnp.float32,
            )
            residue = residue - picked
            level_rows.append(
                jnp.einsum(
                    "cnk,cnd->kd",
                    onehot.astype(jnp.float32),
                    -2.0 * masked * residue,
                    precision=lax.Precision.HIGHEST,
                    preferred_element_type=jnp.float32,
                )
            )
            commit_sum = commit_sum + residue
            loss_local = loss_local + jnp.sum(masked * residue * residue)
            group_code = group_code + picked
        book_rows.append(jnp.stack(level_rows))
        commit_parts.append(2.0 * commit_weight * masked * commit_sum)
        quant_parts.append(group_code)
    loss_local = (1.0 + commit_weight) * loss_local
    quantized = jnp.concatenate(quant_parts, axis=2).astype(jnp.bfloat16)
    loss_sum = lax.psum(loss_local, ("clip", "tm"))
    masked_loss = loss_sum / (total_count * channels)
    widened = jnp.einsum(
        "cnd,de->cne", quantized, widening_filter, preferred_element_type=jnp.float32
    )
    decoder_start = (
        widened.reshape(clips, frames, channels) + widening_offset.astype(jnp.float32)
    ).astype(jnp.bfloat16)
    stream = decoder_start.astype(jnp.float32)
    decoded, decoder_kept = stack_forward(
        stream,
        decoder_dilated_filters,
        decoder_dilated_offsets,
        decoder_pointwise_tables,
        decoder_pointwise_offsets,
        first_frame,
        frames,
    )
    output = decoded.astype(jnp.bfloat16)
    grad_decoder, decoder_grads = stack_backward(
        result_cotangent.astype(jnp.float32),
        decoder_kept,
        decoder_dilated_filters,
        decoder_pointwise_tables,
    )
    widened_grad = grad_decoder.astype(jnp.bfloat16)
    spreading_grad = jnp.sum(widened_grad.astype(jnp.float32), axis=(0, 1))
    folded_grad = widened_grad.reshape(clips, latents, HOP_FACTOR * channels)
    upsample_grad = jnp.einsum(
        "cnd,cne->de", quantized, folded_grad, preferred_element_type=jnp.float32
    )
    latent_grad = jnp.einsum(
        "cne,de->cnd", folded_grad, widening_filter, preferred_element_type=jnp.float32
    )
    hidden_first_half = (latent_grad + jnp.concatenate(commit_parts, axis=2)).astype(jnp.bfloat16)
    pooling_grad = jnp.sum(hidden_first_half.astype(jnp.float32), axis=(0, 1))
    downsampling_gradient = jnp.einsum(
        "cnk,cnd->kd", reduced_samples, hidden_first_half, preferred_element_type=jnp.float32
    )
    pooled_grad = jnp.einsum(
        "npk,xk->npx", hidden_first_half, reducing_filter, preferred_element_type=jnp.float32
    )
    pooled_grad = pooled_grad.reshape(clips, frames, channels) * elu_slope(encoded)
    grad_encoder, encoder_grads = stack_backward(
        pooled_grad, encoder_kept, encoder_dilated_kernels, encoder_pointwise_tables
    )
    input_grad = grad_encoder.astype(jnp.bfloat16)
    codebook_grad = jnp.stack(book_rows)
    matrices = (
        encoder_grads[0],
        encoder_grads[2],
        downsampling_gradient,
        codebook_grad,
        upsample_grad,
        decoder_grads[0],
        decoder_grads[2],
    )
    matrices = over_segments(over_clips(matrices))
    biases = lax.psum(
        (
            encoder_grads[1],
            encoder_grads[3],
            pooling_grad,
            spreading_grad,
            decoder_grads[1],
            decoder_grads[3],
        ),
        ("clip", "tm"),
    )
    return (
        output,
        quantized,
        masked_loss,
        input_grad,
        matrices[0],
        biases[0],
        matrices[1],
        biases[1],
        matrices[2],
        biases[2],
        matrices[3],
        matrices[4],
        biases[3],
        matrices[5],
        biases[4],
        matrices[6],
        biases[5],
    )

PAD = 32
RIM = 32
STRIP = 16
CHUNKS = 1
HALO = 16
LANES = 128
LATENT_REACH = 10
GRAD_REACH = 6
NT = (((1,), (1,)), ((), ()))
VMEM_BYTES = 60 * 1024 * 1024


def elu(values):
    return jnp.where(values > 0, values, jnp.exp(jnp.minimum(values, 0.0)) - 1.0)


def slope_from_elu(activated):
    return jnp.where(activated > 0, 1.0, activated + 1.0)


def whole(array):
    return pl.BlockSpec(array.shape, lambda *i: (0,) * len(array.shape))


def smem():
    return pl.BlockSpec(memory_space=pltpu.SMEM)


def compiler_params(axes=1):
    return pltpu.CompilerParams(
        vmem_limit_bytes=VMEM_BYTES, dimension_semantics=("arbitrary",) * axes
    )


def spread(block, lines, pieces, step):
    for tile in range(lines.shape[0]):
        lanes = slice(tile * LANES, (tile + 1) * LANES)
        for start, count, row in pieces:
            lines[tile, pl.ds(HOP_FACTOR * row + step, count, HOP_FACTOR), :] = block[
                start : start + count, lanes
            ]


def start_kernel(codes_ref, tables_ref, filter_ref, offset_ref, q_ref, start_ref, picked_ref, lines):
    clips, count = codes_ref.shape[:2]
    own = count - 2 * HALO
    channels = start_ref.shape[2]
    entries = tables_ref.shape[2]
    entry = lax.broadcasted_iota(jnp.int32, (count, entries), 1)
    offset = offset_ref[...].astype(jnp.float32)
    far = LATENT_REACH - GRAD_REACH
    pieces = (
        (0, own, LATENT_REACH),
        (own, GRAD_REACH, far),
        (own + GRAD_REACH, far, 0),
        (own + HALO, LATENT_REACH, LATENT_REACH + own),
    )
    for clip in range(clips):
        groups = []
        for group in range(GROUPS):
            total = None
            for level in range(LEVELS):
                column = group * LEVELS + level
                onehot = jnp.where(codes_ref[clip, :, column : column + 1] == entry, 1.0, 0.0)
                rows = jnp.dot(
                    onehot.astype(jnp.bfloat16),
                    tables_ref[group, level],
                    preferred_element_type=jnp.float32,
                )
                picked_ref[column, clip] = rows
                total = rows if total is None else total + rows
            groups.append(total)
        quantized = jnp.concatenate(groups, axis=1).astype(jnp.bfloat16)
        q_ref[clip] = quantized[:own]
        for step in range(HOP_FACTOR):
            block = jnp.dot(
                quantized,
                filter_ref[:, step * channels : (step + 1) * channels],
                preferred_element_type=jnp.float32,
            )
            spread(block + offset, lines, pieces, step)
        for tile in range(channels // LANES):
            start_ref[clip, :, tile * LANES : (tile + 1) * LANES] = lines[tile].astype(
                jnp.bfloat16
            )


def start_frames(codes, tables, widening, offset):
    clips, count, _ = codes.shape
    own = count - 2 * HALO
    channels = widening.shape[0]
    frames = HOP_FACTOR * (own + 2 * LATENT_REACH)
    outs = (
        jax.ShapeDtypeStruct((clips, own, channels), jnp.bfloat16),
        jax.ShapeDtypeStruct((clips, frames, channels), jnp.bfloat16),
        jax.ShapeDtypeStruct((GROUPS * LEVELS, clips, count, channels // GROUPS), jnp.float32),
    )
    offset = offset.reshape(1, channels)
    return pl.pallas_call(
        start_kernel,
        grid=(1,),
        in_specs=[whole(codes), whole(tables), whole(widening), whole(offset)],
        out_specs=[whole(out) for out in outs],
        out_shape=outs,
        scratch_shapes=[pltpu.VMEM((channels // LANES, frames, LANES), jnp.float32)],
        compiler_params=compiler_params(),
        name="decoder_start",
    )(codes, tables, widening, offset)


def latent_kernel(
    extents,
    pooled_ref,
    filter_ref,
    offset_ref,
    picked_ref,
    grad_ref,
    send_ref,
    sum_ref,
    out_ref,
    lines,
    pool,
):
    clips, length, channels = pooled_ref.shape
    count = grad_ref.shape[1]
    latents = count - 2 * HALO
    own = HOP_FACTOR * latents
    first = (length - own) // 2
    width = channels // GROUPS
    tiles = channels // LANES
    long = HOP_FACTOR * channels
    for tile in range(tiles):
        lines[tile, length:, :] = jnp.zeros((lines.shape[1] - length, LANES), jnp.float32)
    for clip in range(clips):
        for tile in range(tiles):
            lines[tile, :length, :] = pooled_ref[
                clip, :, tile * LANES : (tile + 1) * LANES
            ].astype(jnp.float32)
        rows = slice(clip * latents, (clip + 1) * latents)
        for step in range(HOP_FACTOR):
            for tile in range(tiles):
                columns = slice(step * channels + tile * LANES, step * channels + (tile + 1) * LANES)
                for to, size, start in (
                    (0, latents, first),
                    (latents, HALO, 0),
                    (latents + HALO, HALO, first + own),
                ):
                    part = lines[tile, pl.ds(start + step, size, HOP_FACTOR), :]
                    part = part.astype(jnp.bfloat16)
                    pool[clip * count + to : clip * count + to + size, columns] = part
                    if to == 0:
                        send_ref[rows, columns] = part
    latent = jnp.dot(
        pool[...], filter_ref[...], preferred_element_type=jnp.float32
    ) + offset_ref[...].astype(jnp.float32)
    row = lax.broadcasted_iota(jnp.int32, (count, width), 0)
    frame = jnp.where(
        row < latents,
        row,
        jnp.where(row < latents + HALO, row - latents - GRAD_REACH, row - HALO),
    )
    position = extents[0] + HOP_FACTOR * frame
    lane = lax.broadcasted_iota(jnp.int32, (latents, LANES), 1)
    pooling = jnp.zeros((1, channels), jnp.float32)
    losses = [jnp.zeros((1, width), jnp.float32) for _ in range(GROUPS)]
    pieces = (
        (0, latents, GRAD_REACH),
        (latents, GRAD_REACH, 0),
        (latents + HALO, GRAD_REACH, GRAD_REACH + latents),
    )
    for clip in range(clips):
        rows = slice(clip * latents, (clip + 1) * latents)
        masked = jnp.where(position < extents[1 + clip], 1.0, 0.0)
        halves = []
        for group in range(GROUPS):
            columns = slice(group * width, (group + 1) * width)
            residue = latent[clip * count : (clip + 1) * count, columns]
            commit = jnp.zeros_like(residue)
            for level in range(LEVELS):
                book = group * LEVELS + level
                residue = residue - picked_ref[book, clip]
                square = (masked * residue * residue)[:latents]
                losses[group] = losses[group] + jnp.sum(square, axis=0, keepdims=True)
                commit = commit + residue
                gap = (-2.0 * masked * residue)[:latents]
                for tile in range(width // LANES):
                    part = gap[:, tile * LANES : (tile + 1) * LANES]
                    turned = pltpu.roll(part, LANES // 2, 1)
                    to = long + channels + book * 2 * width + tile * 2 * LANES
                    send_ref[rows, to : to + LANES] = jnp.where(
                        lane < LANES // 2, part, turned
                    ).astype(jnp.bfloat16)
                    send_ref[rows, to + LANES : to + 2 * LANES] = jnp.where(
                        lane < LANES // 2, turned, part
                    ).astype(jnp.bfloat16)
            glatent = grad_ref[clip, :, columns] + 2.0 * commit_weight * masked * commit
            halves.append(glatent.astype(jnp.bfloat16))
        glatent = jnp.concatenate(halves, axis=1)
        send_ref[rows, long : long + channels] = glatent[:latents]
        pooling = pooling + jnp.sum(
            glatent[:latents].astype(jnp.float32), axis=0, keepdims=True
        )
        for step in range(HOP_FACTOR):
            block = lax.dot_general(
                glatent,
                filter_ref[step * channels : (step + 1) * channels, :],
                NT,
                preferred_element_type=jnp.float32,
            )
            spread(block, lines, pieces, step)
        for tile in range(tiles):
            lanes = slice(tile * LANES, (tile + 1) * LANES)
            pooled = pooled_ref[clip, :, lanes].astype(jnp.float32)
            out_ref[clip, :, lanes] = lines[tile, :length, :] * slope_from_elu(pooled)
    sum_ref[0:1, :] = pooling
    sum_ref[1:2, :] = jnp.concatenate(losses, axis=1)
    total = 0
    for clip in range(clips):
        total = total + (extents[1 + clip] + HOP_FACTOR - 1) // HOP_FACTOR
    sum_ref[2:3, :] = jnp.full((1, channels), total, jnp.int32).astype(jnp.float32)


def latent_frames(extents, pooled, reducing, offset, picked, latent_grad):
    clips, length, channels = pooled.shape
    count = latent_grad.shape[1]
    latents = count - 2 * HALO
    offset = offset.reshape(1, channels)
    outs = (
        jax.ShapeDtypeStruct((clips * latents, (HOP_FACTOR + 5) * channels), jnp.bfloat16),
        jax.ShapeDtypeStruct((8, channels), jnp.float32),
        jax.ShapeDtypeStruct(pooled.shape, jnp.float32),
    )
    rows = length + HOP_FACTOR * HALO
    return pl.pallas_call(
        latent_kernel,
        grid=(1,),
        in_specs=[
            smem(),
            whole(pooled),
            whole(reducing),
            whole(offset),
            whole(picked),
            whole(latent_grad),
        ],
        out_specs=[whole(out) for out in outs],
        out_shape=outs,
        scratch_shapes=[
            pltpu.VMEM((channels // LANES, rows, LANES), jnp.float32),
            pltpu.VMEM((clips * count, HOP_FACTOR * channels), jnp.bfloat16),
        ],
        compiler_params=compiler_params(),
        name="latent_frames",
    )(extents, pooled, reducing, offset, picked, latent_grad)


def dilation_of(unit):
    return jnp.where(unit == 0, 1, jnp.where(unit == 1, 3, 9)).astype(jnp.int32)


def row_of(unit, ref):
    rows = ref[...].astype(jnp.float32)
    return jnp.where(unit == 0, rows[0:1], jnp.where(unit == 1, rows[1:2], rows[2:3]))


def forward_kernel(
    out_first,
    activate,
    where_ref,
    h_ref,
    w_ref,
    b_ref,
    m_ref,
    s_ref,
    e_ref,
    p_ref,
    out_ref,
    stream,
    lines,
):
    clips, length, channels = h_ref.shape
    unit, clip = pl.program_id(0), pl.program_id(1)
    dilation = dilation_of(unit)
    low, high = where_ref[0], where_ref[1]
    tiles = channels // LANES
    rows = length // CHUNKS

    @pl.when(jnp.logical_and(unit == 0, clip == 0))
    def _():
        for tile in range(tiles):
            lines[tile, :PAD, :] = jnp.zeros((PAD, LANES), jnp.float32)
            lines[tile, PAD + length :, :] = jnp.zeros((PAD, LANES), jnp.float32)

    @pl.when(unit == 0)
    def _():
        stream[clip] = h_ref[clip].astype(jnp.float32)

    position = lax.broadcasted_iota(jnp.int32, (length, LANES), 0)
    inside = (position >= low) & (position < high)
    for tile in range(tiles):
        lanes = slice(tile * LANES, (tile + 1) * LANES)
        active = jnp.where(inside, elu(stream[clip, :, lanes]), 0.0).astype(jnp.bfloat16)
        e_ref[0, 0, :, lanes] = active
        lines[tile, PAD : PAD + length, :] = active.astype(jnp.float32)
    kernel = w_ref[0].reshape(KSIZE * channels, channels)
    mixer = m_ref[0]
    bias = row_of(unit, b_ref)
    shift = row_of(unit, s_ref)
    for chunk in range(CHUNKS):
        taps = []
        for tap in range(KSIZE):
            start = PAD + chunk * rows + (tap - KSIZE // 2) * dilation
            for tile in range(tiles):
                taps.append(lines[tile, pl.ds(start, rows), :].astype(jnp.bfloat16))
        before = jnp.dot(
            jnp.concatenate(taps, axis=1), kernel, preferred_element_type=jnp.float32
        )
        pointed = elu(before + bias).astype(jnp.bfloat16)
        span = slice(chunk * rows, (chunk + 1) * rows)
        p_ref[0, 0, span, :] = pointed
        branch = jnp.dot(pointed, mixer, preferred_element_type=jnp.float32) + shift
        stream[clip, span, :] = stream[clip, span, :] + branch

    @pl.when(unit == UNITS - 1)
    def _():
        final = stream[clip, out_first : out_first + out_ref.shape[1], :]
        out_ref[0] = (elu(final) if activate else final).astype(out_ref.dtype)


def forward_units(where, h, kernels, biases, mixers, shifts, out_rows, activate):
    clips, length, channels = h.shape
    kept = jax.ShapeDtypeStruct((UNITS, clips, length, channels), jnp.bfloat16)
    kept_spec = pl.BlockSpec((1, 1, length, channels), lambda u, c: (u, c, 0, 0))
    return pl.pallas_call(
        functools.partial(forward_kernel, (length - out_rows) // 2, activate),
        grid=(UNITS, clips),
        in_specs=[
            smem(),
            whole(h),
            pl.BlockSpec((1, KSIZE, channels, channels), lambda u, c: (u, 0, 0, 0)),
            whole(biases),
            pl.BlockSpec((1, channels, channels), lambda u, c: (u, 0, 0)),
            whole(shifts),
        ],
        out_specs=[
            kept_spec,
            kept_spec,
            pl.BlockSpec(
                (1, out_rows, channels), lambda u, c: (jnp.where(u == UNITS - 1, c, 0), 0, 0)
            ),
        ],
        out_shape=(
            kept,
            kept,
            jax.ShapeDtypeStruct((clips, out_rows, channels), jnp.bfloat16),
        ),
        scratch_shapes=[
            pltpu.VMEM((clips, length, channels), jnp.float32),
            pltpu.VMEM((channels // LANES, length + 2 * PAD, LANES), jnp.float32),
        ],
        compiler_params=compiler_params(2),
        name="units_forward",
    )(where, h, kernels, biases, mixers, shifts)


def backward_kernel(
    unit_first,
    units,
    own,
    final,
    data,
    place,
    gh_ref,
    p_ref,
    e_ref,
    m_ref,
    *rest,
):
    if data:
        w_ref, send_ref, keep_ref, sum_ref, out_ref, grad, lines, turned = rest
    else:
        send_ref, keep_ref, sum_ref, grad, turned = rest
    clips, length, channels = gh_ref.shape
    step, clip = pl.program_id(0), pl.program_id(1)
    dilation = dilation_of(unit_first - step)
    tiles = channels // LANES
    kept_length = p_ref.shape[2]
    kept_first = (kept_length - length) // 2
    own_first = (length - own) // 2
    wide = own + 2 * RIM
    rows = own + 2 * STRIP
    first = own_first - STRIP
    low, high, core = place[0], place[1], place[2]

    if data:

        @pl.when(jnp.logical_and(step == 0, clip == 0))
        def _():
            for tile in range(tiles):
                lines[tile, :PAD, :] = jnp.zeros((PAD, LANES), jnp.float32)
                lines[tile, PAD + length :, :] = jnp.zeros((PAD, LANES), jnp.float32)

    @pl.when(step == 0)
    def _():
        grad[clip] = gh_ref[clip].astype(jnp.float32)

    gc = grad[clip].astype(jnp.bfloat16)
    send_ref[0, 0, wide : wide + own, :] = gc[own_first : own_first + own]
    gp = lax.dot_general(gc, m_ref[0], NT, preferred_element_type=jnp.float32)
    pointed = p_ref[0, 0, kept_first : kept_first + length, :].astype(jnp.float32)
    position = lax.broadcasted_iota(jnp.int32, (length, channels), 0)
    inside = (position >= low) & (position < high)
    ga = jnp.where(inside, gp * slope_from_elu(pointed), 0.0).astype(jnp.bfloat16)
    send_ref[0, 0, :wide, :] = ga[own_first - RIM : own_first + own + RIM]
    ga = ga.astype(jnp.float32)
    a_sum = jnp.sum(ga[own_first : own_first + own], axis=0, keepdims=True)
    c_sum = jnp.sum(gc[own_first : own_first + own].astype(jnp.float32), axis=0, keepdims=True)
    o_sum = jnp.zeros_like(a_sum)
    if data:
        for tile in range(tiles):
            lines[tile, PAD : PAD + length, :] = ga[:, tile * LANES : (tile + 1) * LANES]
        kernel = jnp.concatenate([w_ref[0, tap] for tap in range(KSIZE)], axis=1)
        size = rows // CHUNKS
        for chunk in range(CHUNKS):
            begin = first + chunk * size
            moved = jnp.concatenate(
                [
                    lines[
                        tile, pl.ds(PAD + begin - (tap - KSIZE // 2) * dilation, size), :
                    ].astype(jnp.bfloat16)
                    for tap in range(KSIZE)
                    for tile in range(tiles)
                ],
                axis=1,
            )
            total = lax.dot_general(moved, kernel, NT, preferred_element_type=jnp.float32)
            active = e_ref[0, 0, kept_first + begin : kept_first + begin + size, :]
            grad[clip, begin : begin + size, :] = grad[
                clip, begin : begin + size, :
            ] + total * slope_from_elu(active.astype(jnp.float32))

        if final:
            own_grad = grad[clip, own_first : own_first + own, :].astype(jnp.bfloat16)
            o_sum = jnp.sum(own_grad.astype(jnp.float32), axis=0, keepdims=True)

            @pl.when(step == units - 1)
            def _():
                out_ref[0] = own_grad
        else:

            @pl.when(step == units - 1)
            def _():
                out_ref[0] = grad[clip]

    sums = jnp.concatenate([a_sum, c_sum, o_sum], axis=0)

    @pl.when(clip == 0)
    def _():
        sum_ref[0, :3, :] = sums

    @pl.when(clip > 0)
    def _():
        sum_ref[0, :3, :] = sum_ref[0, :3, :] + sums

    base = wide + own
    block = channels // 8
    start = (kept_length - own) // 2
    for which, ref in enumerate((e_ref, p_ref)):
        turned[...] = jnp.transpose(ref[0, 0, start : start + own, :])
        for rx in range(2):
            for ry in range(2):
                pair = jnp.bitwise_xor(place[4], ry) * 4 + jnp.bitwise_xor(place[3], rx) * 2
                to = which * (channels // 2) + (rx * 2 + ry) * block
                mine = pl.multiple_of((pair + core) * block, block)
                other = pl.multiple_of((pair + 1 - core) * block, block)
                keep_ref[0, 0, to : to + block, :] = turned[pl.ds(mine, block), :]
                send_ref[0, 0, base + to : base + to + block, :] = turned[pl.ds(other, block), :]


def backward_units(place, gh, p, e, kernels, mixers, unit_first, units, own, data=True):
    clips, length, channels = gh.shape
    kept_length = p.shape[2]
    payload = 2 * own + 2 * RIM + channels
    final = unit_first - units + 1 == 0
    kept_spec = pl.BlockSpec(
        (1, 1, kept_length, channels), lambda u, c: (unit_first - u, c, 0, 0)
    )
    out = (
        jax.ShapeDtypeStruct((clips, own, channels), jnp.bfloat16)
        if final
        else jax.ShapeDtypeStruct((clips, length, channels), jnp.float32)
    )
    tiles = channels // LANES
    operands = [place, gh, p, e, mixers]
    in_specs = [
        smem(),
        whole(gh),
        kept_spec,
        kept_spec,
        pl.BlockSpec((1, channels, channels), lambda u, c: (unit_first - u, 0, 0)),
    ]
    out_specs = [
        pl.BlockSpec((1, 1, payload, channels), lambda u, c: (u, c, 0, 0)),
        pl.BlockSpec((1, 1, channels, own), lambda u, c: (u, c, 0, 0)),
        pl.BlockSpec((1, 8, channels), lambda u, c: (u, 0, 0)),
    ]
    outs = [
        jax.ShapeDtypeStruct((units, clips, payload, channels), jnp.bfloat16),
        jax.ShapeDtypeStruct((units, clips, channels, own), jnp.bfloat16),
        jax.ShapeDtypeStruct((units, 8, channels), jnp.float32),
    ]
    scratch = [pltpu.VMEM((clips, length, channels), jnp.float32)]
    if data:
        operands.append(kernels)
        in_specs.append(
            pl.BlockSpec((1, KSIZE, channels, channels), lambda u, c: (unit_first - u, 0, 0, 0))
        )
        outs.append(out)
        out_specs.append(
            pl.BlockSpec(
                (1,) + out.shape[1:], lambda u, c: (jnp.where(u == units - 1, c, 0), 0, 0)
            )
        )
        scratch.append(pltpu.VMEM((tiles, length + 2 * PAD, LANES), jnp.float32))
    return pl.pallas_call(
        functools.partial(backward_kernel, unit_first, units, own, final, data),
        grid=(units, clips),
        in_specs=in_specs,
        out_specs=out_specs,
        out_shape=outs,
        scratch_shapes=scratch + [pltpu.VMEM((channels, own), jnp.bfloat16)],
        compiler_params=compiler_params(2),
        name="units_backward",
    )(*operands)


def stream_kernel(own, gh_ref, send_ref, e_ref, w_ref, out_ref, lines):
    length, channels = gh_ref.shape[1:]
    tiles = channels // LANES
    first = (length - own) // 2
    kept_first = (e_ref.shape[2] - own) // 2
    wide = own + 2 * RIM
    for tile in range(tiles):
        lanes = slice(tile * LANES, (tile + 1) * LANES)
        lines[tile] = send_ref[0, 0, :wide, lanes].astype(jnp.float32)
    kernel = jnp.concatenate([w_ref[0, tap] for tap in range(KSIZE)], axis=1)
    size = own // CHUNKS
    for chunk in range(CHUNKS):
        begin = chunk * size
        moved = jnp.concatenate(
            [
                lines[tile, start : start + size, :].astype(jnp.bfloat16)
                for start in (RIM + begin - tap + KSIZE // 2 for tap in range(KSIZE))
                for tile in range(tiles)
            ],
            axis=1,
        )
        total = lax.dot_general(moved, kernel, NT, preferred_element_type=jnp.float32)
        active = e_ref[0, 0, kept_first + begin : kept_first + begin + size, :]
        stream = gh_ref[0, first + begin : first + begin + size, :]
        out_ref[0, begin : begin + size, :] = (
            stream + total * slope_from_elu(active.astype(jnp.float32))
        ).astype(out_ref.dtype)


def stream_gradient(gh, send, e, kernels, own):
    clips, length, channels = gh.shape
    payload, kept_length = send.shape[2], e.shape[2]
    return pl.pallas_call(
        functools.partial(stream_kernel, own),
        grid=(clips,),
        in_specs=[
            pl.BlockSpec((1, length, channels), lambda c: (c, 0, 0)),
            pl.BlockSpec((1, 1, payload, channels), lambda c: (0, c, 0, 0)),
            pl.BlockSpec((1, 1, kept_length, channels), lambda c: (0, c, 0, 0)),
            pl.BlockSpec((1, KSIZE, channels, channels), lambda c: (0, 0, 0, 0)),
        ],
        out_specs=pl.BlockSpec((1, own, channels), lambda c: (c, 0, 0)),
        out_shape=jax.ShapeDtypeStruct((clips, own, channels), jnp.bfloat16),
        scratch_shapes=[
            pltpu.VMEM((channels // LANES, own + 2 * RIM, LANES), jnp.float32)
        ],
        compiler_params=compiler_params(),
        name="stream_gradient",
    )(gh, send, e, kernels)


def emit(result, start, tap_rows, first_axis, send_ref, keep_ref):
    result = result.astype(jnp.bfloat16)
    quarter = result.shape[0] // 4
    for rx in range(2):
        for ry in range(2):
            first, second = (rx, ry) if first_axis == 0 else (ry, rx)
            target = send_ref if first == 1 else keep_ref
            rows = slice((rx * 2 + ry) * quarter, (rx * 2 + ry + 1) * quarter)
            for segment in range(4):
                target[second, segment, pl.ds(start, tap_rows), :] = result[
                    rows, segment * LANES : (segment + 1) * LANES
                ]


def emit_outputs(rows):
    out = jax.ShapeDtypeStruct((2, 4, rows, LANES), jnp.bfloat16)
    return (out,) * 4


def weights_kernel(
    unit_first, units, own, with_up, place, mine_ref, other_ref, keep_ref, *rest
):
    if with_up:
        up_mine, up_other, filter_ref, sx, kx, sy, ky, latent_ref, lines, turned = rest
    else:
        sx, kx, sy, ky, lines = rest
    clips, channels = mine_ref.shape[1], mine_ref.shape[3]
    tiles = channels // LANES
    half = channels // 2
    block = channels // 8
    wide = own + 2 * RIM
    base = wide + own
    sources = (mine_ref, other_ref)
    step = pl.program_id(0)
    unit = unit_first - step // (KSIZE + 1)
    tap = lax.rem(step, KSIZE + 1)
    dilation = dilation_of(unit)
    normal = step < units * (KSIZE + 1)

    @pl.when(jnp.logical_and(normal, tap == 0))
    def _():
        for source in range(2):
            for clip in range(clips):
                for tile in range(tiles):
                    lines[source * clips + clip, tile, :, :] = sources[source][
                        0, clip, :wide, tile * LANES : (tile + 1) * LANES
                    ].astype(jnp.float32)

    def left(which):
        pieces = [
            keep_ref[0, clip, which * half : (which + 1) * half, :] for clip in range(clips)
        ] + [
            other_ref[0, clip, base + which * half : base + (which + 1) * half, :]
            for clip in range(clips)
        ]
        return jnp.concatenate(pieces, axis=1)

    def right():
        start = RIM - (tap - KSIZE // 2) * dilation
        return jnp.concatenate(
            [
                jnp.concatenate(
                    [
                        lines[item, tile, pl.ds(start, own), :].astype(jnp.bfloat16)
                        for tile in range(tiles)
                    ],
                    axis=1,
                )
                for item in range(2 * clips)
            ],
            axis=0,
        )

    half_taps = (KSIZE + 1) // 2

    @pl.when(jnp.logical_and(normal, tap < half_taps))
    def _():
        result = jnp.dot(left(0), right(), preferred_element_type=jnp.float32)
        emit(result, pl.multiple_of(tap * block, block), block, 0, sx, kx)

    @pl.when(jnp.logical_and(normal, jnp.logical_and(tap >= half_taps, tap < KSIZE)))
    def _():
        result = jnp.dot(left(0), right(), preferred_element_type=jnp.float32)
        start = pl.multiple_of((tap - half_taps) * block, block)
        emit(result, start, block, 1, sy, ky)

    @pl.when(jnp.logical_and(normal, tap == KSIZE))
    def _():
        grads = jnp.concatenate(
            [source[0, clip, wide:base, :] for source in sources for clip in range(clips)], axis=0
        )
        result = jnp.dot(left(1), grads, preferred_element_type=jnp.float32)
        emit(result, (half_taps - 1) * block, block, 1, sy, ky)

    if with_up:

        @pl.when(jnp.logical_not(normal))
        def _():
            up_kernel(place, up_mine, up_other, sx, kx, sy, ky, turned)
            latent_ref[...] = lax.dot_general(
                up_mine[:, channels:], filter_ref[...], NT, preferred_element_type=jnp.float32
            )


def weights_units(place, mine, other, keep, unit_first, own, up=None, skip=0, count=None):
    units, clips, payload, channels = mine.shape
    units = units if count is None else count
    steps = units * (KSIZE + 1)
    taps = KSIZE + 1
    rows = channels // 2
    groups = units + (0 if up is None else 1)
    out = jax.ShapeDtypeStruct((2, 4, groups * rows, LANES), jnp.bfloat16)
    out_spec = pl.BlockSpec((2, 4, rows, LANES), lambda i: (0, 0, i // taps, 0))

    def of_unit(array):
        return pl.BlockSpec(
            (1,) + array.shape[1:], lambda i: (skip + jnp.minimum(i // taps, units - 1), 0, 0, 0)
        )

    scratch = [pltpu.VMEM((2 * clips, channels // LANES, own + 2 * RIM, LANES), jnp.float32)]
    more = ()
    out_specs, outs = [out_spec] * 4, (out,) * 4
    if up is not None:
        more = tuple(up)
        outs += (jax.ShapeDtypeStruct((up[0].shape[0], channels), jnp.float32),)
        out_specs.append(whole(outs[4]))
        scratch.append(pltpu.VMEM((channels, 2 * up[0].shape[0]), jnp.bfloat16))
    return pl.pallas_call(
        functools.partial(weights_kernel, unit_first, units, own, up is not None),
        grid=(steps + (0 if up is None else 1),),
        in_specs=[smem(), of_unit(mine), of_unit(other), of_unit(keep)]
        + [whole(array) for array in more],
        out_specs=out_specs,
        out_shape=outs,
        scratch_shapes=scratch,
        compiler_params=compiler_params(),
        name="units_weights",
    )(place, mine, other, keep, *more)


def relative_rows(place, ref, block, start, count):
    pieces = []
    for rx in range(2):
        for ry in range(2):
            pair = jnp.bitwise_xor(place[4], ry) * 4 + jnp.bitwise_xor(place[3], rx) * 2
            first = pl.multiple_of((pair + place[2]) * block + start, 16)
            pieces.append(ref[pl.ds(first, count), :])
    return jnp.concatenate(pieces, axis=0)


def up_kernel(place, mine_ref, other_ref, sx, kx, sy, ky, turned):
    latents = mine_ref.shape[0]
    channels = turned.shape[0]
    for source, ref in enumerate((mine_ref, other_ref)):
        turned[:, source * latents : (source + 1) * latents] = jnp.transpose(ref[:, :channels])
    left = relative_rows(place, turned, channels // 8, 0, channels // 8)
    for tap in range(8):
        right = jnp.concatenate(
            [
                jnp.concatenate(
                    [
                        ref[:, channels + (z * 8 + tap) * LANES : channels + (z * 8 + tap + 1) * LANES]
                        for z in range(4)
                    ],
                    axis=1,
                )
                for ref in (mine_ref, other_ref)
            ],
            axis=0,
        )
        result = jnp.dot(left, right, preferred_element_type=jnp.float32)
        if tap < 4:
            emit(result, tap * (channels // 8), channels // 8, 0, sx, kx)
        else:
            emit(result, (tap - 4) * (channels // 8), channels // 8, 1, sy, ky)


def down_kernel(place, codes_ref, mine_ref, other_ref, sx, kx, sy, ky, turned):
    latents = mine_ref.shape[0]
    long = turned.shape[0]
    channels = long // 8
    refs = (mine_ref, other_ref)
    for source, ref in enumerate(refs):
        turned[:, source * latents : (source + 1) * latents] = jnp.transpose(ref[:, :long])
    right = jnp.concatenate([ref[:, long : long + channels] for ref in refs], axis=0)
    block = channels // 8
    for tap in range(8):
        left = relative_rows(place, turned, channels, tap * block, block)
        result = jnp.dot(left, right, preferred_element_type=jnp.float32)
        if tap < 4:
            emit(result, tap * block, block, 0, sx, kx)
        else:
            emit(result, (tap - 4) * block, block, 1, sy, ky)
    lane = lax.broadcasted_iota(jnp.int32, (4 * 64, channels), 1)
    row = lax.broadcasted_iota(jnp.int32, (64, 2 * latents), 0)
    for book in range(4):
        gaps = jnp.concatenate(
            [
                ref[:, long + channels + book * channels : long + channels + (book + 1) * channels]
                for ref in refs
            ],
            axis=0,
        )
        codes = codes_ref[book : book + 1, :]
        parts = []
        for part in range(2):
            pieces = []
            for rx in range(2):
                for ry in range(2):
                    pair = jnp.bitwise_xor(place[4], ry) * 4 + jnp.bitwise_xor(place[3], rx) * 2
                    first = (pair + place[2]) * 128 + part * 64
                    pieces.append(jnp.where(codes == row + first, 1.0, 0.0).astype(jnp.bfloat16))
            parts.append(
                jnp.dot(
                    jnp.concatenate(pieces, axis=0), gaps, preferred_element_type=jnp.float32
                )
            )
        result = jnp.where(lax.rem(lane, LANES) < 64, parts[0], parts[1])
        if book < 2:
            emit(result, 4 * block + book * 64, 64, 0, sx, kx)
        else:
            emit(result, 4 * block + (book - 2) * 64, 64, 1, sy, ky)


def down_gradient(place, codes, mine, other, channels):
    outs = emit_outputs(channels // 2 + 128)
    return pl.pallas_call(
        down_kernel,
        grid=(1,),
        in_specs=[smem(), whole(codes), whole(mine), whole(other)],
        out_specs=[whole(out) for out in outs],
        out_shape=outs,
        scratch_shapes=[pltpu.VMEM((8 * channels, 2 * mine.shape[0]), jnp.bfloat16)],
        compiler_params=compiler_params(),
        name="downsample_weights",
    )(place, codes, mine, other)


def swap(block, bit):
    return lax.ppermute(block, "clip", [(i, i ^ bit) for i in range(lax.axis_size("clip"))])


def turn(block, distance):
    count = lax.axis_size("tm")
    return lax.ppermute(block, "tm", [(i, (i + distance) % count) for i in range(count)])


def added(*parts):
    total = parts[0].astype(jnp.float32)
    for part in parts[1:]:
        total = total + part.astype(jnp.float32)
    return total


def after(value, *others):
    return lax.optimization_barrier((value,) + others)[0]


class Lane:
    def __init__(self):
        self.clock = None
        self.ready = ()
        self.flights = []

    def fly(self, arrays, then, kernels=1):
        self.flights.append([kernels, arrays, then])

    def land(self, outs):
        arrived = [flight for flight in self.flights if flight[0] <= 1]
        self.flights = [[n - 1, arrays, then] for n, arrays, then in self.flights if n > 1]
        flat = [array for _, arrays, _ in arrived for array in arrays]
        held = lax.optimization_barrier(tuple(outs) + tuple(flat))
        outs, flat = held[: len(outs)], held[len(outs) :]
        self.clock = outs[0]
        self.ready = ()
        for _, arrays, then in arrived:
            then(*flat[: len(arrays)])
            flat = flat[len(arrays) :]
        return outs

    def run(self, kernel, first, *others):
        if self.clock is not None:
            first = after(first, self.clock, *self.ready)
        return self.land(kernel(first, *others))

    def scatter(self, pieces, done, kernels=(1, 1)):
        sx, kx, sy, ky = pieces

        def second(ax, ay):
            bx = added(kx[1], ax[1]).astype(jnp.bfloat16)
            by = added(ky[1], ay[1]).astype(jnp.bfloat16)
            self.ready += (bx, by)

            def third(cx, cy):
                blocks = jnp.concatenate(
                    [
                        added(kx[0], ax[0], cx).astype(jnp.bfloat16),
                        added(ky[0], ay[0], cy).astype(jnp.bfloat16),
                    ],
                    axis=1,
                )
                self.ready += (blocks,)
                done(blocks)

            self.fly((swap(bx, 4), swap(by, 2)), third, kernels[1])

        self.fly((swap(sx, 2), swap(sy, 4)), second, kernels[0])

    def segments(self, groups, done):
        blocks = jnp.concatenate(groups, axis=1) if len(groups) > 1 else groups[0]
        self.ready += (blocks,)
        total = lax.psum_scatter(blocks, "tm", scatter_dimension=0).astype(jnp.float32)
        start = 0
        for group in groups:
            done.append(total[start : start + group.shape[1]])
            start += group.shape[1]

    def everywhere(self, value, split, done):
        steps = [("tm", bit) for bit in (1, 2)] + [("clip", bit) for bit in (1, 2, 4)]

        def step(value, index):
            if index == len(steps):
                parts = split(value)
                self.ready += parts
                done.extend(parts)
                return
            axis, bit = steps[index]
            pairs = [(i, i ^ bit) for i in range(lax.axis_size(axis))]
            self.ready += (value,)
            self.fly(
                (lax.ppermute(value, axis, pairs),), lambda other: step(value + other, index + 1)
            )

        step(value, 0)

    def finish(self):
        while self.flights:
            tick = self.ready or (self.clock,)
            self.land(tick)


def neighbours(block, reach):
    ends = lax.axis_size("tm") - 1
    head = block[:, :reach]
    tail = block[:, block.shape[1] - reach :]
    return (
        lax.ppermute(tail, "tm", [(i, i + 1) for i in range(ends)]),
        lax.ppermute(head, "tm", [(i + 1, i) for i in range(ends)]),
    )


def latent_rows(block, below, above):
    widths = ((0, 0), (0, HALO - below.shape[1]), (0, 0))
    return jnp.concatenate([block, jnp.pad(below, widths), jnp.pad(above, widths)], axis=1)


def with_both(one, reach_one, two, reach_two):
    ends = lax.axis_size("tm") - 1
    tail = jnp.concatenate(
        [one[:, one.shape[1] - reach_one :], two[:, two.shape[1] - reach_two :]], axis=1
    )
    head = jnp.concatenate([one[:, :reach_one], two[:, :reach_two]], axis=1)
    below = lax.ppermute(tail, "tm", [(i, i + 1) for i in range(ends)])
    above = lax.ppermute(head, "tm", [(i + 1, i) for i in range(ends)])
    return (
        jnp.concatenate([below[:, :reach_one], one, above[:, :reach_one]], axis=1),
        jnp.concatenate([below[:, reach_one:], two, above[:, reach_one:]], axis=1),
    )


def split_units(reduced, channels):
    block = channels // 8
    taps = [part.reshape(8, block, LANES) for part in reduced]
    return jnp.stack([part[:KSIZE] for part in taps]), jnp.stack([part[KSIZE] for part in taps])


def fast_device(
    incoming_samples,
    sample_extents,
    chosen_entries,
    encoder_dilated_kernels,
    encoder_dilated_biases,
    encoder_pointwise_tables,
    encoder_pointwise_offsets,
    reducing_filter,
    reducing_offset,
    quantizer_tables,
    widening_filter,
    widening_offset,
    decoder_dilated_filters,
    decoder_dilated_offsets,
    decoder_pointwise_tables,
    decoder_pointwise_offsets,
    result_cotangent,
):
    f32, bf16 = jnp.float32, jnp.bfloat16
    segment = lax.axis_index("tm")
    member = lax.axis_index("clip")
    clips, frames, channels = incoming_samples.shape
    latents = frames // HOP_FACTOR
    all_frames = frames * lax.axis_size("tm")
    first_frame = segment * frames
    group_width = channels // GROUPS

    def bounds(reach):
        return jnp.stack([reach - first_frame, all_frames - first_frame + reach])

    coordinates = jnp.stack(
        [member % 2, (member // 2) % 2, (member // 4) % 2, segment]
    ).astype(jnp.int32)

    def placed(reach):
        return jnp.concatenate([bounds(reach).astype(jnp.int32), coordinates])

    reach = LATENT_REACH * HOP_FACTOR
    grad_reach = GRAD_REACH * HOP_FACTOR
    where = bounds(reach).astype(jnp.int32)
    place = placed(grad_reach)

    lane = Lane()
    below, above = neighbours(chosen_entries, LATENT_REACH)
    far = LATENT_REACH - GRAD_REACH
    below = jnp.concatenate([below[:, far:], below[:, :far]], axis=1)
    codes = latent_rows(chosen_entries, below, above)
    cotangent, samples = with_both(result_cotangent, grad_reach, incoming_samples, reach)
    own_codes = chosen_entries.reshape(clips * latents, GROUPS * LEVELS).T
    pair_codes = []
    lane.fly(
        (swap(own_codes, 1),),
        lambda other: pair_codes.append(jnp.concatenate([own_codes, other], axis=1)),
        2,
    )

    quantized, start, picked = lane.run(
        lambda c: start_frames(c, quantizer_tables, widening_filter, widening_offset), codes
    )

    e_decoder, p_decoder, output = lane.run(
        lambda h: forward_units(
            where,
            h,
            decoder_dilated_filters,
            decoder_dilated_offsets,
            decoder_pointwise_tables,
            decoder_pointwise_offsets,
            frames,
            False,
        ),
        start,
    )

    reduced = {}
    sizes = {"a": 2, "b": 2, "c": 2}
    batches = {name: [] for name in sizes}
    order = {name: [] for name in sizes}

    def into(batch, name):
        def done(blocks):
            batches[batch].append(blocks)
            order[batch].append(name)
            if len(batches[batch]) == sizes[batch]:
                reduced[batch] = []
                lane.segments(batches[batch], reduced[batch])

        return done

    def backward(grad, p, e, kernels, tables, unit, units, data=True, kernels_between=1):
        send, keep, sums, *grad = lane.run(
            lambda g: backward_units(place, g, p, e, kernels, tables, unit, units, frames, data),
            grad,
        )
        grad = grad[0] if data else None
        work = [send, None, keep]

        def arrived(other):
            work[1] = other

        lane.fly((swap(send, 1),), arrived, kernels_between)
        return grad, work, sums

    def weights(work, unit, batch, name, up=None, kernels=(1, 1), skip=0, count=None):
        send, other, keep = work
        pieces = lane.run(
            lambda mine: weights_units(
                place, mine, other, keep, unit, frames, up, skip, count
            ),
            send,
        )
        lane.scatter(pieces[:4], into(batch, name), kernels)
        return pieces[4:]

    decoder = (p_decoder, e_decoder, decoder_dilated_filters, decoder_pointwise_tables)
    grad_start, decoder_last, sums_last = backward(cotangent, *decoder, 2, 1)
    grad_start, decoder_rest, sums_rest = backward(grad_start, *decoder, 1, 2)

    widened_grad = grad_start
    folded = widened_grad.reshape(clips * latents, HOP_FACTOR * channels)
    up_send = jnp.concatenate([quantized.reshape(clips * latents, channels), folded], axis=1)
    up = (up_send, swap(up_send, 1), widening_filter)
    weights(decoder_last, 2, "a", "d2", None, (1, 2))
    (latent_grad,) = weights(decoder_rest, 1, "a", "d10up", up, (2, 1))
    latent_grad = latent_grad.reshape(clips, latents, channels)
    latent_grads = []
    lane.fly(
        neighbours(latent_grad, GRAD_REACH),
        lambda below, above: latent_grads.append(latent_rows(latent_grad, below, above)),
    )

    e_encoder, p_encoder, pooled_wide = lane.run(
        lambda h: forward_units(
            where,
            h,
            encoder_dilated_kernels,
            encoder_dilated_biases,
            encoder_pointwise_tables,
            encoder_pointwise_offsets,
            frames + 2 * grad_reach,
            True,
        ),
        samples,
    )
    extents = jnp.concatenate([jnp.reshape(first_frame, (1,)), sample_extents]).astype(jnp.int32)
    down_send, latent_sums, pooled_grad = lane.run(
        lambda p: latent_frames(
            extents, p, reducing_filter, reducing_offset, picked, latent_grads[0]
        ),
        pooled_wide,
    )
    down_other = []
    lane.fly((swap(down_send, 1),), down_other.append)

    encoder = (p_encoder, e_encoder, encoder_dilated_kernels, encoder_pointwise_tables)
    grad, work, sums = backward(pooled_grad, *encoder, 2, 2, kernels_between=2)
    sums_2, sums_1 = sums[:1], sums[1:]
    pieces = lane.run(
        lambda mine: down_gradient(place, pair_codes[0], mine, down_other[0], channels), down_send
    )
    lane.scatter(pieces, into("b", "down"), (2, 1))
    _, work_0, sums_0 = backward(grad, *encoder, 0, 1, False)
    weights(work, 2, "b", "e2", skip=0, count=1)
    small = jnp.concatenate(
        [
            sums.reshape(-1, channels)
            for sums in (sums_0, sums_1, sums_2, sums_rest, sums_last, latent_sums)
        ],
        axis=0,
    )
    summed = []

    def parts(small):
        rows = small.reshape(7, 8, channels)
        loss_sum = (1.0 + commit_weight) * jnp.sum(rows[6, 1])
        total_count = rows[6, 2, 0] / lax.axis_size("tm")
        decoder_rows = jnp.stack([rows[4], rows[3], rows[5]])
        return (
            loss_sum / (total_count * channels),
            rows[:3, 0],
            rows[:3, 1],
            rows[6, 0],
            rows[4, 2],
            decoder_rows[:, 0],
            decoder_rows[:, 1],
        )

    lane.everywhere(small, parts, summed)
    weights(work, 1, "c", "e1", skip=1, count=1)
    weights(work_0, 0, "c", "e0")
    (input_grad,) = lane.run(
        lambda g: (stream_gradient(g, work_0[0], e_encoder, encoder_dilated_kernels, frames),),
        grad,
    )
    lane.finish()
    result = {}
    for batch in order:
        for name, part in zip(order[batch], reduced[batch]):
            result[name] = part

    block = channels // 8
    rest = result["d10up"].reshape(2, UNITS, channels // 2, LANES)
    decoder_parts = [rest[:, 1], rest[:, 0], result["d2"]]
    encoder_parts = [result["e0"], result["e1"], result["e2"]]
    analysis, mixers = split_units(encoder_parts, channels)
    synthesis, remixers = split_units(decoder_parts, channels)
    up_rows = rest[:, 2].reshape(8, block, LANES)
    upsample = up_rows.transpose(1, 0, 2).reshape(block, 8 * LANES)
    halves = result["down"].reshape(2, channels // 2 + 128, LANES)
    downsample = halves[:, : channels // 2].reshape(8 * block, LANES)
    codebooks = (
        halves[:, channels // 2 :]
        .reshape(GROUPS, LEVELS, 64, 2, 64)
        .transpose(0, 1, 3, 2, 4)
        .reshape(GROUPS, LEVELS, 128, 64)
    )
    masked_loss, offsets, shifts, pooling, spreading, biasing, tilting = summed
    return (
        output,
        quantized,
        masked_loss,
        input_grad,
        analysis,
        offsets,
        mixers,
        shifts,
        downsample,
        pooling,
        codebooks,
        upsample,
        spreading,
        synthesis,
        biasing,
        remixers,
        tilting,
    )


def solution(mesh):
    placed = (
        P("clip", "tm", None),
        P("clip"),
        P("clip", "tm", None),
        P(),
        P(),
        P(),
        P(),
        P(),
        P(),
        P(),
        P(),
        P(),
        P(),
        P(),
        P(),
        P(),
        P("clip", "tm", None),
    )
    matched = mesh.shape["clip"] == 8 and mesh.shape["tm"] == 4
    return jax.shard_map(
        fast_device if matched else on_device,
        mesh=mesh,
        in_specs=placed,
        out_specs=(
            P("clip", "tm", None),
            P("clip", "tm", None),
            P(),
            P("clip", "tm", None),
            P(None, None, "clip", "tm"),
            P(),
            P(None, "clip", "tm"),
            P(),
            P("clip", "tm"),
            P(),
            P(None, None, "clip", "tm"),
            P("clip", "tm"),
            P(),
            P(None, None, "clip", "tm"),
            P(),
            P(None, "clip", "tm"),
            P(),
        ),
        check_vma=False,
    )
```
